32 devices in a mesh: band: 4 (over y, x), row: 8 (over z, core).
Axes of the slice: x: 2, y: 2, z: 4, core: 2. Of those that a mesh axis runs over, the one named last changes fastest.
Arguments:
- amplitude: bfloat16 [512, 8192], P('row'), may hold values from 0.5 to 1.5
- seg_map: int32 [512, 8192], P('row'), may hold values from 0 to 1199, as said below
- seg_box: int32 [4, 1200], replicated, may hold values from 0 to 8191, as said below
- seg_coeffs: float32 [3, 1200], replicated, may hold values from -1 to 1
- probe_freq: int32 [2, 2], replicated, may hold values from 3 to 23
- probe_amp: float32 [2], replicated, may hold values from 0.3 to 0.8
- measured: float32 [8, 256, 4, 2, 256], P('band', 'row'), may hold values from -6 to 6
Outputs:
- gradient: float32 [3, 1200], replicated
The draws below stay inside these ranges and needn't reach their ends.
Inputs may be any that keep to these rules, and one draw needn't show every extreme that they name: `seg_map`: segments lie in 16 rows of rectangular tiles of whole pupil rows, 75 tiles side by side in each, alternate rows offset by half a tile; segment numbers rise by tile row, then by column; every segment has samples. `seg_box`: the bounds of each segment's samples in seg_map, rows first.
All inputs are finite; a program needn't handle non-finite values.
Results may differ from the reference program's by a relative error of at most 0.0015.
Values may be sent and summed in bfloat16 or wider, within the bound.
No kernel may reach another device: no remote copies, remote signals or barrier semaphores. Data moves between devices by JAX's collectives and lax.ppermute only.
A program may use at most 192 MiB of HBM per device.

```python
import math
import jax
import jax.numpy as jnp
from jax import lax

NC = 8192
NR = 512
M = 256
BANDS = 8
PAIRS = 2
PROBES = 4
SEG = 1200
SROWS = 16


def segment_layout(key):
    key = jax.random.fold_in(key, 11)
    key_rows, key_cols = jax.random.split(key)
    per_row = SEG // SROWS
    step_rows = NR // SROWS
    jitter_rows = step_rows // 4
    inner_rows = jnp.arange(1, SROWS, dtype=jnp.int32) * step_rows + jax.random.randint(key_rows, (SROWS - 1,), -jitter_rows, jitter_rows + 1, dtype=jnp.int32)
    row_edges = jnp.concatenate([jnp.zeros((1,), jnp.int32), inner_rows, jnp.full((1,), NR, jnp.int32)])
    width = NC // per_row
    jitter_cols = width // 4
    offset = jnp.arange(SROWS, dtype=jnp.int32) % 2 * (width // 2)
    inner_cols = jnp.arange(1, per_row, dtype=jnp.int32)[None, :] * width + offset[:, None] + jax.random.randint(key_cols, (SROWS, per_row - 1), -jitter_cols, jitter_cols + 1, dtype=jnp.int32)
    col_edges = jnp.concatenate([jnp.zeros((SROWS, 1), jnp.int32), inner_cols, jnp.full((SROWS, 1), NC, jnp.int32)], axis=1)
    rows_all = jnp.arange(NR, dtype=jnp.int32)
    tile_row = jnp.sum((rows_all[:, None] >= inner_rows[None, :]).astype(jnp.int32), axis=1)
    cols_all = jnp.arange(NC, dtype=jnp.int32)
    count_table = jnp.sum((cols_all[None, :, None] >= inner_cols[:, None, :]).astype(jnp.int32), axis=2)
    seg_map = tile_row[:, None] * per_row + jnp.take(count_table, tile_row, axis=0)
    box = jnp.stack([jnp.repeat(row_edges[:-1], per_row), jnp.repeat(row_edges[1:] - 1, per_row), col_edges[:, :-1].reshape(-1), (col_edges[:, 1:] - 1).reshape(-1)])
    return (seg_map.astype(jnp.int32), box.astype(jnp.int32))


def draw_seg_map(key, part):
    return segment_layout(key)[0]


def draw_seg_box(key, part):
    return segment_layout(key)[1]


def place_ends(array, rng, low, top_value):
    spot = [jax.random.randint(jax.random.fold_in(rng, axis), (), 0, length) for axis, length in enumerate(array.shape)]
    widest = array.shape.index(max(array.shape))
    neighbour = spot[:widest] + [(spot[widest] + 1) % array.shape[widest]] + spot[widest + 1:]
    return array.at[tuple(spot)].set(low).at[tuple(neighbour)].set(top_value)


def steps_of(own_key, dims, cuts, least, top_value):
    gain = 1.0
    for position, parts in cuts:
        heights = jax.random.uniform(jax.random.fold_in(jax.random.fold_in(own_key, 6), position), (parts,), jnp.float32, least / len(cuts), top_value / len(cuts))
        gain = gain * jnp.repeat(jnp.exp(heights), dims[position] // parts).reshape((-1,) + (1,) * (len(dims) - 1 - position))
    return gain


def bell_draw(own_key, shape, scale, reach, cuts=(), kind=jnp.bfloat16):
    values = jax.random.normal(own_key, shape, jnp.float32) * scale
    if len(cuts) > 0:
        values = steps_of(own_key, shape, cuts, -0.22, 0.18) * values
    return jnp.clip(values, min=-reach, max=reach).astype(kind)


def setup_inputs(seed: int = 0) -> dict:
    key_of = jax.random.split(jax.random.key(seed), 8)
    amplitude = jnp.clip(0.5 + 1.0 * jax.random.uniform(key_of[0], (NR, NC), jnp.float32) ** steps_of(key_of[0], (NR, NC), ((0, 8),), -0.2, 0.2), 0.5, 1.5).astype(jnp.bfloat16)
    seg_map = draw_seg_map(jax.random.fold_in(key_of[7], 71), 0)
    seg_box = draw_seg_box(jax.random.fold_in(key_of[7], 71), 0)
    seg_coeffs = jnp.clip(jax.random.uniform(key_of[3], (3, SEG), jnp.float32, -1.0, 1.0), -1.0, 1.0)
    probe_freq = place_ends(jax.random.randint(key_of[4], (PAIRS, 2), 3, 24), jax.random.fold_in(key_of[4], 1), 3, 23).astype(jnp.int32)
    probe_amp = jnp.clip(jax.random.uniform(key_of[5], (PAIRS,), jnp.float32, 0.3, 0.8), 0.3, 0.8)
    measured = bell_draw(key_of[6], (BANDS, M, PROBES, 2, M), 1.0, 6.0, ((0, 4), (1, 8)), jnp.float32)
    return dict(amplitude=amplitude, seg_map=seg_map, seg_box=seg_box, seg_coeffs=seg_coeffs, probe_freq=probe_freq, probe_amp=probe_amp, measured=measured)


TWO_PI = 2.0 * math.pi
SAMPLING = 0.5
SPREAD = 0.2

def wave_tables(coords, band, count):
    ratio = 1.0 + SPREAD * ((band + 0.5) / BANDS - 0.5)
    focal = (jnp.arange(count, dtype=jnp.float32) - count / 2 + 0.5) * SAMPLING
    angle = TWO_PI * focal[:, None] * coords[None, :] / ratio
    return jnp.stack([jnp.cos(angle), jnp.sin(angle)]).astype(jnp.bfloat16)

def column_coords():
    return (jnp.arange(NC, dtype=jnp.float32) + 0.5) / NC - 0.5

def row_coords(rows_global, total_rows):
    return (rows_global.astype(jnp.float32) + 0.5) / NC - total_rows / (2.0 * NC)

def segment_basis(seg_map, seg_box, seg_coeffs, rows_global):
    bounds = seg_box.astype(jnp.float32)
    middle_row = 0.5 * (bounds[0] + bounds[1])
    half_row = 0.5 * (bounds[1] - bounds[0] + 1.0)
    middle_col = 0.5 * (bounds[2] + bounds[3])
    half_col = 0.5 * (bounds[3] - bounds[2] + 1.0)
    columns = jnp.arange(NC, dtype=jnp.float32)
    across = (columns[None, :] - jnp.take(middle_col, seg_map)) / jnp.take(half_col, seg_map)
    down = (rows_global.astype(jnp.float32)[:, None] - jnp.take(middle_row, seg_map)) / jnp.take(half_row, seg_map)
    phase = jnp.take(seg_coeffs[0], seg_map) + jnp.take(seg_coeffs[1], seg_map) * across + jnp.take(seg_coeffs[2], seg_map) * down
    return (phase, across, down)

def probe_waves(probe_freq, probe_amp, rows_global, total_rows):
    freq = probe_freq.astype(jnp.float32)
    columns = column_coords()
    rows_here = row_coords(rows_global, total_rows)
    angle = TWO_PI * (freq[:, 0, None, None] * columns[None, None, :] + freq[:, 1, None, None] * rows_here[None, :, None])
    waves = probe_amp[:, None, None] * jnp.sin(angle)
    return jnp.stack([waves, -waves], axis=1).reshape(2 * PAIRS, rows_here.shape[0], NC)

def reference(amplitude, seg_map, seg_box, seg_coeffs, probe_freq, probe_amp, measured):
    rows_global = jnp.arange(NR, dtype=jnp.int32)
    normf = 1.0 / math.sqrt(NR * NC)
    phase, across, down = segment_basis(seg_map, seg_box, seg_coeffs, rows_global)
    waves = probe_waves(probe_freq, probe_amp, rows_global, NR)
    magnitude = amplitude.astype(jnp.float32)
    row_values = row_coords(rows_global, NR)

    def band_step(accum, inputs):
        band_index, measured_band = inputs
        band = band_index.astype(jnp.float32)
        pupil_table = wave_tables(column_coords(), band, M)
        row_table = wave_tables(row_values, band, M)

        def probe_step(inner, probe_inputs):
            wave, measured_probe = probe_inputs
            total_phase = phase + wave
            field_real = magnitude * jnp.cos(total_phase)
            field_imag = magnitude * jnp.sin(total_phase)
            field_low = jnp.stack([field_real, field_imag]).astype(jnp.bfloat16).reshape(2 * NR, NC)
            section_one = jnp.dot(field_low, pupil_table.reshape(2 * M, NC).T, preferred_element_type=jnp.float32).reshape(2, NR, 2, M)
            y_real = section_one[0, :, 0] + section_one[1, :, 1]
            y_imag = section_one[1, :, 0] - section_one[0, :, 1]
            half_way = jnp.stack([y_real, y_imag]).astype(jnp.bfloat16)
            section_two = jnp.dot(half_way.transpose(2, 0, 1).reshape(2 * M, NR), row_table.reshape(2 * M, NR).T, preferred_element_type=jnp.float32).reshape(M, 2, 2, M)
            f_real = section_two[:, 0, 0] + section_two[:, 1, 1]
            f_imag = section_two[:, 1, 0] - section_two[:, 0, 1]
            focal = jnp.stack([f_real, f_imag], axis=1) * normf
            residual = (focal - measured_probe).astype(jnp.bfloat16)
            back_two = jnp.dot(residual.reshape(2 * M, M), row_table.transpose(1, 0, 2).reshape(M, 2 * NR), preferred_element_type=jnp.float32).reshape(M, 2, 2, NR)
            h_real = back_two[:, 0, 0] - back_two[:, 1, 1]
            h_imag = back_two[:, 1, 0] + back_two[:, 0, 1]
            hidden_side = jnp.stack([h_real, h_imag], axis=1).astype(jnp.bfloat16)
            back_one = jnp.dot(hidden_side.reshape(M, 2 * NR).T, pupil_table.transpose(1, 0, 2).reshape(M, 2 * NC), preferred_element_type=jnp.float32).reshape(2, NR, 2, NC)
            g_real = back_one[0, :, 0] - back_one[1, :, 1]
            g_imag = back_one[1, :, 0] + back_one[0, :, 1]
            return (inner + (g_imag * field_real - g_real * field_imag), None)
        result, unused = lax.scan(probe_step, accum, (waves, measured_band.transpose(1, 0, 2, 3)))
        return (result, None)
    start = jnp.zeros((NR, NC), jnp.float32)
    weight, unused = lax.scan(band_step, start, (jnp.arange(BANDS, dtype=jnp.int32), measured))
    weight = weight * (2.0 * normf / (BANDS * PROBES))
    flat_ids = seg_map.reshape(-1)
    sums = [jax.ops.segment_sum(term.reshape(-1), flat_ids, num_segments=SEG) for term in (weight, weight * across, weight * down)]
    return jnp.stack(sums)
```

```python
import functools
import math

import jax
import jax.numpy as jnp
from jax import lax
from jax.experimental import pallas as pl
from jax.experimental.pallas import tpu as pltpu
from jax.sharding import PartitionSpec as P

SROWS = 16
SAMPLING = 0.5
SPREAD = 0.2
TWO_PI = 2.0 * math.pi
LANES = 128
F32 = jnp.float32
BF16 = jnp.bfloat16

SIN_HALF = (0.9999999971, -0.1666666029, 0.008333109246, -0.0001981365728, 2.616271295e-06)
COS_HALF = (0.9999999682, -0.4999993032, 0.04166421727, -0.001385868782, 2.327410856e-05)
SIN_WAVE = (0.9999999964, -0.166666488, 0.008331936401, -0.000194912576)
COS_WAVE = (0.9999999679, -0.499998396, 0.04165412354, -0.001357443708)
SIN_TURN = (
    6.283185307, -41.34170222, 81.60524741, -76.70580003,
    42.05775188, -15.08655272, 3.781282403, -0.6207370354,
)
COS_TURN = (
    0.9999999999, -19.73920874, 64.93938905, -85.45665775,
    60.24212493, -26.40463062, 7.800022219, -1.452987552,
)


def series(coeffs, t):
    value = jnp.full_like(t, coeffs[-1])
    for c in reversed(coeffs[:-1]):
        value = value * t + c
    return value


def turn_cos_sin(turns):
    t = turns - jnp.floor(turns + 0.5)
    square = t * t
    return series(COS_TURN, square), t * series(SIN_TURN, square)


def iota(shape, axis):
    return lax.broadcasted_iota(jnp.int32, shape, axis)


def focal_scale(m_positive, band, band_total):
    ratio = 1.0 + SPREAD * ((band.astype(F32) + 0.5) / band_total - 0.5)
    return m_positive / ratio


def band_lanes(first_band, bands, half, band_total, rows):
    pieces = []
    for b in range(bands):
        q = (iota((rows, half), 1).astype(F32) + 0.5) * SAMPLING
        band = jnp.full((rows, half), 1, jnp.int32) * (first_band + b)
        pieces.append(focal_scale(q, band, band_total))
    return jnp.concatenate(pieces, axis=1)


def column_tables(first_band, bands, half, band_total, cols, tile_ref, shift_ref):
    q = band_lanes(first_band, bands, half, band_total, LANES)
    c, s = turn_cos_sin(q * (iota(q.shape, 0).astype(F32) / cols))
    tile_ref[0] = c
    tile_ref[1] = s
    tiles = cols // LANES
    q = band_lanes(first_band, bands, half, band_total, tiles)
    x = (iota(q.shape, 0).astype(F32) * LANES + 0.5) / cols - 0.5
    c, s = turn_cos_sin(q * x)
    shift_ref[0] = c
    shift_ref[1] = s


def write_table(table_ref, tile_ref, shift_ref, first_tile, tiles, bands, half):
    for i in range(tiles):
        sc = shift_ref[0, pl.ds(first_tile + i, 1), :]
        ss = shift_ref[1, pl.ds(first_tile + i, 1), :]
        for b in range(bands):
            lanes = slice(b * half, (b + 1) * half)
            for k in range(0, LANES, 16):
                tc = tile_ref[0, k : k + 16, lanes]
                ts = tile_ref[1, k : k + 16, lanes]
                rows = slice(i * LANES + k, i * LANES + k + 16)
                table_ref[rows, 2 * b * half : (2 * b + 1) * half] = (
                    tc * sc[:, lanes] - ts * ss[:, lanes]
                ).astype(BF16)
                table_ref[rows, (2 * b + 1) * half : (2 * b + 2) * half] = (
                    ts * sc[:, lanes] + tc * ss[:, lanes]
                ).astype(BF16)


def tile_row_pieces(seg_ref, per_row, width):
    for t in range(SROWS):
        yield t, pltpu.roll(seg_ref[...], (width - t * per_row) % width, axis=1)[:, :LANES]


def field_kernel(
    dims, pos_ref, box_ref, freq_ref, amp_ref, seg_ref, amplitude_ref, map_ref,
    x_ref, across_ref, y_ref,
    tables, bases, slot_tables, waves, tile_ref, shift_ref, table_ref, total_ref, slot_map,
):
    rows, cols, block, bands, half, band_total, total_rows, per_row, pairs, vloc, owners = dims
    step = pl.program_id(0)
    row0 = pos_ref[0] * rows

    @pl.when(step == 0)
    def _():
        width = seg_ref.shape[1]
        for g in range(rows // 8):
            here = (row0 + g * 8 + iota((8, LANES), 0)).astype(F32)
            values = [jnp.zeros((8, LANES), F32)] * 4
            base = jnp.zeros((8, LANES), jnp.int32)
            for t, piece in tile_row_pieces(seg_ref, per_row, width):
                part = [jnp.broadcast_to(piece[k : k + 1], (8, LANES)) for k in range(7)]
                low, high = part[3][:, :1], part[4][:, :1]
                mine = (here >= low) & (here <= high)
                down = (here - 0.5 * (part[3] + part[4])) / (0.5 * (part[4] - part[3] + 1.0))
                new = (
                    0.5 * (part[0] + part[2] * down),
                    0.5 * part[1],
                    0.5 * (part[5] + part[6]),
                    2.0 / (part[6] - part[5] + 1.0),
                )
                values = [jnp.where(mine, n, v) for n, v in zip(new, values)]
                base = jnp.where(mine, t * per_row, base)
            for k in range(4):
                tables[k, g * 8 : (g + 1) * 8] = values[k]
            bases[g * 8 : (g + 1) * 8] = base
        for t, piece in tile_row_pieces(seg_ref, per_row, width):
            slot_tables[0, t : t + 1] = 0.5 * (piece[5:6] + piece[6:7])
            slot_tables[1, t : t + 1] = 2.0 / (piece[6:7] - piece[5:6] + 1.0)
        y = ((row0 + iota((rows, LANES), 0)).astype(F32) + 0.5) / cols - total_rows / (2.0 * cols)
        for j in range(pairs):
            c, s = turn_cos_sin(freq_ref[j, 1].astype(F32) * y)
            waves[2 * j] = amp_ref[j] * c
            waves[2 * j + 1] = amp_ref[j] * s
        column_tables(pos_ref[1] * bands, bands, half, band_total, cols, tile_ref, shift_ref)
        total_ref[...] = jnp.zeros_like(total_ref)

    for t in range(SROWS):
        first = jnp.clip(box_ref[0, t * per_row] - row0, 0, rows - 1)
        slot_map[t : t + 1, :] = map_ref[pl.ds(first, 1), :] - t * per_row
    chunks = block // LANES
    for i in range(chunks):
        lanes = slice(i * LANES, (i + 1) * LANES)
        column = (iota((8, LANES), 1) + (step * block + i * LANES)).astype(F32)
        for t in range(0, SROWS, 8):
            index = slot_map[t : t + 8, lanes] & (LANES - 1)
            mid = jnp.take_along_axis(slot_tables[0, t : t + 8], index, axis=1)
            inv = jnp.take_along_axis(slot_tables[1, t : t + 8], index, axis=1)
            across_ref[t : t + 8, lanes] = (column - mid) * inv

    row = iota((8, block), 0)
    freq = jnp.zeros((8, block), F32)
    for j in range(pairs):
        freq = jnp.where(row // 2 == j, freq_ref[j, 0].astype(F32), freq)
    x = ((iota((8, block), 1) + step * block).astype(F32) + 0.5) / cols - 0.5
    turn_c, turn_s = turn_cos_sin(freq * x)
    columns_wave = jnp.where(row % 2 == 0, turn_s, turn_c)

    write_table(table_ref, tile_ref, shift_ref, step * chunks, chunks, bands, half)

    for i in range(chunks):
        lanes = slice(i * LANES, (i + 1) * LANES)
        column = (iota((16, LANES), 1) + (step * block + i * LANES)).astype(F32)
        for g in range(0, rows, 16):
            here = slice(g, g + 16)
            index = map_ref[here, lanes] - bases[here]

            def pick(k):
                return jnp.concatenate(
                    [
                        jnp.take_along_axis(tables[k, g + h : g + h + 8], index[h : h + 8], axis=1)
                        for h in (0, 8)
                    ],
                    axis=0,
                )

            half_phase = pick(0) + pick(1) * ((column - pick(2)) * pick(3))
            square = half_phase * half_phase
            s = half_phase * series(SIN_HALF, square)
            c = series(COS_HALF, square)
            twice = s + s
            size = amplitude_ref[here, lanes].astype(F32)
            real = size * (1.0 - twice * s)
            imag = size * (twice * c)
            for j in range(pairs):
                wave = (
                    columns_wave[2 * j : 2 * j + 1, lanes] * waves[2 * j, here]
                    + columns_wave[2 * j + 1 : 2 * j + 2, lanes] * waves[2 * j + 1, here]
                )
                square = wave * wave
                parts = (series(COS_WAVE, square), wave * series(SIN_WAVE, square))
                for k in range(2):
                    at = (2 * j + k) * 2 * rows + g
                    x_ref[at : at + 16, lanes] = (real * parts[k]).astype(BF16)
                    x_ref[at + rows : at + rows + 16, lanes] = (imag * parts[k]).astype(BF16)

    total_ref[...] += jnp.dot(x_ref[...], table_ref[...], preferred_element_type=F32)

    @pl.when(step == pl.num_programs(0) - 1)
    def _():
        r2 = 2 * rows
        m = iota((half, half), 0)
        n = iota((half, half), 1)
        straight = (m == n).astype(F32).astype(BF16)
        turned = (m + n == half - 1).astype(F32).astype(BF16)
        for b in range(bands):
            for p in range(2 * pairs):
                cos_part = total_ref[p * r2 : (p + 1) * r2, 2 * b * half : (2 * b + 1) * half]
                sin_part = total_ref[p * r2 : (p + 1) * r2, (2 * b + 1) * half : (2 * b + 2) * half]
                swapped = jnp.concatenate([sin_part[rows:], -sin_part[:rows]], axis=0)
                nt = (((1,), (1,)), ((), ()))
                low = lax.dot_general(
                    turned, (cos_part - swapped).astype(BF16), nt, preferred_element_type=F32
                ).astype(BF16)
                high = lax.dot_general(
                    straight, (cos_part + swapped).astype(BF16), nt, preferred_element_type=F32
                ).astype(BF16)
                if owners:
                    each = half // vloc
                    for d in range(each):
                        piece = slice(d * vloc, (d + 1) * vloc)
                        y_ref[d, b, p * vloc : (p + 1) * vloc, :] = low[piece]
                        y_ref[each + d, b, p * vloc : (p + 1) * vloc, :] = high[piece]
                else:
                    y_ref[b, p, :half, :] = low
                    y_ref[b, p, half:, :] = high


def focal_kernel(dims, pos_ref, y_ref, measured_ref, h_ref, table_ref):
    rows, cols, bands, focal, band_total, total_rows, sources, scale = dims
    r2 = 2 * rows
    for b in range(bands):
        band = jnp.full((rows, focal), 1, jnp.int32) * (pos_ref[1] * bands + b)
        q = (iota((rows, focal), 1).astype(F32) + (0.5 - focal / 2)) * SAMPLING
        q = focal_scale(q, band, band_total)
        tile_c, tile_s = turn_cos_sin(q * (iota(q.shape, 0).astype(F32) / cols))
        first = iota((sources, focal), 0).astype(F32) * rows + 0.5
        y = first / cols - total_rows / (2.0 * cols)
        shift_c, shift_s = turn_cos_sin(jnp.broadcast_to(q[:1], y.shape) * y)
        for d in range(sources):
            sc, ss = shift_c[d : d + 1], shift_s[d : d + 1]
            c = (tile_c * sc - tile_s * ss).astype(BF16)
            s_value = tile_s * sc + tile_c * ss
            s = s_value.astype(BF16)
            table_ref[d * r2 : d * r2 + rows, :focal] = c
            table_ref[d * r2 : d * r2 + rows, focal:] = (-s_value).astype(BF16)
            table_ref[d * r2 + rows : (d + 1) * r2, :focal] = s
            table_ref[d * r2 + rows : (d + 1) * r2, focal:] = c
        lhs = jnp.concatenate([y_ref[d, b] for d in range(sources)], axis=1)
        f = jnp.dot(lhs, table_ref[...], preferred_element_type=F32)
        residual = (f * (2.0 * scale) - measured_ref[b]).astype(BF16)
        spread = lax.dot_general(
            residual, table_ref[...], (((1,), (1,)), ((), ())), preferred_element_type=F32
        )
        for d in range(sources):
            h_ref[d, b] = spread[:, d * r2 : (d + 1) * r2].astype(BF16)


def weight_kernel(
    dims, pos_ref, box_ref, seg_ref, h_ref, x_ref, across_ref, out_ref,
    left_ref, pick_ref, tile_ref, shift_ref, table_ref, g_ref, weight_ref, sums_ref, slot_ref,
):
    (
        rows, cols, block, bands, half, band_total, per_row, pairs, vloc, sources, scale
    ) = dims
    step = pl.program_id(0)
    row0 = pos_ref[0] * rows
    r2 = 2 * rows
    nt = (((1,), (1,)), ((), ()))

    @pl.when(step == 0)
    def _():
        column_tables(pos_ref[1] * bands, bands, half, band_total, cols, tile_ref, shift_ref)
        m = iota((half, 2 * half), 0)
        v = iota((half, 2 * half), 1)
        upper = (v == half + m).astype(F32)
        lower = (v == half - 1 - m).astype(F32)
        even, odd = (upper + lower).astype(BF16), (upper - lower).astype(BF16)
        same = (iota((r2, r2), 0) == iota((r2, r2), 1)).astype(F32).astype(BF16)
        for b in range(bands):
            for p in range(2 * pairs):
                if sources:
                    block_h = jnp.concatenate(
                        [h_ref[d, b, p * vloc : (p + 1) * vloc, :] for d in range(sources)], axis=0
                    )
                else:
                    block_h = h_ref[b, p]

                def fold(mirror):
                    folded = jnp.dot(mirror, block_h, preferred_element_type=F32).astype(BF16)
                    return lax.dot_general(same, folded, nt, preferred_element_type=F32)

                plus, minus = fold(even), fold(odd)
                at = slice(p * r2, (p + 1) * r2)
                left_ref[at, 2 * b * half : (2 * b + 1) * half] = plus.astype(BF16)
                left_ref[at, (2 * b + 1) * half : (2 * b + 2) * half] = jnp.concatenate(
                    [-minus[rows:], minus[:rows]], axis=0
                ).astype(BF16)
        slot = iota((SROWS, r2), 0)
        lane = iota((SROWS, r2), 1)
        here = (row0 + lane % rows).astype(F32)
        low = jnp.zeros((SROWS, r2), F32)
        high = jnp.zeros((SROWS, r2), F32)
        for t in range(SROWS):
            low = jnp.where(slot == t, box_ref[0, t * per_row].astype(F32), low)
            high = jnp.where(slot == t, box_ref[1, t * per_row].astype(F32), high)
        mine = ((here >= low) & (here <= high)).astype(F32)
        down = mine * ((here - 0.5 * (low + high)) / (0.5 * (high - low + 1.0)))
        down_high = down.astype(BF16)
        pick_ref[:SROWS] = mine.astype(BF16)
        pick_ref[SROWS : 2 * SROWS] = down_high
        pick_ref[2 * SROWS :] = (down - down_high.astype(F32)).astype(BF16)
        out_ref[...] = jnp.zeros_like(out_ref)

    chunks = block // LANES
    write_table(table_ref, tile_ref, shift_ref, step * chunks, chunks, bands, half)
    g_ref[...] = lax.dot_general(left_ref[...], table_ref[...], nt, preferred_element_type=F32)
    for i in range(chunks):
        lanes = slice(i * LANES, (i + 1) * LANES)
        for g in range(0, rows, 16):
            value = jnp.zeros((16, LANES), F32)
            for p in range(2 * pairs):
                re = slice(p * r2 + g, p * r2 + g + 16)
                im = slice(p * r2 + rows + g, p * r2 + rows + g + 16)
                value = value + (
                    x_ref[re, lanes].astype(F32) * g_ref[im, lanes]
                    - x_ref[im, lanes].astype(F32) * g_ref[re, lanes]
                )
            high = value.astype(BF16)
            weight_ref[g : g + 16, lanes] = high
            weight_ref[rows + g : rows + g + 16, lanes] = (value - high.astype(F32)).astype(BF16)
    sums = jnp.dot(pick_ref[...], weight_ref[...], preferred_element_type=F32)
    sums_ref[step, 0] = sums[:SROWS]
    sums_ref[step, 1] = sums[:SROWS] * across_ref[...]
    sums_ref[step, 2] = sums[SROWS : 2 * SROWS] + sums[2 * SROWS :]

    @pl.when(step == pl.num_programs(0) - 1)
    def _():
        width = seg_ref.shape[1]
        for t, piece in tile_row_pieces(seg_ref, per_row, width):
            top, bottom = box_ref[0, t * per_row], box_ref[1, t * per_row]

            @pl.when((top < row0 + rows) & (bottom >= row0))
            def _():
                left, right = piece[5:6], piece[6:7]
                slot_ref[...] = jnp.zeros_like(slot_ref)

                def add(i, carry):
                    column = (iota((block, LANES), 0) + i * block).astype(F32)
                    inside = ((column >= left) & (column <= right)).astype(F32).astype(BF16)
                    terms = [sums_ref[i, q, t : t + 1, :] for q in range(3)]
                    highs = [x.astype(BF16) for x in terms]
                    lows = [(x - h.astype(F32)) for x, h in zip(terms, highs)]
                    stacked = jnp.concatenate(
                        [h.astype(F32) for h in highs] + lows + lows[:2], axis=0
                    ).astype(BF16)
                    slot_ref[...] += jnp.dot(stacked, inside, preferred_element_type=F32)
                    return carry

                lax.fori_loop(0, pl.num_programs(0), add, 0)
                for q in range(3):
                    out_ref[q, t : t + 1] = (slot_ref[q : q + 1] + slot_ref[q + 3 : q + 4]) * scale


def body(amplitude, seg_map, seg_box, seg_coeffs, probe_freq, probe_amp, measured):
    rows, cols = amplitude.shape
    owners = lax.axis_size("row")
    band_axis = lax.axis_size("band")
    total_rows = rows * owners
    bands, vloc, probes, _, focal = measured.shape
    pairs = probes // 2
    half = focal // 2
    band_total = bands * band_axis
    segments = seg_coeffs.shape[1]
    per_row = segments // SROWS
    arrays = 2 * pairs
    r2 = 2 * rows
    normf = 1.0 / math.sqrt(total_rows * cols)
    aligned = vloc % 16 == 0
    block = 512
    steps = cols // block

    pos = jnp.stack([lax.axis_index("row"), lax.axis_index("band")]).astype(jnp.int32)
    width = -(-(segments + LANES) // LANES) * LANES
    seg_table = jnp.pad(
        jnp.concatenate([seg_coeffs, seg_box.astype(F32)], axis=0), ((0, 1), (0, width - segments))
    )
    smem = pl.BlockSpec(memory_space=pltpu.SMEM)
    whole = pl.BlockSpec(memory_space=pltpu.VMEM)
    k_width = 2 * bands * half

    def resident(shape):
        return pl.BlockSpec(shape, lambda i: (0,) * len(shape), pipeline_mode=pl.Buffered(1))

    y_shape = (owners, bands, arrays * vloc, r2) if aligned else (bands, arrays, focal, r2)
    fields, across, half_way = pl.pallas_call(
        functools.partial(
            field_kernel,
            (rows, cols, block, bands, half, band_total, total_rows, per_row, pairs, vloc, aligned),
        ),
        grid=(steps,),
        in_specs=[
            smem, smem, smem, smem,
            resident((8, width)),
            pl.BlockSpec((rows, block), lambda i: (0, i)),
            pl.BlockSpec((rows, block), lambda i: (0, i)),
        ],
        out_specs=[
            pl.BlockSpec((arrays * r2, block), lambda i: (0, i)),
            pl.BlockSpec((SROWS, block), lambda i: (0, i)),
            pl.BlockSpec(y_shape, lambda i: (0,) * len(y_shape)),
        ],
        out_shape=[
            jax.ShapeDtypeStruct((arrays * r2, cols), BF16),
            jax.ShapeDtypeStruct((SROWS, cols), F32),
            jax.ShapeDtypeStruct(y_shape, BF16),
        ],
        scratch_shapes=[
            pltpu.VMEM((4, rows, LANES), F32),
            pltpu.VMEM((rows, LANES), jnp.int32),
            pltpu.VMEM((2, SROWS, LANES), F32),
            pltpu.VMEM((2 * pairs, rows, LANES), F32),
            pltpu.VMEM((2, LANES, bands * half), F32),
            pltpu.VMEM((2, cols // LANES, bands * half), F32),
            pltpu.VMEM((block, k_width), BF16),
            pltpu.VMEM((arrays * r2, k_width), F32),
            pltpu.VMEM((SROWS, block), jnp.int32),
        ],
        compiler_params=pltpu.CompilerParams(dimension_semantics=("arbitrary",)),
        name="field",
    )(pos, seg_box, probe_freq, probe_amp, seg_table, amplitude, seg_map)

    if not aligned:
        half_way = (
            half_way.reshape(bands, arrays, owners, vloc, r2)
            .transpose(2, 0, 1, 3, 4)
            .reshape(owners, bands, arrays * vloc, r2)
        )
    regrouped = lax.all_to_all(half_way, "row", split_axis=0, concat_axis=0, tiled=True)

    plus, minus = measured[:, :, 0::2], measured[:, :, 1::2]
    total, difference = plus + minus, plus - minus
    turned = jnp.stack([difference[:, :, :, 1], -difference[:, :, :, 0]], axis=3)
    targets = jnp.stack([total, turned], axis=3)
    targets = targets.transpose(0, 2, 3, 1, 4, 5).reshape(bands, arrays * vloc, 2 * focal)

    spread = pl.pallas_call(
        functools.partial(
            focal_kernel, (rows, cols, bands, focal, band_total, total_rows, owners, normf)
        ),
        in_specs=[smem, whole, whole],
        out_specs=whole,
        out_shape=jax.ShapeDtypeStruct((owners, bands, arrays * vloc, r2), BF16),
        scratch_shapes=[pltpu.VMEM((owners * r2, 2 * focal), BF16)],
        name="focal",
    )(pos, regrouped, targets)

    hidden = lax.all_to_all(spread, "row", split_axis=0, concat_axis=0, tiled=True)
    if not aligned:
        hidden = (
            hidden.reshape(owners, bands, arrays, vloc, r2)
            .transpose(1, 2, 0, 3, 4)
            .reshape(bands, arrays, focal, r2)
        )

    scale = 2.0 * normf / (band_total * probes)
    local = pl.pallas_call(
        functools.partial(
            weight_kernel,
            (
                rows, cols, block, bands, half, band_total, per_row, pairs, vloc,
                owners if aligned else 0, scale,
            ),
        ),
        grid=(steps,),
        in_specs=[
            smem, smem,
            resident((8, width)),
            resident(hidden.shape),
            pl.BlockSpec((arrays * r2, block), lambda i: (0, i)),
            pl.BlockSpec((SROWS, block), lambda i: (0, i)),
        ],
        out_specs=pl.BlockSpec((3, SROWS, LANES), lambda i: (0, 0, 0)),
        out_shape=jax.ShapeDtypeStruct((3, SROWS, LANES), F32),
        scratch_shapes=[
            pltpu.VMEM((arrays * r2, k_width), BF16),
            pltpu.VMEM((3 * SROWS, r2), BF16),
            pltpu.VMEM((2, LANES, bands * half), F32),
            pltpu.VMEM((2, cols // LANES, bands * half), F32),
            pltpu.VMEM((block, k_width), BF16),
            pltpu.VMEM((arrays * r2, block), F32),
            pltpu.VMEM((r2, block), BF16),
            pltpu.VMEM((steps, 3, SROWS, block), F32),
            pltpu.VMEM((8, LANES), F32),
        ],
        compiler_params=pltpu.CompilerParams(dimension_semantics=("arbitrary",)),
        name="weight",
    )(pos, seg_box, seg_table, hidden, fields, across)

    devices = owners * band_axis
    axes = ("band", "row")
    shares = local.reshape(devices, -1)
    mine = jnp.sum(lax.all_to_all(shares, axes, split_axis=0, concat_axis=0, tiled=True), axis=0)
    copies = jnp.broadcast_to(mine[None], shares.shape)
    gathered = lax.all_to_all(copies, axes, split_axis=0, concat_axis=0, tiled=True)
    return gathered.reshape(3, SROWS, LANES)[:, :, :per_row].reshape(3, segments)


def solution(mesh):
    in_specs = (
        P("row", None),
        P("row", None),
        P(),
        P(),
        P(),
        P(),
        P("band", "row", None, None, None),
    )
    return jax.shard_map(body, mesh=mesh, in_specs=in_specs, out_specs=P(), check_vma=False)
```

```python
import functools
import math

import jax
import jax.numpy as jnp
from jax import lax
from jax.experimental import pallas as pl
from jax.experimental.pallas import tpu as pltpu
from jax.sharding import PartitionSpec as P

SROWS = 16
SAMPLING = 0.5
SPREAD = 0.2
TWO_PI = 2.0 * math.pi
LANES = 128
F32 = jnp.float32
BF16 = jnp.bfloat16

SIN_HALF = (0.9999999971, -0.1666666029, 0.008333109246, -0.0001981365728, 2.616271295e-06)
COS_HALF = (0.9999999682, -0.4999993032, 0.04166421727, -0.001385868782, 2.327410856e-05)
SIN_WAVE = (0.9999999964, -0.166666488, 0.008331936401, -0.000194912576)
COS_WAVE = (0.9999999679, -0.499998396, 0.04165412354, -0.001357443708)
SIN_TURN = (
    6.283185307, -41.34170222, 81.60524741, -76.70580003,
    42.05775188, -15.08655272, 3.781282403, -0.6207370354,
)
COS_TURN = (
    0.9999999999, -19.73920874, 64.93938905, -85.45665775,
    60.24212493, -26.40463062, 7.800022219, -1.452987552,
)


def series(coeffs, t):
    value = jnp.full_like(t, coeffs[-1])
    for c in reversed(coeffs[:-1]):
        value = value * t + c
    return value


def turn_cos_sin(turns):
    t = turns - jnp.floor(turns + 0.5)
    square = t * t
    return series(COS_TURN, square), t * series(SIN_TURN, square)


def iota(shape, axis):
    return lax.broadcasted_iota(jnp.int32, shape, axis)


def focal_scale(m_positive, band, band_total):
    ratio = 1.0 + SPREAD * ((band.astype(F32) + 0.5) / band_total - 0.5)
    return m_positive / ratio


def band_lanes(first_band, bands, half, band_total, rows):
    pieces = []
    for b in range(bands):
        q = (iota((rows, half), 1).astype(F32) + 0.5) * SAMPLING
        band = jnp.full((rows, half), 1, jnp.int32) * (first_band + b)
        pieces.append(focal_scale(q, band, band_total))
    return jnp.concatenate(pieces, axis=1)


def column_tables(first_band, bands, half, band_total, cols, tile_ref, shift_ref):
    q = band_lanes(first_band, bands, half, band_total, LANES)
    c, s = turn_cos_sin(q * (iota(q.shape, 0).astype(F32) / cols))
    tile_ref[0] = c
    tile_ref[1] = s
    tiles = cols // (2 * LANES)
    q = band_lanes(first_band, bands, half, band_total, tiles)
    x = (iota(q.shape, 0).astype(F32) * LANES + 0.5) / cols - 0.5
    c, s = turn_cos_sin(q * x)
    shift_ref[0] = c
    shift_ref[1] = s


def write_table(cos_ref, sin_ref, tile_ref, shift_ref, first_tile, tiles):
    for i in range(tiles):
        sc = shift_ref[0, pl.ds(first_tile + i, 1), :]
        ss = shift_ref[1, pl.ds(first_tile + i, 1), :]
        for k in range(0, LANES, 16):
            tc = tile_ref[0, k : k + 16]
            ts = tile_ref[1, k : k + 16]
            rows = slice(i * LANES + k, i * LANES + k + 16)
            cos_ref[rows] = (tc * sc - ts * ss).astype(BF16)
            sin_ref[rows] = (ts * sc + tc * ss).astype(BF16)


def load_segments(coeffs_ref, boxes_ref, seg_ref):
    seg_ref[...] = jnp.zeros_like(seg_ref)
    seg_ref[0:3, : coeffs_ref.shape[1]] = coeffs_ref[...]
    seg_ref[3:7, : boxes_ref.shape[1]] = boxes_ref[...].astype(F32)


def reverse(x):
    back = LANES - 1 - iota((8, LANES), 1)
    pieces = [gather_lanes(x[k : k + 8], back) for k in range(0, x.shape[0], 8)]
    return pieces[0] if len(pieces) == 1 else jnp.concatenate(pieces, axis=0)


def gather_lanes(x, index):
    return jnp.take_along_axis(x, index, axis=1, mode="promise_in_bounds")


def tile_row_pieces(seg_ref, per_row, width):
    for t in range(SROWS):
        yield t, pltpu.roll(seg_ref[...], (width - t * per_row) % width, axis=1)[:, :LANES]


def field_kernel(
    dims, pos_ref, box_ref, freq_ref, amp_ref, coeffs_ref, boxes_ref,
    amplitude_ref, amplitude_far_ref, map_ref, map_far_ref,
    x_ref, across_ref, index_ref, y_ref,
    seg_ref, tables, bases, slot_tables, waves, tile_ref, shift_ref, cos_ref, sin_ref,
    even_ref, odd_ref, total_ref, slot_map,
):
    rows, cols, block, bands, half, band_total, total_rows, per_row, pairs, vloc, owners = dims
    step = pl.program_id(0)
    row0 = pos_ref[0] * rows
    chunks = block // LANES
    maps = (map_ref, map_far_ref)
    amplitudes = (amplitude_ref, amplitude_far_ref)

    @pl.when(step == 0)
    def _():
        load_segments(coeffs_ref, boxes_ref, seg_ref)
        width = seg_ref.shape[1]
        groups = rows // 8
        values = [[jnp.zeros((8, LANES), F32)] * 4 for _ in range(groups)]
        base = [jnp.zeros((8, LANES), jnp.int32)] * groups
        for t, piece in tile_row_pieces(seg_ref, per_row, width):
            part = [jnp.broadcast_to(piece[k : k + 1], (8, LANES)) for k in range(7)]
            low, high = part[3][:, :1], part[4][:, :1]
            mid_row = 0.5 * (part[3] + part[4])
            inv_row = 1.0 / (part[4] - part[3] + 1.0)
            slope, mid = 0.5 * part[1], 0.5 * (part[5] + part[6])
            inv = 2.0 / (part[6] - part[5] + 1.0)
            slot_tables[0, t : t + 1] = mid[:1]
            slot_tables[1, t : t + 1] = inv[:1]
            for g in range(groups):
                here = (row0 + g * 8 + iota((8, LANES), 0)).astype(F32)
                mine = (here >= low) & (here <= high)
                new = (0.5 * part[0] + part[2] * ((here - mid_row) * inv_row), slope, mid, inv)
                values[g] = [jnp.where(mine, n, v) for n, v in zip(new, values[g])]
                base[g] = jnp.where(mine, t * per_row, base[g])
        for g in range(groups):
            for k in range(4):
                tables[k, g * 8 : (g + 1) * 8] = values[g][k]
            bases[g * 8 : (g + 1) * 8] = base[g]
        y = ((row0 + iota((rows, LANES), 0)).astype(F32) + 0.5) / cols - total_rows / (2.0 * cols)
        for j in range(pairs):
            c, s = turn_cos_sin(freq_ref[j, 1].astype(F32) * y)
            waves[2 * j] = amp_ref[j] * c
            waves[2 * j + 1] = amp_ref[j] * s
        column_tables(pos_ref[1] * bands, bands, half, band_total, cols, tile_ref, shift_ref)
        total_ref[...] = jnp.zeros_like(total_ref)

    row = iota((8, block), 0)
    freq = jnp.zeros((8, block), F32)
    for j in range(pairs):
        freq = jnp.where(row // 2 == j, freq_ref[j, 0].astype(F32), freq)
    x = ((iota((8, block), 1) + step * block).astype(F32) + 0.5) / cols - 0.5
    turn_c, turn_s = turn_cos_sin(freq * x)
    columns_wave = jnp.where(row % 2 == 0, turn_s, turn_c)

    for t in range(SROWS):
        first = jnp.clip(box_ref[0, t * per_row] - row0, 0, rows - 1)
        for side in range(2):
            slot_map[side, t : t + 1, :] = maps[side][pl.ds(first, 1), :] - t * per_row

    write_table(cos_ref, sin_ref, tile_ref, shift_ref, step * chunks, chunks)

    for i in range(chunks):
        lanes = slice(i * LANES, (i + 1) * LANES)
        far_lanes = slice((chunks - 1 - i) * LANES, (chunks - i) * LANES)
        near_column = (iota((16, LANES), 1) + (step * block + i * LANES)).astype(F32)
        columns = (near_column, (cols - 1.0) - near_column)
        for side in range(2):
            for t in range(0, SROWS, 8):
                index = slot_map[side, t : t + 8, far_lanes if side else lanes] & (LANES - 1)
                if side:
                    index = reverse(index)
                mid = gather_lanes(slot_tables[0, t : t + 8], index)
                inv = gather_lanes(slot_tables[1, t : t + 8], index)
                across_ref[side, t : t + 8, lanes] = (columns[side][:8] - mid) * inv
                index_ref[side, t : t + 8, lanes] = index
        for g in range(0, rows, 16):
            here = slice(g, g + 16)
            fields = []
            for side in range(2):
                source = far_lanes if side else lanes
                index = maps[side][here, source] - bases[here]
                size = amplitudes[side][here, source].astype(F32)
                if side:
                    index, size = reverse(index), reverse(size)

                def pick(k):
                    return jnp.concatenate(
                        [
                            gather_lanes(tables[k, g + h : g + h + 8], index[h : h + 8])
                            for h in (0, 8)
                        ],
                        axis=0,
                    )

                half_phase = pick(0) + pick(1) * ((columns[side] - pick(2)) * pick(3))
                square = half_phase * half_phase
                s = half_phase * series(SIN_HALF, square)
                c = series(COS_HALF, square)
                twice = s + s
                fields.append((size * (1.0 - twice * s), size * (twice * c)))
            for j in range(pairs):
                from_sin = columns_wave[2 * j : 2 * j + 1, lanes] * waves[2 * j, here]
                from_cos = columns_wave[2 * j + 1 : 2 * j + 2, lanes] * waves[2 * j + 1, here]
                parts = []
                for wave in (from_cos + from_sin, from_cos - from_sin):
                    square = wave * wave
                    parts.append((series(COS_WAVE, square), wave * series(SIN_WAVE, square)))
                for k in range(2):
                    for o in range(2):
                        at = (4 * j + 2 * k + o) * rows + g
                        near = fields[0][o] * parts[0][k]
                        far = fields[1][o] * parts[1][k]
                        x_ref[0, at : at + 16, lanes] = near.astype(BF16)
                        x_ref[1, at : at + 16, lanes] = far.astype(BF16)
                        even_ref[at : at + 16, lanes] = (near + far).astype(BF16)
                        odd_ref[at : at + 16, lanes] = (near - far).astype(BF16)

    total_ref[0] += jnp.dot(even_ref[...], cos_ref[...], preferred_element_type=F32)
    total_ref[1] += jnp.dot(odd_ref[...], sin_ref[...], preferred_element_type=F32)

    @pl.when(step == pl.num_programs(0) - 1)
    def _():
        r2 = 2 * rows
        m = iota((half, half), 0)
        n = iota((half, half), 1)
        straight = (m == n).astype(F32).astype(BF16)
        turned = (m + n == half - 1).astype(F32).astype(BF16)
        nt = (((1,), (1,)), ((), ()))
        for b in range(bands):
            for p in range(2 * pairs):
                cos_part = total_ref[0, p * r2 : (p + 1) * r2, b * half : (b + 1) * half]
                sin_part = total_ref[1, p * r2 : (p + 1) * r2, b * half : (b + 1) * half]
                swapped = jnp.concatenate([sin_part[rows:], -sin_part[:rows]], axis=0)
                low = lax.dot_general(
                    turned, (cos_part - swapped).astype(BF16), nt, preferred_element_type=F32
                ).astype(BF16)
                high = lax.dot_general(
                    straight, (cos_part + swapped).astype(BF16), nt, preferred_element_type=F32
                ).astype(BF16)
                if owners:
                    each = half // vloc
                    for d in range(each):
                        piece = slice(d * vloc, (d + 1) * vloc)
                        y_ref[d, b, p * vloc : (p + 1) * vloc, :] = low[piece]
                        y_ref[each + d, b, p * vloc : (p + 1) * vloc, :] = high[piece]
                else:
                    y_ref[b, p, :half, :] = low
                    y_ref[b, p, half:, :] = high


def focal_kernel(dims, pos_ref, y_ref, measured_ref, h_ref, table_ref):
    rows, cols, bands, focal, band_total, total_rows, sources, scale = dims
    r2 = 2 * rows
    for b in range(bands):
        band = jnp.full((rows, focal), 1, jnp.int32) * (pos_ref[1] * bands + b)
        q = (iota((rows, focal), 1).astype(F32) + (0.5 - focal / 2)) * SAMPLING
        q = focal_scale(q, band, band_total)
        tile_c, tile_s = turn_cos_sin(q * (iota(q.shape, 0).astype(F32) / cols))
        first = iota((sources, focal), 0).astype(F32) * rows + 0.5
        y = first / cols - total_rows / (2.0 * cols)
        shift_c, shift_s = turn_cos_sin(jnp.broadcast_to(q[:1], y.shape) * y)
        for d in range(sources):
            sc, ss = shift_c[d : d + 1], shift_s[d : d + 1]
            c = (tile_c * sc - tile_s * ss).astype(BF16)
            s_value = tile_s * sc + tile_c * ss
            s = s_value.astype(BF16)
            table_ref[d * r2 : d * r2 + rows, :focal] = c
            table_ref[d * r2 : d * r2 + rows, focal:] = (-s_value).astype(BF16)
            table_ref[d * r2 + rows : (d + 1) * r2, :focal] = s
            table_ref[d * r2 + rows : (d + 1) * r2, focal:] = c
        lhs = jnp.concatenate([y_ref[d, b] for d in range(sources)], axis=1)
        f = jnp.dot(lhs, table_ref[...], preferred_element_type=F32)
        residual = (f * (2.0 * scale) - measured_ref[b]).astype(BF16)
        spread = lax.dot_general(
            residual, table_ref[...], (((1,), (1,)), ((), ())), preferred_element_type=F32
        )
        for d in range(sources):
            h_ref[d, b] = spread[:, d * r2 : (d + 1) * r2].astype(BF16)


def weight_kernel(
    dims, pos_ref, box_ref, h_ref, x_ref, across_ref, index_ref, out_ref,
    left_ref, pick_ref, tile_ref, shift_ref, cos_ref, sin_ref, p_ref, q_ref, weight_ref, sums_ref,
    term_ref,
):
    rows, cols, block, bands, half, band_total, per_row, pairs, vloc, sources, scale = dims
    step = pl.program_id(0)
    row0 = pos_ref[0] * rows
    r2 = 2 * rows
    nt = (((1,), (1,)), ((), ()))

    @pl.when(step == 0)
    def _():
        column_tables(pos_ref[1] * bands, bands, half, band_total, cols, tile_ref, shift_ref)
        m = iota((half, 2 * half), 0)
        v = iota((half, 2 * half), 1)
        upper = (v == half + m).astype(F32)
        lower = (v == half - 1 - m).astype(F32)
        even, odd = (upper + lower).astype(BF16), (upper - lower).astype(BF16)
        same = (iota((r2, r2), 0) == iota((r2, r2), 1)).astype(F32).astype(BF16)
        for b in range(bands):
            for p in range(2 * pairs):
                if sources:
                    block_h = jnp.concatenate(
                        [h_ref[d, b, p * vloc : (p + 1) * vloc, :] for d in range(sources)], axis=0
                    )
                else:
                    block_h = h_ref[b, p]

                def fold(mirror):
                    folded = jnp.dot(mirror, block_h, preferred_element_type=F32).astype(BF16)
                    return lax.dot_general(same, folded, nt, preferred_element_type=F32)

                plus, minus = fold(even), fold(odd)
                at = slice(p * r2, (p + 1) * r2)
                left_ref[0, at, b * half : (b + 1) * half] = plus.astype(BF16)
                left_ref[1, at, b * half : (b + 1) * half] = jnp.concatenate(
                    [-minus[rows:], minus[:rows]], axis=0
                ).astype(BF16)
        slot = iota((SROWS, r2), 0)
        lane = iota((SROWS, r2), 1)
        here = (row0 + lane % rows).astype(F32)
        low = jnp.zeros((SROWS, r2), F32)
        high = jnp.zeros((SROWS, r2), F32)
        for t in range(SROWS):
            low = jnp.where(slot == t, box_ref[0, t * per_row].astype(F32), low)
            high = jnp.where(slot == t, box_ref[1, t * per_row].astype(F32), high)
        mine = ((here >= low) & (here <= high)).astype(F32)
        down = mine * ((here - 0.5 * (low + high)) / (0.5 * (high - low + 1.0)))
        down_high = down.astype(BF16)
        pick_ref[:SROWS] = mine.astype(BF16)
        pick_ref[SROWS : 2 * SROWS] = down_high
        pick_ref[2 * SROWS :] = (down - down_high.astype(F32)).astype(BF16)
        out_ref[...] = jnp.zeros_like(out_ref)

    chunks = block // LANES
    write_table(cos_ref, sin_ref, tile_ref, shift_ref, step * chunks, chunks)
    p_ref[...] = lax.dot_general(left_ref[0], cos_ref[...], nt, preferred_element_type=F32)
    q_ref[...] = lax.dot_general(left_ref[1], sin_ref[...], nt, preferred_element_type=F32)
    for i in range(chunks):
        lanes = slice(i * LANES, (i + 1) * LANES)
        for g in range(0, rows, 16):
            near = jnp.zeros((16, LANES), F32)
            far = jnp.zeros((16, LANES), F32)
            for p in range(2 * pairs):
                re = slice(p * r2 + g, p * r2 + g + 16)
                im = slice(p * r2 + rows + g, p * r2 + rows + g + 16)
                p_re, p_im, q_re, q_im = p_ref[re, lanes], p_ref[im, lanes], q_ref[re, lanes], q_ref[im, lanes]
                near = near + (
                    x_ref[0, re, lanes].astype(F32) * (p_im + q_im)
                    - x_ref[0, im, lanes].astype(F32) * (p_re + q_re)
                )
                far = far + (
                    x_ref[1, re, lanes].astype(F32) * (p_im - q_im)
                    - x_ref[1, im, lanes].astype(F32) * (p_re - q_re)
                )
            for side, value in enumerate((near, far)):
                high = value.astype(BF16)
                to = slice(side * block + i * LANES, side * block + (i + 1) * LANES)
                weight_ref[g : g + 16, to] = high
                weight_ref[rows + g : rows + g + 16, to] = (value - high.astype(F32)).astype(BF16)
    sums = jnp.dot(pick_ref[...], weight_ref[...], preferred_element_type=F32)
    for side in range(2):
        mine = sums[:, side * block : (side + 1) * block]
        sums_ref[step, side, 0] = mine[:SROWS]
        sums_ref[step, side, 1] = mine[:SROWS] * across_ref[side]
        sums_ref[step, side, 2] = mine[SROWS : 2 * SROWS] + mine[2 * SROWS :]
        term_ref[step, side] = index_ref[side]

    @pl.when(step == pl.num_programs(0) - 1)
    def _():
        tops = [box_ref[0, t * per_row] for t in range(SROWS)]
        bottoms = [box_ref[1, t * per_row] for t in range(SROWS)]
        first = sum((bottom < row0).astype(jnp.int32) for bottom in bottoms)
        last = sum((top < row0 + rows).astype(jnp.int32) for top in tops)

        def tile_row(t, carry):
            def add(i, total):
                for side in range(2):
                    index = term_ref[i, side, pl.ds(t, 1), :]
                    inside = (iota((LANES, block), 0) == index).astype(F32).astype(BF16)
                    terms = [sums_ref[i, side, q, pl.ds(t, 1), :] for q in range(3)]
                    highs = [x.astype(BF16).astype(F32) for x in terms]
                    lows = [x - h for x, h in zip(terms, highs)]
                    stacked = jnp.concatenate(highs + lows + lows[:2], axis=0).astype(BF16)
                    total = total + lax.dot_general(
                        stacked, inside, nt, preferred_element_type=F32
                    )
                return total

            total = lax.fori_loop(0, pl.num_programs(0), add, jnp.zeros((8, LANES), F32))
            for q in range(3):
                out_ref[q, pl.ds(t, 1)] = (total[q : q + 1] + total[q + 3 : q + 4]) * scale
            return carry

        lax.fori_loop(first, last, tile_row, 0)


def body(amplitude, seg_map, seg_box, seg_coeffs, probe_freq, probe_amp, measured):
    rows, cols = amplitude.shape
    owners = lax.axis_size("row")
    band_axis = lax.axis_size("band")
    total_rows = rows * owners
    bands, vloc, probes, _, focal = measured.shape
    pairs = probes // 2
    half = focal // 2
    band_total = bands * band_axis
    segments = seg_coeffs.shape[1]
    per_row = segments // SROWS
    arrays = 2 * pairs
    r2 = 2 * rows
    normf = 1.0 / math.sqrt(total_rows * cols)
    aligned = vloc % 16 == 0
    block = 512
    blocks = cols // block
    steps = blocks // 2

    pos = jnp.stack([lax.axis_index("row"), lax.axis_index("band")]).astype(jnp.int32)
    width = -(-(segments + LANES) // LANES) * LANES
    smem = pl.BlockSpec(memory_space=pltpu.SMEM)
    whole = pl.BlockSpec(memory_space=pltpu.VMEM)
    k_width = bands * half

    def resident(shape):
        return pl.BlockSpec(shape, lambda i: (0,) * len(shape), pipeline_mode=pl.Buffered(1))

    near = pl.BlockSpec((rows, block), lambda i: (0, i))
    far = pl.BlockSpec((rows, block), lambda i: (0, blocks - 1 - i))
    x_spec = pl.BlockSpec((2, arrays * r2, block), lambda i: (0, 0, i))
    slot_spec = pl.BlockSpec((2, SROWS, block), lambda i: (0, 0, i))
    y_shape = (owners, bands, arrays * vloc, r2) if aligned else (bands, arrays, focal, r2)
    fields, across, index, half_way = pl.pallas_call(
        functools.partial(
            field_kernel,
            (rows, cols, block, bands, half, band_total, total_rows, per_row, pairs, vloc, aligned),
        ),
        grid=(steps,),
        in_specs=[
            smem, smem, smem, smem,
            resident(seg_coeffs.shape),
            resident(seg_box.shape),
            near, far, near, far,
        ],
        out_specs=[
            x_spec,
            slot_spec,
            slot_spec,
            pl.BlockSpec(y_shape, lambda i: (0,) * len(y_shape)),
        ],
        out_shape=[
            jax.ShapeDtypeStruct((2, arrays * r2, cols // 2), BF16),
            jax.ShapeDtypeStruct((2, SROWS, cols // 2), F32),
            jax.ShapeDtypeStruct((2, SROWS, cols // 2), jnp.int32),
            jax.ShapeDtypeStruct(y_shape, BF16),
        ],
        scratch_shapes=[
            pltpu.VMEM((8, width), F32),
            pltpu.VMEM((4, rows, LANES), F32),
            pltpu.VMEM((rows, LANES), jnp.int32),
            pltpu.VMEM((2, SROWS, LANES), F32),
            pltpu.VMEM((2 * pairs, rows, LANES), F32),
            pltpu.VMEM((2, LANES, k_width), F32),
            pltpu.VMEM((2, cols // (2 * LANES), k_width), F32),
            pltpu.VMEM((block, k_width), BF16),
            pltpu.VMEM((block, k_width), BF16),
            pltpu.VMEM((arrays * r2, block), BF16),
            pltpu.VMEM((arrays * r2, block), BF16),
            pltpu.VMEM((2, arrays * r2, k_width), F32),
            pltpu.VMEM((2, SROWS, block), jnp.int32),
        ],
        compiler_params=pltpu.CompilerParams(dimension_semantics=("arbitrary",)),
        name="field",
    )(pos, seg_box, probe_freq, probe_amp, seg_coeffs, seg_box,
      amplitude, amplitude, seg_map, seg_map)

    if not aligned:
        half_way = (
            half_way.reshape(bands, arrays, owners, vloc, r2)
            .transpose(2, 0, 1, 3, 4)
            .reshape(owners, bands, arrays * vloc, r2)
        )
    regrouped = lax.all_to_all(half_way, "row", split_axis=0, concat_axis=0, tiled=True)

    plus, minus = measured[:, :, 0::2], measured[:, :, 1::2]
    total, difference = plus + minus, plus - minus
    turned = jnp.stack([difference[:, :, :, 1], -difference[:, :, :, 0]], axis=3)
    targets = jnp.stack([total, turned], axis=3)
    targets = targets.transpose(0, 2, 3, 1, 4, 5).reshape(bands, arrays * vloc, 2 * focal)

    spread = pl.pallas_call(
        functools.partial(
            focal_kernel, (rows, cols, bands, focal, band_total, total_rows, owners, normf)
        ),
        in_specs=[smem, whole, whole],
        out_specs=whole,
        out_shape=jax.ShapeDtypeStruct((owners, bands, arrays * vloc, r2), BF16),
        scratch_shapes=[pltpu.VMEM((owners * r2, 2 * focal), BF16)],
        name="focal",
    )(pos, regrouped, targets)

    hidden = lax.all_to_all(spread, "row", split_axis=0, concat_axis=0, tiled=True)
    if not aligned:
        hidden = (
            hidden.reshape(owners, bands, arrays, vloc, r2)
            .transpose(1, 2, 0, 3, 4)
            .reshape(bands, arrays, focal, r2)
        )

    scale = 2.0 * normf / (band_total * probes)
    local = pl.pallas_call(
        functools.partial(
            weight_kernel,
            (
                rows, cols, block, bands, half, band_total, per_row, pairs, vloc,
                owners if aligned else 0, scale,
            ),
        ),
        grid=(steps,),
        in_specs=[smem, smem, resident(hidden.shape), x_spec, slot_spec, slot_spec],
        out_specs=pl.BlockSpec((3, SROWS, LANES), lambda i: (0, 0, 0)),
        out_shape=jax.ShapeDtypeStruct((3, SROWS, LANES), F32),
        scratch_shapes=[
            pltpu.VMEM((2, arrays * r2, k_width), BF16),
            pltpu.VMEM((3 * SROWS, r2), BF16),
            pltpu.VMEM((2, LANES, k_width), F32),
            pltpu.VMEM((2, cols // (2 * LANES), k_width), F32),
            pltpu.VMEM((block, k_width), BF16),
            pltpu.VMEM((block, k_width), BF16),
            pltpu.VMEM((arrays * r2, block), F32),
            pltpu.VMEM((arrays * r2, block), F32),
            pltpu.VMEM((r2, 2 * block), BF16),
            pltpu.VMEM((steps, 2, 3, SROWS, block), F32),
            pltpu.VMEM((steps, 2, SROWS, block), jnp.int32),
        ],
        compiler_params=pltpu.CompilerParams(dimension_semantics=("arbitrary",)),
        name="weight",
    )(pos, seg_box, hidden, fields, across, index)

    devices = owners * band_axis
    axes = ("band", "row")
    shares = local.reshape(devices, -1)
    mine = jnp.sum(lax.all_to_all(shares, axes, split_axis=0, concat_axis=0, tiled=True), axis=0)
    copies = jnp.broadcast_to(mine[None], shares.shape)
    gathered = lax.all_to_all(copies, axes, split_axis=0, concat_axis=0, tiled=True)
    return gathered.reshape(3, SROWS, LANES)[:, :, :per_row].reshape(3, segments)


def solution(mesh):
    in_specs = (
        P("row", None),
        P("row", None),
        P(),
        P(),
        P(),
        P(),
        P("band", "row", None, None, None),
    )
    return jax.shard_map(body, mesh=mesh, in_specs=in_specs, out_specs=P(), check_vma=False)
```

```python
import functools
import math

import jax
import jax.numpy as jnp
from jax import lax
from jax.experimental import pallas as pl
from jax.experimental.pallas import tpu as pltpu
from jax.sharding import PartitionSpec as P

SROWS = 16
SAMPLING = 0.5
SPREAD = 0.2
TWO_PI = 2.0 * math.pi
LANES = 128
F32 = jnp.float32
BLOCKS = (512, 2048, 512)
BF16 = jnp.bfloat16

SIN_HALF = (0.9999999971, -0.1666666029, 0.008333109246, -0.0001981365728, 2.616271295e-06)
COS_HALF = (0.9999999682, -0.4999993032, 0.04166421727, -0.001385868782, 2.327410856e-05)
SIN_WAVE = (0.9999999964, -0.166666488, 0.008331936401, -0.000194912576)
COS_WAVE = (0.9999999679, -0.499998396, 0.04165412354, -0.001357443708)
SIN_TURN = (
    6.283185307, -41.34170222, 81.60524741, -76.70580003,
    42.05775188, -15.08655272, 3.781282403, -0.6207370354,
)
COS_TURN = (
    0.9999999999, -19.73920874, 64.93938905, -85.45665775,
    60.24212493, -26.40463062, 7.800022219, -1.452987552,
)


def series(coeffs, t):
    value = jnp.full_like(t, coeffs[-1])
    for c in reversed(coeffs[:-1]):
        value = value * t + c
    return value


def turn_cos_sin(turns):
    t = turns - jnp.floor(turns + 0.5)
    square = t * t
    return series(COS_TURN, square), t * series(SIN_TURN, square)


def iota(shape, axis):
    return lax.broadcasted_iota(jnp.int32, shape, axis)


def focal_scale(m_positive, band, band_total):
    ratio = 1.0 + SPREAD * ((band.astype(F32) + 0.5) / band_total - 0.5)
    return m_positive / ratio


def band_lanes(first_band, bands, half, band_total, rows):
    pieces = []
    for b in range(bands):
        q = (iota((rows, half), 1).astype(F32) + 0.5) * SAMPLING
        band = jnp.full((rows, half), 1, jnp.int32) * (first_band + b)
        pieces.append(focal_scale(q, band, band_total))
    return jnp.concatenate(pieces, axis=1)


def column_tables(first_band, bands, half, band_total, cols, tile_ref, shift_ref):
    q = band_lanes(first_band, bands, half, band_total, LANES)
    c, s = turn_cos_sin(q * (iota(q.shape, 0).astype(F32) / cols))
    tile_ref[0] = c
    tile_ref[1] = s
    tiles = cols // (2 * LANES)
    q = band_lanes(first_band, bands, half, band_total, tiles)
    x = (iota(q.shape, 0).astype(F32) * LANES + 0.5) / cols - 0.5
    c, s = turn_cos_sin(q * x)
    shift_ref[0] = c
    shift_ref[1] = s


def write_table(cos_ref, sin_ref, tile_ref, shift_ref, first_tile, tiles):
    for i in range(tiles):
        sc = shift_ref[0, pl.ds(first_tile + i, 1), :]
        ss = shift_ref[1, pl.ds(first_tile + i, 1), :]
        for k in range(0, LANES, 16):
            tc = tile_ref[0, k : k + 16]
            ts = tile_ref[1, k : k + 16]
            rows = slice(i * LANES + k, i * LANES + k + 16)
            cos_ref[rows] = (tc * sc - ts * ss).astype(BF16)
            sin_ref[rows] = (ts * sc + tc * ss).astype(BF16)


def load_segments(coeffs_ref, boxes_ref, seg_ref):
    seg_ref[...] = jnp.zeros_like(seg_ref)
    seg_ref[0:3, : coeffs_ref.shape[1]] = coeffs_ref[...]
    seg_ref[3:7, : boxes_ref.shape[1]] = boxes_ref[...].astype(F32)


def reverse(x):
    back = LANES - 1 - iota((8, LANES), 1)
    pieces = [gather_lanes(x[k : k + 8], back) for k in range(0, x.shape[0], 8)]
    return pieces[0] if len(pieces) == 1 else jnp.concatenate(pieces, axis=0)


def gather_lanes(x, index):
    return jnp.take_along_axis(x, index, axis=1, mode="promise_in_bounds")


def tile_row_pieces(seg_ref, per_row, width):
    for t in range(SROWS):
        yield t, pltpu.roll(seg_ref[...], (width - t * per_row) % width, axis=1)[:, :LANES]


def probe_setup(pos_ref, freq_ref, amp_ref, j, rows, cols, total_rows, waves):
    row = pos_ref[0] * rows + iota((rows, LANES), 0)
    y = (row.astype(F32) + 0.5) / cols - total_rows / (2.0 * cols)
    c, s = turn_cos_sin(freq_ref[j, 1].astype(F32) * y)
    waves[2 * j] = amp_ref[j] * c
    waves[2 * j + 1] = amp_ref[j] * s


def column_wave(freq_ref, pairs, step, block, cols):
    row = iota((8, block), 0)
    freq = jnp.zeros((8, block), F32)
    for j in range(pairs):
        freq = jnp.where(row // 2 == j, freq_ref[j, 0].astype(F32), freq)
    x = ((iota((8, block), 1) + step * block).astype(F32) + 0.5) / cols - 0.5
    c, s = turn_cos_sin(freq * x)
    return jnp.where(row % 2 == 0, s, c)


def emit_pair(j, column, waves, fields, here, lanes, g, rows, x_ref, even_ref, odd_ref):
    from_sin = column[2 * j : 2 * j + 1, lanes] * waves[2 * j, here]
    from_cos = column[2 * j + 1 : 2 * j + 2, lanes] * waves[2 * j + 1, here]
    parts = []
    for wave in (from_cos + from_sin, from_cos - from_sin):
        square = wave * wave
        parts.append(
            (
                series(COS_WAVE, square).astype(BF16),
                (wave * series(SIN_WAVE, square)).astype(BF16),
            )
        )
    for k in range(2):
        for o in range(2):
            at = (2 * k + o) * rows + g
            near = fields[0][o] * parts[0][k]
            far = fields[1][o] * parts[1][k]
            x_ref[j, 0, at : at + 16, lanes] = near
            x_ref[j, 1, at : at + 16, lanes] = far
            at = at + 4 * j * rows
            even_ref[at : at + 16, lanes] = near + far
            odd_ref[at : at + 16, lanes] = near - far


def emit_half_way(pairs, total_ref, y_ref, rows, bands, half, vloc, owners):
    r2 = 2 * rows
    m = iota((half, half), 0)
    n = iota((half, half), 1)
    straight = (m == n).astype(F32).astype(BF16)
    turned = (m + n == half - 1).astype(F32).astype(BF16)
    nt = (((1,), (1,)), ((), ()))
    for b in range(bands):
        for p in range(2 * pairs):
            at = slice(p * r2, (p + 1) * r2)
            cos_part = total_ref[0, at, b * half : (b + 1) * half]
            sin_part = total_ref[1, at, b * half : (b + 1) * half]
            swapped = jnp.concatenate([sin_part[rows:], -sin_part[:rows]], axis=0)
            low = lax.dot_general(
                turned, (cos_part - swapped).astype(BF16), nt, preferred_element_type=F32
            ).astype(BF16)
            high = lax.dot_general(
                straight, (cos_part + swapped).astype(BF16), nt, preferred_element_type=F32
            ).astype(BF16)
            if owners:
                each = half // vloc
                for d in range(each):
                    own = slice(d * vloc, (d + 1) * vloc)
                    y_ref[d, b, p * vloc : (p + 1) * vloc, :] = low[own]
                    y_ref[each + d, b, p * vloc : (p + 1) * vloc, :] = high[own]
            else:
                y_ref[b, p, :half, :] = low
                y_ref[b, p, half:, :] = high


def field_kernel(
    dims, pos_ref, box_ref, freq_ref, amp_ref, coeffs_ref, boxes_ref,
    amplitude_ref, amplitude_far_ref, map_ref, map_far_ref,
    x_ref, tile_ref, shift_ref, across_ref, index_ref, y_ref, *rest
):
    dims, pairs = dims
    (
        seg_ref, tables, bases, slot_tables, waves, cos_ref, sin_ref, even_ref, odd_ref, total_ref, slot_map,
    ) = rest
    rows, cols, block, bands, half, band_total, total_rows, per_row, vloc, owners = dims
    step = pl.program_id(0)
    row0 = pos_ref[0] * rows
    chunks = block // LANES
    maps = (map_ref, map_far_ref)
    amplitudes = (amplitude_ref, amplitude_far_ref)

    @pl.when(step == 0)
    def _():
        load_segments(coeffs_ref, boxes_ref, seg_ref)
        width = seg_ref.shape[1]
        groups = rows // 8
        values = [[jnp.zeros((8, LANES), F32)] * 3 for _ in range(groups)]
        base = [jnp.zeros((8, LANES), jnp.int32)] * groups
        for t, piece in tile_row_pieces(seg_ref, per_row, width):
            part = [jnp.broadcast_to(piece[k : k + 1], (8, LANES)) for k in range(7)]
            low, high = part[3][:, :1], part[4][:, :1]
            mid_row = 0.5 * (part[3] + part[4])
            inv_row = 1.0 / (part[4] - part[3] + 1.0)
            mid = 0.5 * (part[5] + part[6])
            inv = 2.0 / (part[6] - part[5] + 1.0)
            slope = 0.5 * part[1] * inv
            slot_tables[0, t : t + 1] = mid[:1]
            slot_tables[1, t : t + 1] = inv[:1]
            for g in range(groups):
                here = (row0 + g * 8 + iota((8, LANES), 0)).astype(F32)
                mine = (here >= low) & (here <= high)
                new = (0.5 * part[0] + part[2] * ((here - mid_row) * inv_row), slope, mid)
                values[g] = [jnp.where(mine, n, v) for n, v in zip(new, values[g])]
                base[g] = jnp.where(mine, t * per_row, base[g])
        for g in range(groups):
            for k in range(3):
                tables[k, g * 8 : (g + 1) * 8] = values[g][k]
            bases[g * 8 : (g + 1) * 8] = base[g]
        for j in range(pairs):
            probe_setup(pos_ref, freq_ref, amp_ref, j, rows, cols, total_rows, waves)
        column_tables(pos_ref[1] * bands, bands, half, band_total, cols, tile_ref, shift_ref)
        total_ref[...] = jnp.zeros_like(total_ref)

    for t in range(SROWS):
        first = jnp.clip(box_ref[0, t * per_row] - row0, 0, rows - 1)
        for side in range(2):
            slot_map[side, t : t + 1, :] = maps[side][pl.ds(first, 1), :] - t * per_row

    column = column_wave(freq_ref, pairs, step, block, cols)
    write_table(cos_ref, sin_ref, tile_ref, shift_ref, step * chunks, chunks)

    for i in range(chunks):
        lanes = slice(i * LANES, (i + 1) * LANES)
        far_lanes = slice((chunks - 1 - i) * LANES, (chunks - i) * LANES)
        near_column = (iota((8, LANES), 1) + (step * block + i * LANES)).astype(F32)
        columns = (near_column, (cols - 1.0) - near_column)
        for side in range(2):
            for t in range(0, SROWS, 8):
                index = slot_map[side, t : t + 8, far_lanes if side else lanes] & (LANES - 1)
                if side:
                    index = reverse(index)
                mid = gather_lanes(slot_tables[0, t : t + 8], index)
                inv = gather_lanes(slot_tables[1, t : t + 8], index)
                across_ref[side, t : t + 8, lanes] = (columns[side] - mid) * inv
                index_ref[side, t : t + 8, lanes] = index
        for g in range(0, rows, 16):
            here = slice(g, g + 16)
            fields = []
            for side in range(2):
                source = far_lanes if side else lanes
                size = amplitudes[side][here, source].astype(F32)
                halves = []
                for h in (0, 8):
                    own = slice(g + h, g + h + 8)
                    index = maps[side][own, source] - bases[own]
                    if side:
                        index = reverse(index)
                    half_phase = gather_lanes(tables[0, own], index) + gather_lanes(
                        tables[1, own], index
                    ) * (columns[side] - gather_lanes(tables[2, own], index))
                    square = half_phase * half_phase
                    s = half_phase * series(SIN_HALF, square)
                    c = series(COS_HALF, square)
                    twice = s + s
                    own_size = size[h : h + 8]
                    if side:
                        own_size = reverse(own_size)
                    halves.append((own_size * (1.0 - twice * s), own_size * (twice * c)))
                both = [
                    jnp.concatenate([halves[0][o], halves[1][o]], axis=0).astype(BF16)
                    for o in range(2)
                ]
                fields.append(both)
            for j in range(pairs):
                emit_pair(
                    j, column, waves, fields, here, lanes, g, rows, x_ref, even_ref, odd_ref
                )

    total_ref[0] += jnp.dot(even_ref[...], cos_ref[...], preferred_element_type=F32)
    total_ref[1] += jnp.dot(odd_ref[...], sin_ref[...], preferred_element_type=F32)

    @pl.when(step == pl.num_programs(0) - 1)
    def _():
        emit_half_way(pairs, total_ref, y_ref, rows, bands, half, vloc, owners)


def row_table_kernel(dims, pos_ref, table_ref):
    rows, cols, bands, focal, band_total, total_rows, sources = dims
    r2 = 2 * rows
    for b in range(bands):
        band = jnp.full((rows, focal), 1, jnp.int32) * (pos_ref[1] * bands + b)
        q = (iota((rows, focal), 1).astype(F32) + (0.5 - focal / 2)) * SAMPLING
        q = focal_scale(q, band, band_total)
        tile_c, tile_s = turn_cos_sin(q * (iota(q.shape, 0).astype(F32) / cols))
        first = iota((sources, focal), 0).astype(F32) * rows + 0.5
        y = first / cols - total_rows / (2.0 * cols)
        shift_c, shift_s = turn_cos_sin(jnp.broadcast_to(q[:1], y.shape) * y)
        for d in range(sources):
            sc, ss = shift_c[d : d + 1], shift_s[d : d + 1]
            c = (tile_c * sc - tile_s * ss).astype(BF16)
            s_value = tile_s * sc + tile_c * ss
            s = s_value.astype(BF16)
            table_ref[b, d * r2 : d * r2 + rows, :focal] = c
            table_ref[b, d * r2 : d * r2 + rows, focal:] = (-s_value).astype(BF16)
            table_ref[b, d * r2 + rows : (d + 1) * r2, :focal] = s
            table_ref[b, d * r2 + rows : (d + 1) * r2, focal:] = c


def focal_kernel(dims, y_ref, target_ref, table_ref, h_ref):
    rows, sources, scale = dims
    r2 = 2 * rows
    lhs = jnp.concatenate([y_ref[d] for d in range(sources)], axis=1)
    f = jnp.dot(lhs, table_ref[...], preferred_element_type=F32)
    residual = (f * (2.0 * scale) - target_ref[...]).astype(BF16)
    spread = lax.dot_general(
        residual, table_ref[...], (((1,), (1,)), ((), ())), preferred_element_type=F32
    )
    for d in range(sources):
        h_ref[d] = spread[:, d * r2 : (d + 1) * r2].astype(BF16)


def fold_hidden(pairs, h_ref, left_ref, rows, bands, half, vloc, sources):
    r2 = 2 * rows
    nt = (((1,), (1,)), ((), ()))
    m = iota((half, 2 * half), 0)
    v = iota((half, 2 * half), 1)
    upper = (v == half + m).astype(F32)
    lower = (v == half - 1 - m).astype(F32)
    even, odd = (upper + lower).astype(BF16), (upper - lower).astype(BF16)
    same = (iota((r2, r2), 0) == iota((r2, r2), 1)).astype(F32).astype(BF16)
    for b in range(bands):
        for p in range(2 * pairs):
            if sources:
                block_h = jnp.concatenate(
                    [h_ref[d, b, p * vloc : (p + 1) * vloc, :] for d in range(sources)], axis=0
                )
            else:
                block_h = h_ref[b, p]

            def fold(mirror):
                folded = jnp.dot(mirror, block_h, preferred_element_type=F32).astype(BF16)
                return lax.dot_general(same, folded, nt, preferred_element_type=F32)

            plus, minus = fold(even), fold(odd)
            at = slice(p * r2, (p + 1) * r2)
            left_ref[0, at, b * half : (b + 1) * half] = plus.astype(BF16)
            left_ref[1, at, b * half : (b + 1) * half] = jnp.concatenate(
                [-minus[rows:], minus[:rows]], axis=0
            ).astype(BF16)


def weight_kernel(
    dims, pos_ref, box_ref, h_ref, x_ref, tile_ref, shift_ref, across_ref, index_ref,
    out_ref, left_ref, pick_ref, cos_ref, sin_ref, p_ref, q_ref, weight_ref, sums_ref, term_ref,
):
    rows, cols, block, part, bands, half, per_row, pairs, vloc, sources, scale = dims
    step = pl.program_id(0)
    row0 = pos_ref[0] * rows
    r2 = 2 * rows
    nt = (((1,), (1,)), ((), ()))

    @pl.when(step == 0)
    def _():
        fold_hidden(pairs, h_ref, left_ref, rows, bands, half, vloc, sources)
        slot = iota((SROWS, r2), 0)
        lane = iota((SROWS, r2), 1)
        here = (row0 + lane % rows).astype(F32)
        low = jnp.zeros((SROWS, r2), F32)
        high = jnp.zeros((SROWS, r2), F32)
        for t in range(SROWS):
            low = jnp.where(slot == t, box_ref[0, t * per_row].astype(F32), low)
            high = jnp.where(slot == t, box_ref[1, t * per_row].astype(F32), high)
        mine = ((here >= low) & (here <= high)).astype(F32)
        down = mine * ((here - 0.5 * (low + high)) / (0.5 * (high - low + 1.0)))
        down_high = down.astype(BF16)
        pick_ref[:SROWS] = mine.astype(BF16)
        pick_ref[SROWS : 2 * SROWS] = down_high
        pick_ref[2 * SROWS :] = (down - down_high.astype(F32)).astype(BF16)
        out_ref[...] = jnp.zeros_like(out_ref)

    tiles = part // LANES
    for k in range(block // part):
        slot = k % 2
        write_table(
            cos_ref.at[slot], sin_ref.at[slot], tile_ref, shift_ref,
            step * (block // LANES) + k * tiles, tiles,
        )
        p_ref[slot] = lax.dot_general(left_ref[0], cos_ref[slot], nt, preferred_element_type=F32)
        q_ref[slot] = lax.dot_general(left_ref[1], sin_ref[slot], nt, preferred_element_type=F32)
        for i in range(tiles):
            lanes = slice(i * LANES, (i + 1) * LANES)
            at = slice(k * part + i * LANES, k * part + (i + 1) * LANES)
            for g in range(0, rows, 16):
                near, far = None, None
                for p in range(2 * pairs):
                    j, first = divmod(p, 2)
                    re = slice(p * r2 + g, p * r2 + g + 16)
                    im = slice(p * r2 + rows + g, p * r2 + rows + g + 16)
                    xre = slice(first * r2 + g, first * r2 + g + 16)
                    xim = slice(first * r2 + rows + g, first * r2 + rows + g + 16)
                    p_re, p_im = p_ref[slot, re, lanes], p_ref[slot, im, lanes]
                    q_re, q_im = q_ref[slot, re, lanes], q_ref[slot, im, lanes]
                    x = [
                        [x_ref[j, side, rows_, at].astype(F32) for rows_ in (xre, xim)]
                        for side in range(2)
                    ]
                    near_term = x[0][0] * (p_im + q_im) - x[0][1] * (p_re + q_re)
                    far_term = x[1][0] * (p_im - q_im) - x[1][1] * (p_re - q_re)
                    near = near_term if near is None else near + near_term
                    far = far_term if far is None else far + far_term
                for side, value in enumerate((near, far)):
                    high = value.astype(BF16)
                    to = slice(side * block + at.start, side * block + at.stop)
                    weight_ref[g : g + 16, to] = high
                    weight_ref[rows + g : rows + g + 16, to] = (
                        value - high.astype(F32)
                    ).astype(BF16)
    sums = jnp.dot(pick_ref[...], weight_ref[...], preferred_element_type=F32)
    for side in range(2):
        mine = sums[:, side * block : (side + 1) * block]
        sums_ref[step, side, 0] = mine[:SROWS]
        sums_ref[step, side, 1] = mine[:SROWS] * across_ref[side]
        sums_ref[step, side, 2] = mine[SROWS : 2 * SROWS] + mine[2 * SROWS :]
        term_ref[step, side] = index_ref[side]

    @pl.when(step == pl.num_programs(0) - 1)
    def _():
        tops = [box_ref[0, t * per_row] for t in range(SROWS)]
        bottoms = [box_ref[1, t * per_row] for t in range(SROWS)]
        first = sum((bottom < row0).astype(jnp.int32) for bottom in bottoms)
        last = sum((top < row0 + rows).astype(jnp.int32) for top in tops)

        def tile_row(t, carry):
            def add(i, total):
                for side in range(2):
                    index = term_ref[i, side, pl.ds(t, 1), :]
                    inside = (iota((LANES, block), 0) == index).astype(F32).astype(BF16)
                    terms = [sums_ref[i, side, q, pl.ds(t, 1), :] for q in range(3)]
                    highs = [x.astype(BF16).astype(F32) for x in terms]
                    lows = [x - h for x, h in zip(terms, highs)]
                    stacked = jnp.concatenate(highs + lows + lows[:2], axis=0).astype(BF16)
                    total = total + lax.dot_general(
                        stacked, inside, nt, preferred_element_type=F32
                    )
                return total

            total = lax.fori_loop(0, pl.num_programs(0), add, jnp.zeros((8, LANES), F32))
            for q in range(3):
                out_ref[q, pl.ds(t, 1)] = (total[q : q + 1] + total[q + 3 : q + 4]) * scale
            return carry

        lax.fori_loop(first, last, tile_row, 0)


def body(amplitude, seg_map, seg_box, seg_coeffs, probe_freq, probe_amp, measured):
    rows, cols = amplitude.shape
    owners = lax.axis_size("row")
    band_axis = lax.axis_size("band")
    total_rows = rows * owners
    bands, vloc, probes, _, focal = measured.shape
    pairs = probes // 2
    half = focal // 2
    band_total = bands * band_axis
    segments = seg_coeffs.shape[1]
    per_row = segments // SROWS
    r2 = 2 * rows
    normf = 1.0 / math.sqrt(total_rows * cols)
    aligned = vloc % 16 == 0
    half_cols = cols // 2
    field_block, block, part = BLOCKS
    k_width = bands * half

    pos = jnp.stack([lax.axis_index("row"), lax.axis_index("band")]).astype(jnp.int32)
    width = -(-(segments + LANES) // LANES) * LANES
    smem = pl.BlockSpec(memory_space=pltpu.SMEM)
    whole = pl.BlockSpec(memory_space=pltpu.VMEM)
    params = pltpu.CompilerParams(dimension_semantics=("arbitrary",))

    def resident(shape):
        return pl.BlockSpec(shape, lambda i: (0,) * len(shape), pipeline_mode=pl.Buffered(1))

    def cost(flops, moved):
        return pl.CostEstimate(flops=int(flops), bytes_accessed=int(moved), transcendentals=0)

    def slot_spec(block):
        return pl.BlockSpec((2, SROWS, block), lambda i: (0, 0, i))

    near = pl.BlockSpec((rows, field_block), lambda i: (0, i))
    far = pl.BlockSpec((rows, field_block), lambda i: (0, cols // field_block - 1 - i))
    tile_shape = (2, LANES, k_width)
    shift_shape = (2, half_cols // LANES, k_width)
    arrays = 2 * pairs
    y_dims = (owners, bands, arrays * vloc, r2) if aligned else (bands, arrays, focal, r2)
    y_spec = pl.BlockSpec(y_dims, lambda i: (0,) * len(y_dims))
    y_shape = jax.ShapeDtypeStruct(y_dims, BF16)
    def field_dims(block):
        return (
            rows, cols, block, bands, half, band_total, total_rows, per_row, vloc, aligned
        )

    matmul = 2 * 4 * rows * half_cols * k_width * 2

    def table_scratch(block):
        return [pltpu.VMEM((block, k_width), BF16), pltpu.VMEM((block, k_width), BF16)]

    fields, tile, shift, across, index, half_way = pl.pallas_call(
        functools.partial(field_kernel, (field_dims(field_block), pairs)),
        grid=(half_cols // field_block,),
        in_specs=[
            smem, smem, smem, smem,
            resident(seg_coeffs.shape),
            resident(seg_box.shape),
            near, far, near, far,
        ],
        out_specs=[
            pl.BlockSpec((pairs, 2, 4 * rows, field_block), lambda i: (0, 0, 0, i)),
            pl.BlockSpec(tile_shape, lambda i: (0, 0, 0)),
            pl.BlockSpec(shift_shape, lambda i: (0, 0, 0)),
            slot_spec(field_block),
            slot_spec(field_block),
            y_spec,
        ],
        out_shape=[
            jax.ShapeDtypeStruct((pairs, 2, 4 * rows, half_cols), BF16),
            jax.ShapeDtypeStruct(tile_shape, F32),
            jax.ShapeDtypeStruct(shift_shape, F32),
            jax.ShapeDtypeStruct((2, SROWS, half_cols), F32),
            jax.ShapeDtypeStruct((2, SROWS, half_cols), jnp.int32),
            y_shape,
        ],
        scratch_shapes=[
            pltpu.VMEM((8, width), F32),
            pltpu.VMEM((3, rows, LANES), F32),
            pltpu.VMEM((rows, LANES), jnp.int32),
            pltpu.VMEM((2, SROWS, LANES), F32),
            pltpu.VMEM((2 * pairs, rows, LANES), F32),
            *table_scratch(field_block),
            pltpu.VMEM((4 * pairs * rows, field_block), BF16),
            pltpu.VMEM((4 * pairs * rows, field_block), BF16),
            pltpu.VMEM((2, 4 * pairs * rows, k_width), F32),
            pltpu.VMEM((2, SROWS, field_block), jnp.int32),
        ],
        compiler_params=params,
        cost_estimate=cost(4 * matmul, 20e6),
        name="field",
    )(pos, seg_box, probe_freq, probe_amp, seg_coeffs, seg_box,
      amplitude, amplitude, seg_map, seg_map)

    if not aligned:
        half_way = (
            half_way.reshape(bands, arrays, owners, vloc, r2)
            .transpose(2, 0, 1, 3, 4)
            .reshape(owners, bands, arrays * vloc, r2)
        )
    received = lax.all_to_all(half_way, "row", split_axis=0, concat_axis=0, tiled=True)

    row_table = pl.pallas_call(
        functools.partial(
            row_table_kernel, (rows, cols, bands, focal, band_total, total_rows, owners)
        ),
        in_specs=[smem],
        out_specs=whole,
        out_shape=jax.ShapeDtypeStruct((bands, owners * r2, 2 * focal), BF16),
        cost_estimate=cost(1e6, 2e6),
        name="row_table",
    )(pos)

    plus, minus = measured[:, :, 0::2], measured[:, :, 1::2]
    total, difference = plus + minus, plus - minus
    turned = jnp.stack([difference[:, :, :, 1], -difference[:, :, :, 0]], axis=3)
    targets = jnp.stack([total, turned], axis=3)
    targets = targets.transpose(0, 2, 3, 1, 4, 5).reshape(bands, arrays * vloc, 2 * focal)

    y_block = pl.BlockSpec((owners, None, arrays * vloc, r2), lambda b: (0, b, 0, 0))
    spread = pl.pallas_call(
        functools.partial(focal_kernel, (rows, owners, normf)),
        grid=(bands,),
        in_specs=[
            y_block,
            pl.BlockSpec((None, arrays * vloc, 2 * focal), lambda b: (b, 0, 0)),
            pl.BlockSpec((None, owners * r2, 2 * focal), lambda b: (b, 0, 0)),
        ],
        out_specs=y_block,
        out_shape=jax.ShapeDtypeStruct((owners, bands, arrays * vloc, r2), BF16),
        compiler_params=params,
        cost_estimate=cost(8 * bands * arrays * vloc * owners * r2 * focal, 4e6),
        name="focal",
    )(received, targets, row_table)
    hidden = lax.all_to_all(spread, "row", split_axis=0, concat_axis=0, tiled=True)
    if not aligned:
        hidden = (
            hidden.reshape(owners, bands, arrays, vloc, r2)
            .transpose(1, 2, 0, 3, 4)
            .reshape(bands, arrays, focal, r2)
        )

    scale = 2.0 * normf / (band_total * probes)
    steps = half_cols // block
    weight_dims = (
        rows, cols, block, part, bands, half, per_row, pairs, vloc,
        owners if aligned else 0, scale,
    )
    local = pl.pallas_call(
        functools.partial(weight_kernel, weight_dims),
        grid=(steps,),
        in_specs=[
            smem, smem, resident(hidden.shape),
            pl.BlockSpec((pairs, 2, 4 * rows, block), lambda i: (0, 0, 0, i)),
            resident(tile_shape), resident(shift_shape), slot_spec(block), slot_spec(block),
        ],
        out_specs=pl.BlockSpec((3, SROWS, LANES), lambda i: (0, 0, 0)),
        out_shape=jax.ShapeDtypeStruct((3, SROWS, LANES), F32),
        scratch_shapes=[
            pltpu.VMEM((2, 4 * pairs * rows, k_width), BF16),
            pltpu.VMEM((3 * SROWS, r2), BF16),
            pltpu.VMEM((2, part, k_width), BF16),
            pltpu.VMEM((2, part, k_width), BF16),
            pltpu.VMEM((2, 4 * pairs * rows, part), F32),
            pltpu.VMEM((2, 4 * pairs * rows, part), F32),
            pltpu.VMEM((r2, 2 * block), BF16),
            pltpu.VMEM((steps, 2, 3, SROWS, block), F32),
            pltpu.VMEM((steps, 2, SROWS, block), jnp.int32),
        ],
        compiler_params=params,
        cost_estimate=cost(4 * matmul, 20e6),
        name="weight",
    )(pos, seg_box, hidden, fields, tile, shift, across, index)

    devices = owners * band_axis
    axes = ("band", "row")
    shares = local.reshape(devices, -1)
    mine = jnp.sum(lax.all_to_all(shares, axes, split_axis=0, concat_axis=0, tiled=True), axis=0)
    copies = jnp.broadcast_to(mine[None], shares.shape)
    gathered = lax.all_to_all(copies, axes, split_axis=0, concat_axis=0, tiled=True)
    return gathered.reshape(3, SROWS, LANES)[:, :, :per_row].reshape(3, segments)


def solution(mesh):
    in_specs = (
        P("row", None),
        P("row", None),
        P(),
        P(),
        P(),
        P(),
        P("band", "row", None, None, None),
    )
    return jax.shard_map(body, mesh=mesh, in_specs=in_specs, out_specs=P(), check_vma=False)
```

```python
import functools
import math

import jax
import jax.numpy as jnp
from jax import lax
from jax.experimental import pallas as pl
from jax.experimental.pallas import tpu as pltpu
from jax.sharding import PartitionSpec as P

SROWS = 16
SAMPLING = 0.5
SPREAD = 0.2
TWO_PI = 2.0 * math.pi
LANES = 128
F32 = jnp.float32
BLOCKS = (512, 2048, 512)
BF16 = jnp.bfloat16

SIN_HALF = (0.9999999971, -0.1666666029, 0.008333109246, -0.0001981365728, 2.616271295e-06)
COS_HALF = (0.9999999682, -0.4999993032, 0.04166421727, -0.001385868782, 2.327410856e-05)
SIN_WAVE = (0.9999999964, -0.166666488, 0.008331936401, -0.000194912576)
COS_WAVE = (0.9999999679, -0.499998396, 0.04165412354, -0.001357443708)
SIN_TURN = (
    6.283185307, -41.34170222, 81.60524741, -76.70580003,
    42.05775188, -15.08655272, 3.781282403, -0.6207370354,
)
COS_TURN = (
    0.9999999999, -19.73920874, 64.93938905, -85.45665775,
    60.24212493, -26.40463062, 7.800022219, -1.452987552,
)


def series(coeffs, t):
    value = jnp.full_like(t, coeffs[-1])
    for c in reversed(coeffs[:-1]):
        value = value * t + c
    return value


def turn_cos_sin(turns):
    t = turns - jnp.floor(turns + 0.5)
    square = t * t
    return series(COS_TURN, square), t * series(SIN_TURN, square)


def iota(shape, axis):
    return lax.broadcasted_iota(jnp.int32, shape, axis)


def focal_scale(m_positive, band, band_total):
    ratio = 1.0 + SPREAD * ((band.astype(F32) + 0.5) / band_total - 0.5)
    return m_positive / ratio


def band_lanes(first_band, bands, half, band_total, rows):
    pieces = []
    for b in range(bands):
        q = (iota((rows, half), 1).astype(F32) + 0.5) * SAMPLING
        band = jnp.full((rows, half), 1, jnp.int32) * (first_band + b)
        pieces.append(focal_scale(q, band, band_total))
    return jnp.concatenate(pieces, axis=1)


def column_tables(first_band, bands, half, band_total, cols, tile_ref, shift_ref):
    q = band_lanes(first_band, bands, half, band_total, LANES)
    c, s = turn_cos_sin(q * (iota(q.shape, 0).astype(F32) / cols))
    tile_ref[0] = c
    tile_ref[1] = s
    tiles = cols // (2 * LANES)
    q = band_lanes(first_band, bands, half, band_total, tiles)
    x = (iota(q.shape, 0).astype(F32) * LANES + 0.5) / cols - 0.5
    c, s = turn_cos_sin(q * x)
    shift_ref[0] = c
    shift_ref[1] = s


def write_table(cos_ref, sin_ref, tile_ref, shift_ref, first_tile, tiles):
    for i in range(tiles):
        sc = shift_ref[0, pl.ds(first_tile + i, 1), :]
        ss = shift_ref[1, pl.ds(first_tile + i, 1), :]
        for k in range(0, LANES, 16):
            tc = tile_ref[0, k : k + 16]
            ts = tile_ref[1, k : k + 16]
            rows = slice(i * LANES + k, i * LANES + k + 16)
            cos_ref[rows] = (tc * sc - ts * ss).astype(BF16)
            sin_ref[rows] = (ts * sc + tc * ss).astype(BF16)


def load_segments(coeffs_ref, boxes_ref, seg_ref):
    seg_ref[...] = jnp.zeros_like(seg_ref)
    seg_ref[0:3, : coeffs_ref.shape[1]] = coeffs_ref[...]
    seg_ref[3:7, : boxes_ref.shape[1]] = boxes_ref[...].astype(F32)


def reverse(x):
    back = LANES - 1 - iota((8, LANES), 1)
    pieces = [gather_lanes(x[k : k + 8], back) for k in range(0, x.shape[0], 8)]
    return pieces[0] if len(pieces) == 1 else jnp.concatenate(pieces, axis=0)


def gather_lanes(x, index):
    return jnp.take_along_axis(x, index, axis=1, mode="promise_in_bounds")


def tile_row_pieces(seg_ref, per_row, width):
    for t in range(SROWS):
        yield t, pltpu.roll(seg_ref[...], (width - t * per_row) % width, axis=1)[:, :LANES]


def probe_setup(pos_ref, freq_ref, amp_ref, j, rows, cols, total_rows, waves):
    row = pos_ref[0] * rows + iota((rows, LANES), 0)
    y = (row.astype(F32) + 0.5) / cols - total_rows / (2.0 * cols)
    c, s = turn_cos_sin(freq_ref[j, 1].astype(F32) * y)
    waves[2 * j] = amp_ref[j] * c
    waves[2 * j + 1] = amp_ref[j] * s


def column_wave(freq_ref, pairs, step, block, cols):
    row = iota((8, block), 0)
    freq = jnp.zeros((8, block), F32)
    for j in range(pairs):
        freq = jnp.where(row // 2 == j, freq_ref[j, 0].astype(F32), freq)
    x = ((iota((8, block), 1) + step * block).astype(F32) + 0.5) / cols - 0.5
    c, s = turn_cos_sin(freq * x)
    return jnp.where(row % 2 == 0, s, c)


def emit_pair(j, column, waves, fields, here, lanes, g, rows, x_ref, even_ref, odd_ref):
    from_sin = column[2 * j : 2 * j + 1, lanes] * waves[2 * j, here]
    from_cos = column[2 * j + 1 : 2 * j + 2, lanes] * waves[2 * j + 1, here]
    parts = []
    for wave in (from_cos + from_sin, from_cos - from_sin):
        square = wave * wave
        parts.append(
            (
                series(COS_WAVE, square).astype(BF16),
                (wave * series(SIN_WAVE, square)).astype(BF16),
            )
        )
    for k in range(2):
        for o in range(2):
            at = (2 * k + o) * rows + g
            near = fields[0][o] * parts[0][k]
            far = fields[1][o] * parts[1][k]
            x_ref[j, 0, at : at + 16, lanes] = near
            x_ref[j, 1, at : at + 16, lanes] = far
            at = at + 4 * j * rows
            even_ref[at : at + 16, lanes] = near + far
            odd_ref[at : at + 16, lanes] = near - far


def emit_half_way(pairs, total_ref, y_ref, rows, bands, half, vloc, owners):
    r2 = 2 * rows
    m = iota((half, half), 0)
    n = iota((half, half), 1)
    straight = (m == n).astype(F32).astype(BF16)
    turned = (m + n == half - 1).astype(F32).astype(BF16)
    nt = (((1,), (1,)), ((), ()))
    for b in range(bands):
        for p in range(2 * pairs):
            at = slice(p * r2, (p + 1) * r2)
            cos_part = total_ref[0, at, b * half : (b + 1) * half]
            sin_part = total_ref[1, at, b * half : (b + 1) * half]
            swapped = jnp.concatenate([sin_part[rows:], -sin_part[:rows]], axis=0)
            low = lax.dot_general(
                turned, (cos_part - swapped).astype(BF16), nt, preferred_element_type=F32
            ).astype(BF16)
            high = lax.dot_general(
                straight, (cos_part + swapped).astype(BF16), nt, preferred_element_type=F32
            ).astype(BF16)
            if owners:
                each = half // vloc
                for d in range(each):
                    own = slice(d * vloc, (d + 1) * vloc)
                    y_ref[d, b, p * vloc : (p + 1) * vloc, :] = low[own]
                    y_ref[each + d, b, p * vloc : (p + 1) * vloc, :] = high[own]
            else:
                y_ref[b, p, :half, :] = low
                y_ref[b, p, half:, :] = high


def field_kernel(
    dims, pos_ref, box_ref, freq_ref, amp_ref, coeffs_ref, boxes_ref,
    amplitude_ref, amplitude_far_ref, map_ref, map_far_ref,
    x_ref, tile_ref, shift_ref, across_ref, index_ref, y_ref, *rest
):
    dims, pairs = dims
    (
        seg_ref, tables, bases, slot_tables, waves, cos_ref, sin_ref, even_ref, odd_ref, total_ref, slot_map,
    ) = rest
    rows, cols, block, bands, half, band_total, total_rows, per_row, vloc, owners = dims
    step = pl.program_id(0)
    row0 = pos_ref[0] * rows
    chunks = block // LANES
    maps = (map_ref, map_far_ref)
    amplitudes = (amplitude_ref, amplitude_far_ref)

    @pl.when(step == 0)
    def _():
        load_segments(coeffs_ref, boxes_ref, seg_ref)
        width = seg_ref.shape[1]
        groups = rows // 8
        values = [[jnp.zeros((8, LANES), F32)] * 3 for _ in range(groups)]
        base = [jnp.zeros((8, LANES), jnp.int32)] * groups
        for t, piece in tile_row_pieces(seg_ref, per_row, width):
            part = [jnp.broadcast_to(piece[k : k + 1], (8, LANES)) for k in range(7)]
            low, high = part[3][:, :1], part[4][:, :1]
            mid_row = 0.5 * (part[3] + part[4])
            inv_row = 1.0 / (part[4] - part[3] + 1.0)
            mid = 0.5 * (part[5] + part[6])
            inv = 2.0 / (part[6] - part[5] + 1.0)
            slope = 0.5 * part[1] * inv
            slot_tables[0, t : t + 1] = mid[:1]
            slot_tables[1, t : t + 1] = inv[:1]
            for g in range(groups):
                here = (row0 + g * 8 + iota((8, LANES), 0)).astype(F32)
                mine = (here >= low) & (here <= high)
                new = (0.5 * part[0] + part[2] * ((here - mid_row) * inv_row), slope, mid)
                values[g] = [jnp.where(mine, n, v) for n, v in zip(new, values[g])]
                base[g] = jnp.where(mine, t * per_row, base[g])
        for g in range(groups):
            for k in range(3):
                tables[k, g * 8 : (g + 1) * 8] = values[g][k]
            bases[g * 8 : (g + 1) * 8] = base[g]
        for j in range(pairs):
            probe_setup(pos_ref, freq_ref, amp_ref, j, rows, cols, total_rows, waves)
        column_tables(pos_ref[1] * bands, bands, half, band_total, cols, tile_ref, shift_ref)
        total_ref[...] = jnp.zeros_like(total_ref)

    for t in range(SROWS):
        first = jnp.clip(box_ref[0, t * per_row] - row0, 0, rows - 1)
        for side in range(2):
            slot_map[side, t : t + 1, :] = maps[side][pl.ds(first, 1), :] - t * per_row

    column = column_wave(freq_ref, pairs, step, block, cols)
    write_table(cos_ref, sin_ref, tile_ref, shift_ref, step * chunks, chunks)

    for i in range(chunks):
        lanes = slice(i * LANES, (i + 1) * LANES)
        far_lanes = slice((chunks - 1 - i) * LANES, (chunks - i) * LANES)
        near_column = (iota((8, LANES), 1) + (step * block + i * LANES)).astype(F32)
        columns = (near_column, (cols - 1.0) - near_column)
        for side in range(2):
            for t in range(0, SROWS, 8):
                index = slot_map[side, t : t + 8, far_lanes if side else lanes] & (LANES - 1)
                if side:
                    index = reverse(index)
                mid = gather_lanes(slot_tables[0, t : t + 8], index)
                inv = gather_lanes(slot_tables[1, t : t + 8], index)
                across_ref[side, t : t + 8, lanes] = (columns[side] - mid) * inv
                index_ref[side, t : t + 8, lanes] = index
        for g in range(0, rows, 16):
            here = slice(g, g + 16)
            fields = []
            for side in range(2):
                source = far_lanes if side else lanes
                size = amplitudes[side][here, source].astype(F32)
                halves = []
                for h in (0, 8):
                    own = slice(g + h, g + h + 8)
                    index = maps[side][own, source] - bases[own]
                    if side:
                        index = reverse(index)
                    half_phase = gather_lanes(tables[0, own], index) + gather_lanes(
                        tables[1, own], index
                    ) * (columns[side] - gather_lanes(tables[2, own], index))
                    square = half_phase * half_phase
                    s = half_phase * series(SIN_HALF, square)
                    c = series(COS_HALF, square)
                    twice = s + s
                    own_size = size[h : h + 8]
                    if side:
                        own_size = reverse(own_size)
                    halves.append((own_size * (1.0 - twice * s), own_size * (twice * c)))
                both = [
                    jnp.concatenate([halves[0][o], halves[1][o]], axis=0).astype(BF16)
                    for o in range(2)
                ]
                fields.append(both)
            for j in range(pairs):
                emit_pair(
                    j, column, waves, fields, here, lanes, g, rows, x_ref, even_ref, odd_ref
                )

    total_ref[0] += jnp.dot(even_ref[...], cos_ref[...], preferred_element_type=F32)
    total_ref[1] += jnp.dot(odd_ref[...], sin_ref[...], preferred_element_type=F32)

    @pl.when(step == pl.num_programs(0) - 1)
    def _():
        emit_half_way(pairs, total_ref, y_ref, rows, bands, half, vloc, owners)


def row_table_kernel(dims, pos_ref, table_ref):
    rows, cols, bands, focal, band_total, total_rows, sources = dims
    r2 = 2 * rows
    for b in range(bands):
        band = jnp.full((rows, focal), 1, jnp.int32) * (pos_ref[1] * bands + b)
        q = (iota((rows, focal), 1).astype(F32) + (0.5 - focal / 2)) * SAMPLING
        q = focal_scale(q, band, band_total)
        tile_c, tile_s = turn_cos_sin(q * (iota(q.shape, 0).astype(F32) / cols))
        first = iota((sources, focal), 0).astype(F32) * rows + 0.5
        y = first / cols - total_rows / (2.0 * cols)
        shift_c, shift_s = turn_cos_sin(jnp.broadcast_to(q[:1], y.shape) * y)
        for d in range(sources):
            sc, ss = shift_c[d : d + 1], shift_s[d : d + 1]
            c = (tile_c * sc - tile_s * ss).astype(BF16)
            s_value = tile_s * sc + tile_c * ss
            s = s_value.astype(BF16)
            table_ref[b, d * r2 : d * r2 + rows, :focal] = c
            table_ref[b, d * r2 : d * r2 + rows, focal:] = (-s_value).astype(BF16)
            table_ref[b, d * r2 + rows : (d + 1) * r2, :focal] = s
            table_ref[b, d * r2 + rows : (d + 1) * r2, focal:] = c


def focal_kernel(dims, y_ref, target_ref, table_ref, h_ref):
    rows, sources, scale = dims
    r2 = 2 * rows
    lhs = jnp.concatenate([y_ref[d] for d in range(sources)], axis=1)
    f = jnp.dot(lhs, table_ref[...], preferred_element_type=F32)
    residual = (f * (2.0 * scale) - target_ref[...]).astype(BF16)
    spread = lax.dot_general(
        residual, table_ref[...], (((1,), (1,)), ((), ())), preferred_element_type=F32
    )
    for d in range(sources):
        h_ref[d] = spread[:, d * r2 : (d + 1) * r2].astype(BF16)


def fold_hidden(pairs, h_ref, left_ref, rows, bands, half, vloc, sources):
    r2 = 2 * rows
    nt = (((1,), (1,)), ((), ()))
    m = iota((half, 2 * half), 0)
    v = iota((half, 2 * half), 1)
    upper = (v == half + m).astype(F32)
    lower = (v == half - 1 - m).astype(F32)
    even, odd = (upper + lower).astype(BF16), (upper - lower).astype(BF16)
    same = (iota((r2, r2), 0) == iota((r2, r2), 1)).astype(F32).astype(BF16)
    for b in range(bands):
        for p in range(2 * pairs):
            if sources:
                block_h = jnp.concatenate(
                    [h_ref[d, b, p * vloc : (p + 1) * vloc, :] for d in range(sources)], axis=0
                )
            else:
                block_h = h_ref[b, p]

            def fold(mirror):
                folded = jnp.dot(mirror, block_h, preferred_element_type=F32).astype(BF16)
                return lax.dot_general(same, folded, nt, preferred_element_type=F32)

            plus, minus = fold(even), fold(odd)
            at = slice(p * r2, (p + 1) * r2)
            left_ref[0, at, b * half : (b + 1) * half] = plus.astype(BF16)
            left_ref[1, at, b * half : (b + 1) * half] = jnp.concatenate(
                [-minus[rows:], minus[:rows]], axis=0
            ).astype(BF16)


def weight_kernel(
    dims, pos_ref, box_ref, h_ref, x_ref, tile_ref, shift_ref, across_ref, index_ref,
    out_ref, give_ref, left_ref, pick_ref, cos_ref, sin_ref, p_ref, q_ref, weight_ref, sums_ref,
    term_ref, flat_ref,
):
    rows, cols, block, part, bands, half, per_row, pairs, vloc, sources, scale = dims
    step = pl.program_id(0)
    row0 = pos_ref[0] * rows
    r2 = 2 * rows
    nt = (((1,), (1,)), ((), ()))

    @pl.when(step == 0)
    def _():
        fold_hidden(pairs, h_ref, left_ref, rows, bands, half, vloc, sources)
        slot = iota((SROWS, r2), 0)
        lane = iota((SROWS, r2), 1)
        here = (row0 + lane % rows).astype(F32)
        low = jnp.zeros((SROWS, r2), F32)
        high = jnp.zeros((SROWS, r2), F32)
        for t in range(SROWS):
            low = jnp.where(slot == t, box_ref[0, t * per_row].astype(F32), low)
            high = jnp.where(slot == t, box_ref[1, t * per_row].astype(F32), high)
        mine = ((here >= low) & (here <= high)).astype(F32)
        down = mine * ((here - 0.5 * (low + high)) / (0.5 * (high - low + 1.0)))
        down_high = down.astype(BF16)
        pick_ref[:SROWS] = mine.astype(BF16)
        pick_ref[SROWS : 2 * SROWS] = down_high
        pick_ref[2 * SROWS :] = (down - down_high.astype(F32)).astype(BF16)

    tiles = part // LANES
    for k in range(block // part):
        slot = k % 2
        write_table(
            cos_ref.at[slot], sin_ref.at[slot], tile_ref, shift_ref,
            step * (block // LANES) + k * tiles, tiles,
        )
        p_ref[slot] = lax.dot_general(left_ref[0], cos_ref[slot], nt, preferred_element_type=F32)
        q_ref[slot] = lax.dot_general(left_ref[1], sin_ref[slot], nt, preferred_element_type=F32)
        for i in range(tiles):
            lanes = slice(i * LANES, (i + 1) * LANES)
            at = slice(k * part + i * LANES, k * part + (i + 1) * LANES)
            for g in range(0, rows, 16):
                near, far = None, None
                for p in range(2 * pairs):
                    j, first = divmod(p, 2)
                    re = slice(p * r2 + g, p * r2 + g + 16)
                    im = slice(p * r2 + rows + g, p * r2 + rows + g + 16)
                    xre = slice(first * r2 + g, first * r2 + g + 16)
                    xim = slice(first * r2 + rows + g, first * r2 + rows + g + 16)
                    p_re, p_im = p_ref[slot, re, lanes], p_ref[slot, im, lanes]
                    q_re, q_im = q_ref[slot, re, lanes], q_ref[slot, im, lanes]
                    x = [
                        [x_ref[j, side, rows_, at].astype(F32) for rows_ in (xre, xim)]
                        for side in range(2)
                    ]
                    near_term = x[0][0] * (p_im + q_im) - x[0][1] * (p_re + q_re)
                    far_term = x[1][0] * (p_im - q_im) - x[1][1] * (p_re - q_re)
                    near = near_term if near is None else near + near_term
                    far = far_term if far is None else far + far_term
                for side, value in enumerate((near, far)):
                    high = value.astype(BF16)
                    to = slice(side * block + at.start, side * block + at.stop)
                    weight_ref[g : g + 16, to] = high
                    weight_ref[rows + g : rows + g + 16, to] = (
                        value - high.astype(F32)
                    ).astype(BF16)
    sums = jnp.dot(pick_ref[...], weight_ref[...], preferred_element_type=F32)
    for side in range(2):
        mine = sums[:, side * block : (side + 1) * block]
        sums_ref[step, side, 0] = mine[:SROWS]
        sums_ref[step, side, 1] = mine[:SROWS] * across_ref[side]
        sums_ref[step, side, 2] = mine[SROWS : 2 * SROWS] + mine[2 * SROWS :]
        term_ref[step, side] = index_ref[side]

    @pl.when(step == pl.num_programs(0) - 1)
    def _():
        tops = [box_ref[0, t * per_row] for t in range(SROWS)]
        bottoms = [box_ref[1, t * per_row] for t in range(SROWS)]
        first = sum((bottom < row0).astype(jnp.int32) for bottom in bottoms)
        last = sum((top < row0 + rows).astype(jnp.int32) for top in tops)

        def tile_row(t, carry):
            def add(i, total):
                for side in range(2):
                    index = term_ref[i, side, pl.ds(t, 1), :].astype(F32).astype(BF16)
                    inside = jnp.where(tile_index == index, one, zero)
                    terms = [sums_ref[i, side, q, pl.ds(t, 1), :] for q in range(3)]
                    highs = [x.astype(BF16).astype(F32) for x in terms]
                    lows = [x - h for x, h in zip(terms, highs)]
                    stacked = jnp.concatenate(highs + lows + lows[:2], axis=0).astype(BF16)
                    total = total + lax.dot_general(
                        stacked, inside, nt, preferred_element_type=F32
                    )
                return total

            total = lax.fori_loop(0, pl.num_programs(0), add, jnp.zeros((8, LANES), F32))
            total = jnp.where(iota((8, LANES), 1) < per_row, total, 0.0)
            padding = jnp.zeros((8, flat_ref.shape[1] - LANES), F32)
            wide = jnp.concatenate([total, padding], axis=1)
            flat_ref[...] += pltpu.roll(wide, t * per_row, axis=1)
            return carry

        tile_index = iota((LANES, block), 0).astype(F32).astype(BF16)
        one = jnp.ones((LANES, block), BF16)
        zero = jnp.zeros((LANES, block), BF16)
        flat_ref[...] = jnp.zeros_like(flat_ref)
        lax.fori_loop(first, last, tile_row, 0)
        odd = pos_ref[0] % 2 == 1
        pieces = flat_ref.shape[1] // (2 * LANES)
        for q in range(3):
            value = (flat_ref[q : q + 1] + flat_ref[q + 3 : q + 4]) * scale
            for i in range(pieces):
                low = value[:, i * LANES : (i + 1) * LANES]
                high = value[:, (pieces + i) * LANES : (pieces + i + 1) * LANES]
                at = q * pieces + i
                out_ref[at : at + 1] = jnp.where(odd, high, low)
                give_ref[at : at + 1] = jnp.where(odd, low, high)


def body(amplitude, seg_map, seg_box, seg_coeffs, probe_freq, probe_amp, measured):
    rows, cols = amplitude.shape
    owners = lax.axis_size("row")
    band_axis = lax.axis_size("band")
    total_rows = rows * owners
    bands, vloc, probes, _, focal = measured.shape
    pairs = probes // 2
    half = focal // 2
    band_total = bands * band_axis
    segments = seg_coeffs.shape[1]
    per_row = segments // SROWS
    r2 = 2 * rows
    normf = 1.0 / math.sqrt(total_rows * cols)
    aligned = vloc % 16 == 0
    half_cols = cols // 2
    field_block, block, part = BLOCKS
    k_width = bands * half

    pos = jnp.stack([lax.axis_index("row"), lax.axis_index("band")]).astype(jnp.int32)
    width = -(-(segments + LANES) // LANES) * LANES
    smem = pl.BlockSpec(memory_space=pltpu.SMEM)
    whole = pl.BlockSpec(memory_space=pltpu.VMEM)
    params = pltpu.CompilerParams(dimension_semantics=("arbitrary",))

    def resident(shape):
        return pl.BlockSpec(shape, lambda i: (0,) * len(shape), pipeline_mode=pl.Buffered(1))

    def cost(flops, moved):
        return pl.CostEstimate(flops=int(flops), bytes_accessed=int(moved), transcendentals=0)

    def slot_spec(block):
        return pl.BlockSpec((2, SROWS, block), lambda i: (0, 0, i))

    near = pl.BlockSpec((rows, field_block), lambda i: (0, i))
    far = pl.BlockSpec((rows, field_block), lambda i: (0, cols // field_block - 1 - i))
    tile_shape = (2, LANES, k_width)
    shift_shape = (2, half_cols // LANES, k_width)
    arrays = 2 * pairs
    y_dims = (owners, bands, arrays * vloc, r2) if aligned else (bands, arrays, focal, r2)
    y_spec = pl.BlockSpec(y_dims, lambda i: (0,) * len(y_dims))
    y_shape = jax.ShapeDtypeStruct(y_dims, BF16)
    def field_dims(block):
        return (
            rows, cols, block, bands, half, band_total, total_rows, per_row, vloc, aligned
        )

    matmul = 2 * 4 * rows * half_cols * k_width * 2

    def table_scratch(block):
        return [pltpu.VMEM((block, k_width), BF16), pltpu.VMEM((block, k_width), BF16)]

    fields, tile, shift, across, index, half_way = pl.pallas_call(
        functools.partial(field_kernel, (field_dims(field_block), pairs)),
        grid=(half_cols // field_block,),
        in_specs=[
            smem, smem, smem, smem,
            resident(seg_coeffs.shape),
            resident(seg_box.shape),
            near, far, near, far,
        ],
        out_specs=[
            pl.BlockSpec((pairs, 2, 4 * rows, field_block), lambda i: (0, 0, 0, i)),
            pl.BlockSpec(tile_shape, lambda i: (0, 0, 0)),
            pl.BlockSpec(shift_shape, lambda i: (0, 0, 0)),
            slot_spec(field_block),
            slot_spec(field_block),
            y_spec,
        ],
        out_shape=[
            jax.ShapeDtypeStruct((pairs, 2, 4 * rows, half_cols), BF16),
            jax.ShapeDtypeStruct(tile_shape, F32),
            jax.ShapeDtypeStruct(shift_shape, F32),
            jax.ShapeDtypeStruct((2, SROWS, half_cols), F32),
            jax.ShapeDtypeStruct((2, SROWS, half_cols), jnp.int32),
            y_shape,
        ],
        scratch_shapes=[
            pltpu.VMEM((8, width), F32),
            pltpu.VMEM((3, rows, LANES), F32),
            pltpu.VMEM((rows, LANES), jnp.int32),
            pltpu.VMEM((2, SROWS, LANES), F32),
            pltpu.VMEM((2 * pairs, rows, LANES), F32),
            *table_scratch(field_block),
            pltpu.VMEM((4 * pairs * rows, field_block), BF16),
            pltpu.VMEM((4 * pairs * rows, field_block), BF16),
            pltpu.VMEM((2, 4 * pairs * rows, k_width), F32),
            pltpu.VMEM((2, SROWS, field_block), jnp.int32),
        ],
        compiler_params=params,
        cost_estimate=cost(4 * matmul, 20e6),
        name="field",
    )(pos, seg_box, probe_freq, probe_amp, seg_coeffs, seg_box,
      amplitude, amplitude, seg_map, seg_map)

    if not aligned:
        half_way = (
            half_way.reshape(bands, arrays, owners, vloc, r2)
            .transpose(2, 0, 1, 3, 4)
            .reshape(owners, bands, arrays * vloc, r2)
        )
    received = lax.all_to_all(half_way, "row", split_axis=0, concat_axis=0, tiled=True)

    row_table = pl.pallas_call(
        functools.partial(
            row_table_kernel, (rows, cols, bands, focal, band_total, total_rows, owners)
        ),
        in_specs=[smem],
        out_specs=whole,
        out_shape=jax.ShapeDtypeStruct((bands, owners * r2, 2 * focal), BF16),
        cost_estimate=cost(1e6, 2e6),
        name="row_table",
    )(pos)

    plus, minus = measured[:, :, 0::2], measured[:, :, 1::2]
    total, difference = plus + minus, plus - minus
    turned = jnp.stack([difference[:, :, :, 1], -difference[:, :, :, 0]], axis=3)
    targets = jnp.stack([total, turned], axis=3)
    targets = targets.transpose(0, 2, 3, 1, 4, 5).reshape(bands, arrays * vloc, 2 * focal)

    y_block = pl.BlockSpec((owners, None, arrays * vloc, r2), lambda b: (0, b, 0, 0))
    spread = pl.pallas_call(
        functools.partial(focal_kernel, (rows, owners, normf)),
        grid=(bands,),
        in_specs=[
            y_block,
            pl.BlockSpec((None, arrays * vloc, 2 * focal), lambda b: (b, 0, 0)),
            pl.BlockSpec((None, owners * r2, 2 * focal), lambda b: (b, 0, 0)),
        ],
        out_specs=y_block,
        out_shape=jax.ShapeDtypeStruct((owners, bands, arrays * vloc, r2), BF16),
        compiler_params=params,
        cost_estimate=cost(8 * bands * arrays * vloc * owners * r2 * focal, 4e6),
        name="focal",
    )(received, targets, row_table)
    hidden = lax.all_to_all(spread, "row", split_axis=0, concat_axis=0, tiled=True)
    if not aligned:
        hidden = (
            hidden.reshape(owners, bands, arrays, vloc, r2)
            .transpose(1, 2, 0, 3, 4)
            .reshape(bands, arrays, focal, r2)
        )

    scale = 2.0 * normf / (band_total * probes)
    steps = half_cols // block
    weight_dims = (
        rows, cols, block, part, bands, half, per_row, pairs, vloc,
        owners if aligned else 0, scale,
    )
    pieces = -(-segments // (2 * LANES))
    share = jax.ShapeDtypeStruct((3 * pieces, LANES), F32)
    kept, given = pl.pallas_call(
        functools.partial(weight_kernel, weight_dims),
        grid=(steps,),
        in_specs=[
            smem, smem, resident(hidden.shape),
            pl.BlockSpec((pairs, 2, 4 * rows, block), lambda i: (0, 0, 0, i)),
            resident(tile_shape), resident(shift_shape), slot_spec(block), slot_spec(block),
        ],
        out_specs=[pl.BlockSpec(share.shape, lambda i: (0, 0))] * 2,
        out_shape=[share, share],
        scratch_shapes=[
            pltpu.VMEM((2, 4 * pairs * rows, k_width), BF16),
            pltpu.VMEM((3 * SROWS, r2), BF16),
            pltpu.VMEM((2, part, k_width), BF16),
            pltpu.VMEM((2, part, k_width), BF16),
            pltpu.VMEM((2, 4 * pairs * rows, part), F32),
            pltpu.VMEM((2, 4 * pairs * rows, part), F32),
            pltpu.VMEM((r2, 2 * block), BF16),
            pltpu.VMEM((steps, 2, 3, SROWS, block), F32),
            pltpu.VMEM((steps, 2, SROWS, block), jnp.int32),
            pltpu.VMEM((8, 2 * pieces * LANES), F32),
        ],
        compiler_params=params,
        cost_estimate=cost(4 * matmul, 20e6),
        name="weight",
    )(pos, seg_box, hidden, fields, tile, shift, across, index)

    axes = ("band", "row")
    devices = owners * band_axis
    groups = [[d for d in range(devices) if d % 2 == core] for core in range(2)]

    def swap_cores(array):
        return lax.ppermute(array, "row", [(i, i ^ 1) for i in range(owners)])

    mine = kept + swap_cores(given)
    copies = jnp.broadcast_to(mine[None], (devices // 2,) + mine.shape)
    everyones = lax.all_to_all(
        copies, axes, split_axis=0, concat_axis=0, tiled=True, axis_index_groups=groups
    )
    mine = jnp.sum(everyones, axis=0)
    other = swap_cores(mine)
    odd = lax.axis_index("row") % 2 == 1
    halves = [jnp.where(odd, other, mine), jnp.where(odd, mine, other)]
    halves = [x.reshape(3, pieces * LANES) for x in halves]
    return jnp.concatenate(halves, axis=1)[:, :segments]


def solution(mesh):
    in_specs = (
        P("row", None),
        P("row", None),
        P(),
        P(),
        P(),
        P(),
        P("band", "row", None, None, None),
    )
    return jax.shard_map(body, mesh=mesh, in_specs=in_specs, out_specs=P(), check_vma=False)
```

```python
import functools
import math

import jax
import jax.numpy as jnp
from jax import lax
from jax.experimental import pallas as pl
from jax.experimental.pallas import tpu as pltpu
from jax.sharding import PartitionSpec as P

SROWS = 16
SAMPLING = 0.5
SPREAD = 0.2
TWO_PI = 2.0 * math.pi
LANES = 128
F32 = jnp.float32
BLOCKS = (512, 2048, 256)
BF16 = jnp.bfloat16

SIN_HALF = (0.9999999971, -0.1666666029, 0.008333109246, -0.0001981365728, 2.616271295e-06)
COS_HALF = (0.9999999682, -0.4999993032, 0.04166421727, -0.001385868782, 2.327410856e-05)
SIN_WAVE = (0.9999999964, -0.166666488, 0.008331936401, -0.000194912576)
COS_WAVE = (0.9999999679, -0.499998396, 0.04165412354, -0.001357443708)
SIN_TURN = (
    6.283185307, -41.34170222, 81.60524741, -76.70580003,
    42.05775188, -15.08655272, 3.781282403, -0.6207370354,
)
COS_TURN = (
    0.9999999999, -19.73920874, 64.93938905, -85.45665775,
    60.24212493, -26.40463062, 7.800022219, -1.452987552,
)


def series(coeffs, t):
    value = jnp.full_like(t, coeffs[-1])
    for c in reversed(coeffs[:-1]):
        value = value * t + c
    return value


def turn_cos_sin(turns):
    t = turns - jnp.floor(turns + 0.5)
    square = t * t
    return series(COS_TURN, square), t * series(SIN_TURN, square)


def iota(shape, axis):
    return lax.broadcasted_iota(jnp.int32, shape, axis)


def focal_scale(m_positive, band, band_total):
    ratio = 1.0 + SPREAD * ((band.astype(F32) + 0.5) / band_total - 0.5)
    return m_positive / ratio


def band_lanes(first_band, bands, half, band_total, rows):
    pieces = []
    for b in range(bands):
        q = (iota((rows, half), 1).astype(F32) + 0.5) * SAMPLING
        band = jnp.full((rows, half), 1, jnp.int32) * (first_band + b)
        pieces.append(focal_scale(q, band, band_total))
    return jnp.concatenate(pieces, axis=1)


def column_tables(first_band, bands, half, band_total, cols, tile_ref, shift_ref):
    q = band_lanes(first_band, bands, half, band_total, LANES)
    c, s = turn_cos_sin(q * (iota(q.shape, 0).astype(F32) / cols))
    tile_ref[0] = c
    tile_ref[1] = s
    tiles = cols // (2 * LANES)
    q = band_lanes(first_band, bands, half, band_total, tiles)
    x = (iota(q.shape, 0).astype(F32) * LANES + 0.5) / cols - 0.5
    c, s = turn_cos_sin(q * x)
    shift_ref[0] = c
    shift_ref[1] = s


def write_table(cos_ref, sin_ref, tile_ref, shift_ref, first_tile, tiles):
    for i in range(tiles):
        sc = shift_ref[0, pl.ds(first_tile + i, 1), :]
        ss = shift_ref[1, pl.ds(first_tile + i, 1), :]
        for k in range(0, LANES, 16):
            tc = tile_ref[0, k : k + 16]
            ts = tile_ref[1, k : k + 16]
            rows = slice(i * LANES + k, i * LANES + k + 16)
            cos_ref[rows] = (tc * sc - ts * ss).astype(BF16)
            sin_ref[rows] = (ts * sc + tc * ss).astype(BF16)


def load_segments(coeffs_ref, boxes_ref, seg_ref):
    seg_ref[...] = jnp.zeros_like(seg_ref)
    seg_ref[0:3, : coeffs_ref.shape[1]] = coeffs_ref[...]
    seg_ref[3:7, : boxes_ref.shape[1]] = boxes_ref[...].astype(F32)


def reverse(x):
    back = LANES - 1 - iota((8, LANES), 1)
    pieces = [gather_lanes(x[k : k + 8], back) for k in range(0, x.shape[0], 8)]
    return pieces[0] if len(pieces) == 1 else jnp.concatenate(pieces, axis=0)


def gather_lanes(x, index):
    return jnp.take_along_axis(x, index, axis=1, mode="promise_in_bounds")


def tile_row_pieces(seg_ref, per_row, width):
    for t in range(SROWS):
        yield t, pltpu.roll(seg_ref[...], (width - t * per_row) % width, axis=1)[:, :LANES]


def probe_setup(pos_ref, freq_ref, amp_ref, j, rows, cols, total_rows, waves):
    row = pos_ref[0] * rows + iota((rows, LANES), 0)
    y = (row.astype(F32) + 0.5) / cols - total_rows / (2.0 * cols)
    c, s = turn_cos_sin(freq_ref[j, 1].astype(F32) * y)
    waves[2 * j] = amp_ref[j] * c
    waves[2 * j + 1] = amp_ref[j] * s


def column_wave(freq_ref, pairs, step, block, cols):
    row = iota((8, block), 0)
    freq = jnp.zeros((8, block), F32)
    for j in range(pairs):
        freq = jnp.where(row // 2 == j, freq_ref[j, 0].astype(F32), freq)
    x = ((iota((8, block), 1) + step * block).astype(F32) + 0.5) / cols - 0.5
    c, s = turn_cos_sin(freq * x)
    return jnp.where(row % 2 == 0, s, c)


def emit_pair(j, column, waves, fields, here, lanes, g, rows, x_ref, even_ref, odd_ref):
    from_sin = column[2 * j : 2 * j + 1, lanes] * waves[2 * j, here]
    from_cos = column[2 * j + 1 : 2 * j + 2, lanes] * waves[2 * j + 1, here]
    parts = []
    for wave in (from_cos + from_sin, from_cos - from_sin):
        square = wave * wave
        parts.append(
            (
                series(COS_WAVE, square).astype(BF16),
                (wave * series(SIN_WAVE, square)).astype(BF16),
            )
        )
    for k in range(2):
        for o in range(2):
            at = (2 * k + o) * rows + g
            near = fields[0][o] * parts[0][k]
            far = fields[1][o] * parts[1][k]
            x_ref[j, 0, at : at + 16, lanes] = near
            x_ref[j, 1, at : at + 16, lanes] = far
            at = at + 4 * j * rows
            even_ref[at : at + 16, lanes] = near + far
            odd_ref[at : at + 16, lanes] = near - far


def emit_half_way(pairs, total_ref, y_ref, rows, bands, half, vloc, owners):
    r2 = 2 * rows
    m = iota((half, half), 0)
    n = iota((half, half), 1)
    straight = (m == n).astype(F32).astype(BF16)
    turned = (m + n == half - 1).astype(F32).astype(BF16)
    nt = (((1,), (1,)), ((), ()))
    for b in range(bands):
        for p in range(2 * pairs):
            at = slice(p * r2, (p + 1) * r2)
            cos_part = total_ref[0, at, b * half : (b + 1) * half]
            sin_part = total_ref[1, at, b * half : (b + 1) * half]
            swapped = jnp.concatenate([sin_part[rows:], -sin_part[:rows]], axis=0)
            low = lax.dot_general(
                turned, (cos_part - swapped).astype(BF16), nt, preferred_element_type=F32
            ).astype(BF16)
            high = lax.dot_general(
                straight, (cos_part + swapped).astype(BF16), nt, preferred_element_type=F32
            ).astype(BF16)
            if owners:
                each = half // vloc
                for d in range(each):
                    own = slice(d * vloc, (d + 1) * vloc)
                    y_ref[d, b, p * vloc : (p + 1) * vloc, :] = low[own]
                    y_ref[each + d, b, p * vloc : (p + 1) * vloc, :] = high[own]
            else:
                y_ref[b, p, :half, :] = low
                y_ref[b, p, half:, :] = high


def field_kernel(
    dims, pos_ref, box_ref, freq_ref, amp_ref, coeffs_ref, boxes_ref,
    amplitude_ref, amplitude_far_ref, map_ref, map_far_ref,
    x_ref, tile_ref, shift_ref, across_ref, index_ref, y_ref, *rest
):
    dims, pairs = dims
    (
        seg_ref, tables, bases, slot_tables, waves, cos_ref, sin_ref, even_ref, odd_ref, total_ref, slot_map,
    ) = rest
    rows, cols, block, bands, half, band_total, total_rows, per_row, vloc, owners = dims
    step = pl.program_id(0)
    row0 = pos_ref[0] * rows
    chunks = block // LANES
    maps = (map_ref, map_far_ref)
    amplitudes = (amplitude_ref, amplitude_far_ref)

    @pl.when(step == 0)
    def _():
        load_segments(coeffs_ref, boxes_ref, seg_ref)
        width = seg_ref.shape[1]
        groups = rows // 8
        values = [[jnp.zeros((8, LANES), F32)] * 3 for _ in range(groups)]
        base = [jnp.zeros((8, LANES), jnp.int32)] * groups
        for t, piece in tile_row_pieces(seg_ref, per_row, width):
            part = [jnp.broadcast_to(piece[k : k + 1], (8, LANES)) for k in range(7)]
            low, high = part[3][:, :1], part[4][:, :1]
            mid_row = 0.5 * (part[3] + part[4])
            inv_row = 1.0 / (part[4] - part[3] + 1.0)
            mid = 0.5 * (part[5] + part[6])
            inv = 2.0 / (part[6] - part[5] + 1.0)
            slope = 0.5 * part[1] * inv
            slot_tables[0, t : t + 1] = mid[:1]
            slot_tables[1, t : t + 1] = inv[:1]
            for g in range(groups):
                here = (row0 + g * 8 + iota((8, LANES), 0)).astype(F32)
                mine = (here >= low) & (here <= high)
                new = (0.5 * part[0] + part[2] * ((here - mid_row) * inv_row), slope, mid)
                values[g] = [jnp.where(mine, n, v) for n, v in zip(new, values[g])]
                base[g] = jnp.where(mine, t * per_row, base[g])
        for g in range(groups):
            for k in range(3):
                tables[k, g * 8 : (g + 1) * 8] = values[g][k]
            bases[g * 8 : (g + 1) * 8] = base[g]
        for j in range(pairs):
            probe_setup(pos_ref, freq_ref, amp_ref, j, rows, cols, total_rows, waves)
        column_tables(pos_ref[1] * bands, bands, half, band_total, cols, tile_ref, shift_ref)
        total_ref[...] = jnp.zeros_like(total_ref)

    for t in range(SROWS):
        first = jnp.clip(box_ref[0, t * per_row] - row0, 0, rows - 1)
        for side in range(2):
            slot_map[side, t : t + 1, :] = maps[side][pl.ds(first, 1), :] - t * per_row

    column = column_wave(freq_ref, pairs, step, block, cols)
    write_table(cos_ref, sin_ref, tile_ref, shift_ref, step * chunks, chunks)

    for i in range(chunks):
        lanes = slice(i * LANES, (i + 1) * LANES)
        far_lanes = slice((chunks - 1 - i) * LANES, (chunks - i) * LANES)
        near_column = (iota((8, LANES), 1) + (step * block + i * LANES)).astype(F32)
        columns = (near_column, (cols - 1.0) - near_column)
        for side in range(2):
            for t in range(0, SROWS, 8):
                index = slot_map[side, t : t + 8, far_lanes if side else lanes] & (LANES - 1)
                if side:
                    index = reverse(index)
                mid = gather_lanes(slot_tables[0, t : t + 8], index)
                inv = gather_lanes(slot_tables[1, t : t + 8], index)
                across_ref[side, t : t + 8, lanes] = (columns[side] - mid) * inv
                index_ref[side, t : t + 8, lanes] = index
        for g in range(0, rows, 16):
            here = slice(g, g + 16)
            fields = []
            for side in range(2):
                source = far_lanes if side else lanes
                size = amplitudes[side][here, source].astype(F32)
                halves = []
                for h in (0, 8):
                    own = slice(g + h, g + h + 8)
                    index = maps[side][own, source] - bases[own]
                    if side:
                        index = reverse(index)
                    half_phase = gather_lanes(tables[0, own], index) + gather_lanes(
                        tables[1, own], index
                    ) * (columns[side] - gather_lanes(tables[2, own], index))
                    square = half_phase * half_phase
                    s = half_phase * series(SIN_HALF, square)
                    c = series(COS_HALF, square)
                    twice = s + s
                    own_size = size[h : h + 8]
                    if side:
                        own_size = reverse(own_size)
                    halves.append((own_size * (1.0 - twice * s), own_size * (twice * c)))
                both = [
                    jnp.concatenate([halves[0][o], halves[1][o]], axis=0).astype(BF16)
                    for o in range(2)
                ]
                fields.append(both)
            for j in range(pairs):
                emit_pair(
                    j, column, waves, fields, here, lanes, g, rows, x_ref, even_ref, odd_ref
                )

    total_ref[0] += jnp.dot(even_ref[...], cos_ref[...], preferred_element_type=F32)
    total_ref[1] += jnp.dot(odd_ref[...], sin_ref[...], preferred_element_type=F32)

    @pl.when(step == pl.num_programs(0) - 1)
    def _():
        emit_half_way(pairs, total_ref, y_ref, rows, bands, half, vloc, owners)


def row_table_kernel(dims, pos_ref, table_ref):
    rows, cols, bands, focal, band_total, total_rows, sources = dims
    r2 = 2 * rows
    for b in range(bands):
        band = jnp.full((rows, focal), 1, jnp.int32) * (pos_ref[1] * bands + b)
        q = (iota((rows, focal), 1).astype(F32) + (0.5 - focal / 2)) * SAMPLING
        q = focal_scale(q, band, band_total)
        tile_c, tile_s = turn_cos_sin(q * (iota(q.shape, 0).astype(F32) / cols))
        first = iota((sources, focal), 0).astype(F32) * rows + 0.5
        y = first / cols - total_rows / (2.0 * cols)
        shift_c, shift_s = turn_cos_sin(jnp.broadcast_to(q[:1], y.shape) * y)
        for d in range(sources):
            sc, ss = shift_c[d : d + 1], shift_s[d : d + 1]
            c = (tile_c * sc - tile_s * ss).astype(BF16)
            s_value = tile_s * sc + tile_c * ss
            s = s_value.astype(BF16)
            table_ref[b, d * r2 : d * r2 + rows, :focal] = c
            table_ref[b, d * r2 : d * r2 + rows, focal:] = (-s_value).astype(BF16)
            table_ref[b, d * r2 + rows : (d + 1) * r2, :focal] = s
            table_ref[b, d * r2 + rows : (d + 1) * r2, focal:] = c


def focal_kernel(dims, y_ref, target_ref, table_ref, h_ref):
    rows, sources, scale = dims
    r2 = 2 * rows
    lhs = jnp.concatenate([y_ref[d] for d in range(sources)], axis=1)
    f = jnp.dot(lhs, table_ref[...], preferred_element_type=F32)
    residual = (f * (2.0 * scale) - target_ref[...]).astype(BF16)
    spread = lax.dot_general(
        residual, table_ref[...], (((1,), (1,)), ((), ())), preferred_element_type=F32
    )
    for d in range(sources):
        h_ref[d] = spread[:, d * r2 : (d + 1) * r2].astype(BF16)


def fold_hidden(pairs, h_ref, left_ref, rows, bands, half, vloc, sources):
    r2 = 2 * rows
    nt = (((1,), (1,)), ((), ()))
    m = iota((half, 2 * half), 0)
    v = iota((half, 2 * half), 1)
    upper = (v == half + m).astype(F32)
    lower = (v == half - 1 - m).astype(F32)
    even, odd = (upper + lower).astype(BF16), (upper - lower).astype(BF16)
    same = (iota((r2, r2), 0) == iota((r2, r2), 1)).astype(F32).astype(BF16)
    for b in range(bands):
        for p in range(2 * pairs):
            if sources:
                block_h = jnp.concatenate(
                    [h_ref[d, b, p * vloc : (p + 1) * vloc, :] for d in range(sources)], axis=0
                )
            else:
                block_h = h_ref[b, p]

            def fold(mirror):
                folded = jnp.dot(mirror, block_h, preferred_element_type=F32).astype(BF16)
                return lax.dot_general(same, folded, nt, preferred_element_type=F32)

            plus, minus = fold(even), fold(odd)
            at = slice(p * r2, (p + 1) * r2)
            left_ref[0, at, b * half : (b + 1) * half] = plus.astype(BF16)
            left_ref[1, at, b * half : (b + 1) * half] = jnp.concatenate(
                [-minus[rows:], minus[:rows]], axis=0
            ).astype(BF16)


def weight_kernel(
    dims, pos_ref, box_ref, h_ref, x_ref, tile_ref, shift_ref, across_ref, index_ref,
    out_ref, give_ref, left_ref, pick_ref, cos_ref, sin_ref, p_ref, q_ref, weight_ref, sums_ref,
    term_ref, flat_ref, slot_ref,
):
    rows, cols, block, part, bands, half, per_row, pairs, vloc, sources, scale = dims
    step = pl.program_id(0)
    row0 = pos_ref[0] * rows
    r2 = 2 * rows
    nt = (((1,), (1,)), ((), ()))

    @pl.when(step == 0)
    def _():
        fold_hidden(pairs, h_ref, left_ref, rows, bands, half, vloc, sources)
        slot = iota((SROWS, r2), 0)
        lane = iota((SROWS, r2), 1)
        here = (row0 + lane % rows).astype(F32)
        low = jnp.zeros((SROWS, r2), F32)
        high = jnp.zeros((SROWS, r2), F32)
        for t in range(SROWS):
            low = jnp.where(slot == t, box_ref[0, t * per_row].astype(F32), low)
            high = jnp.where(slot == t, box_ref[1, t * per_row].astype(F32), high)
        mine = ((here >= low) & (here <= high)).astype(F32)
        down = mine * ((here - 0.5 * (low + high)) / (0.5 * (high - low + 1.0)))
        down_high = down.astype(BF16)
        pick_ref[:SROWS] = mine.astype(BF16)
        pick_ref[SROWS : 2 * SROWS] = down_high
        pick_ref[2 * SROWS :] = (down - down_high.astype(F32)).astype(BF16)

    tiles = part // LANES
    for k in range(block // part):
        slot = k % 2
        write_table(
            cos_ref.at[slot], sin_ref.at[slot], tile_ref, shift_ref,
            step * (block // LANES) + k * tiles, tiles,
        )
        p_ref[slot] = lax.dot_general(left_ref[0], cos_ref[slot], nt, preferred_element_type=F32)
        q_ref[slot] = lax.dot_general(left_ref[1], sin_ref[slot], nt, preferred_element_type=F32)
        for i in range(tiles):
            lanes = slice(i * LANES, (i + 1) * LANES)
            at = slice(k * part + i * LANES, k * part + (i + 1) * LANES)
            for g in range(0, rows, 16):
                near, far = None, None
                for p in range(2 * pairs):
                    j, first = divmod(p, 2)
                    re = slice(p * r2 + g, p * r2 + g + 16)
                    im = slice(p * r2 + rows + g, p * r2 + rows + g + 16)
                    xre = slice(first * r2 + g, first * r2 + g + 16)
                    xim = slice(first * r2 + rows + g, first * r2 + rows + g + 16)
                    p_re, p_im = p_ref[slot, re, lanes], p_ref[slot, im, lanes]
                    q_re, q_im = q_ref[slot, re, lanes], q_ref[slot, im, lanes]
                    x = [
                        [x_ref[j, side, rows_, at].astype(F32) for rows_ in (xre, xim)]
                        for side in range(2)
                    ]
                    near_term = x[0][0] * (p_im + q_im) - x[0][1] * (p_re + q_re)
                    far_term = x[1][0] * (p_im - q_im) - x[1][1] * (p_re - q_re)
                    near = near_term if near is None else near + near_term
                    far = far_term if far is None else far + far_term
                for side, value in enumerate((near, far)):
                    high = value.astype(BF16)
                    to = slice(side * block + at.start, side * block + at.stop)
                    weight_ref[g : g + 16, to] = high
                    weight_ref[rows + g : rows + g + 16, to] = (
                        value - high.astype(F32)
                    ).astype(BF16)
    sums = jnp.dot(pick_ref[...], weight_ref[...], preferred_element_type=F32)
    for side in range(2):
        mine = sums[:, side * block : (side + 1) * block]
        sums_ref[step, side, 0] = mine[:SROWS]
        sums_ref[step, side, 1] = mine[:SROWS] * across_ref[side]
        sums_ref[step, side, 2] = mine[SROWS : 2 * SROWS] + mine[2 * SROWS :]
        term_ref[step, side] = index_ref[side]

    @pl.when(step == pl.num_programs(0) - 1)
    def _():
        tops = [box_ref[0, t * per_row] for t in range(SROWS)]
        bottoms = [box_ref[1, t * per_row] for t in range(SROWS)]
        first = sum((bottom < row0).astype(jnp.int32) for bottom in bottoms)
        last = sum((top < row0 + rows).astype(jnp.int32) for top in tops)

        def tile_row(t, carry):
            def add(i, total):
                for side in range(2):
                    index = term_ref[i, side, pl.ds(t, 1), :].astype(F32).astype(BF16)
                    inside = jnp.where(tile_index == index, one, zero)
                    terms = [sums_ref[i, side, q, pl.ds(t, 1), :] for q in range(3)]
                    highs = [x.astype(BF16).astype(F32) for x in terms]
                    lows = [x - h for x, h in zip(terms, highs)]
                    stacked = jnp.concatenate(highs + lows + lows[:2], axis=0).astype(BF16)
                    total = total + lax.dot_general(
                        stacked, inside, nt, preferred_element_type=F32
                    )
                return total

            total = lax.fori_loop(0, pl.num_programs(0), add, jnp.zeros((8, padded), F32))
            slot_ref[:, :padded] = total
            total = jnp.where(iota((8, LANES), 1) < per_row, slot_ref[...], 0.0)
            padding = jnp.zeros((8, flat_ref.shape[1] - LANES), F32)
            wide = jnp.concatenate([total, padding], axis=1)
            flat_ref[...] += pltpu.roll(wide, t * per_row, axis=1)
            return carry

        padded = -(-per_row // 16) * 16
        tile_index = iota((padded, block), 0).astype(F32).astype(BF16)
        one = jnp.ones((padded, block), BF16)
        zero = jnp.zeros((padded, block), BF16)
        slot_ref[...] = jnp.zeros_like(slot_ref)
        flat_ref[...] = jnp.zeros_like(flat_ref)
        lax.fori_loop(first, last, tile_row, 0)
        odd = pos_ref[0] % 2 == 1
        pieces = flat_ref.shape[1] // (2 * LANES)
        for q in range(3):
            value = (flat_ref[q : q + 1] + flat_ref[q + 3 : q + 4]) * scale
            for i in range(pieces):
                low = value[:, i * LANES : (i + 1) * LANES]
                high = value[:, (pieces + i) * LANES : (pieces + i + 1) * LANES]
                at = q * pieces + i
                out_ref[at : at + 1] = jnp.where(odd, high, low)
                give_ref[at : at + 1] = jnp.where(odd, low, high)


def body(amplitude, seg_map, seg_box, seg_coeffs, probe_freq, probe_amp, measured):
    rows, cols = amplitude.shape
    owners = lax.axis_size("row")
    band_axis = lax.axis_size("band")
    total_rows = rows * owners
    bands, vloc, probes, _, focal = measured.shape
    pairs = probes // 2
    half = focal // 2
    band_total = bands * band_axis
    segments = seg_coeffs.shape[1]
    per_row = segments // SROWS
    r2 = 2 * rows
    normf = 1.0 / math.sqrt(total_rows * cols)
    aligned = vloc % 16 == 0
    half_cols = cols // 2
    field_block, block, part = BLOCKS
    k_width = bands * half

    pos = jnp.stack([lax.axis_index("row"), lax.axis_index("band")]).astype(jnp.int32)
    width = -(-(segments + LANES) // LANES) * LANES
    smem = pl.BlockSpec(memory_space=pltpu.SMEM)
    whole = pl.BlockSpec(memory_space=pltpu.VMEM)
    params = pltpu.CompilerParams(dimension_semantics=("arbitrary",))

    def resident(shape):
        return pl.BlockSpec(shape, lambda i: (0,) * len(shape), pipeline_mode=pl.Buffered(1))

    def cost(flops, moved):
        return pl.CostEstimate(flops=int(flops), bytes_accessed=int(moved), transcendentals=0)

    def slot_spec(block):
        return pl.BlockSpec((2, SROWS, block), lambda i: (0, 0, i))

    near = pl.BlockSpec((rows, field_block), lambda i: (0, i))
    far = pl.BlockSpec((rows, field_block), lambda i: (0, cols // field_block - 1 - i))
    tile_shape = (2, LANES, k_width)
    shift_shape = (2, half_cols // LANES, k_width)
    arrays = 2 * pairs
    y_dims = (owners, bands, arrays * vloc, r2) if aligned else (bands, arrays, focal, r2)
    y_spec = pl.BlockSpec(y_dims, lambda i: (0,) * len(y_dims))
    y_shape = jax.ShapeDtypeStruct(y_dims, BF16)
    def field_dims(block):
        return (
            rows, cols, block, bands, half, band_total, total_rows, per_row, vloc, aligned
        )

    matmul = 2 * 4 * rows * half_cols * k_width * 2

    def table_scratch(block):
        return [pltpu.VMEM((block, k_width), BF16), pltpu.VMEM((block, k_width), BF16)]

    fields, tile, shift, across, index, half_way = pl.pallas_call(
        functools.partial(field_kernel, (field_dims(field_block), pairs)),
        grid=(half_cols // field_block,),
        in_specs=[
            smem, smem, smem, smem,
            resident(seg_coeffs.shape),
            resident(seg_box.shape),
            near, far, near, far,
        ],
        out_specs=[
            pl.BlockSpec((pairs, 2, 4 * rows, field_block), lambda i: (0, 0, 0, i)),
            pl.BlockSpec(tile_shape, lambda i: (0, 0, 0)),
            pl.BlockSpec(shift_shape, lambda i: (0, 0, 0)),
            slot_spec(field_block),
            slot_spec(field_block),
            y_spec,
        ],
        out_shape=[
            jax.ShapeDtypeStruct((pairs, 2, 4 * rows, half_cols), BF16),
            jax.ShapeDtypeStruct(tile_shape, F32),
            jax.ShapeDtypeStruct(shift_shape, F32),
            jax.ShapeDtypeStruct((2, SROWS, half_cols), F32),
            jax.ShapeDtypeStruct((2, SROWS, half_cols), jnp.int32),
            y_shape,
        ],
        scratch_shapes=[
            pltpu.VMEM((8, width), F32),
            pltpu.VMEM((3, rows, LANES), F32),
            pltpu.VMEM((rows, LANES), jnp.int32),
            pltpu.VMEM((2, SROWS, LANES), F32),
            pltpu.VMEM((2 * pairs, rows, LANES), F32),
            *table_scratch(field_block),
            pltpu.VMEM((4 * pairs * rows, field_block), BF16),
            pltpu.VMEM((4 * pairs * rows, field_block), BF16),
            pltpu.VMEM((2, 4 * pairs * rows, k_width), F32),
            pltpu.VMEM((2, SROWS, field_block), jnp.int32),
        ],
        compiler_params=params,
        cost_estimate=cost(4 * matmul, 20e6),
        name="field",
    )(pos, seg_box, probe_freq, probe_amp, seg_coeffs, seg_box,
      amplitude, amplitude, seg_map, seg_map)

    if not aligned:
        half_way = (
            half_way.reshape(bands, arrays, owners, vloc, r2)
            .transpose(2, 0, 1, 3, 4)
            .reshape(owners, bands, arrays * vloc, r2)
        )
    received = lax.all_to_all(half_way, "row", split_axis=0, concat_axis=0, tiled=True)

    row_table = pl.pallas_call(
        functools.partial(
            row_table_kernel, (rows, cols, bands, focal, band_total, total_rows, owners)
        ),
        in_specs=[smem],
        out_specs=whole,
        out_shape=jax.ShapeDtypeStruct((bands, owners * r2, 2 * focal), BF16),
        cost_estimate=cost(1e6, 2e6),
        name="row_table",
    )(pos)

    plus, minus = measured[:, :, 0::2], measured[:, :, 1::2]
    total, difference = plus + minus, plus - minus
    turned = jnp.stack([difference[:, :, :, 1], -difference[:, :, :, 0]], axis=3)
    targets = jnp.stack([total, turned], axis=3)
    targets = targets.transpose(0, 2, 3, 1, 4, 5).reshape(bands, arrays * vloc, 2 * focal)

    y_block = pl.BlockSpec((owners, None, arrays * vloc, r2), lambda b: (0, b, 0, 0))
    spread = pl.pallas_call(
        functools.partial(focal_kernel, (rows, owners, normf)),
        grid=(bands,),
        in_specs=[
            y_block,
            pl.BlockSpec((None, arrays * vloc, 2 * focal), lambda b: (b, 0, 0)),
            pl.BlockSpec((None, owners * r2, 2 * focal), lambda b: (b, 0, 0)),
        ],
        out_specs=y_block,
        out_shape=jax.ShapeDtypeStruct((owners, bands, arrays * vloc, r2), BF16),
        compiler_params=params,
        cost_estimate=cost(8 * bands * arrays * vloc * owners * r2 * focal, 4e6),
        name="focal",
    )(received, targets, row_table)
    hidden = lax.all_to_all(spread, "row", split_axis=0, concat_axis=0, tiled=True)
    if not aligned:
        hidden = (
            hidden.reshape(owners, bands, arrays, vloc, r2)
            .transpose(1, 2, 0, 3, 4)
            .reshape(bands, arrays, focal, r2)
        )

    scale = 2.0 * normf / (band_total * probes)
    steps = half_cols // block
    weight_dims = (
        rows, cols, block, part, bands, half, per_row, pairs, vloc,
        owners if aligned else 0, scale,
    )
    pieces = -(-segments // (2 * LANES))
    share = jax.ShapeDtypeStruct((3 * pieces, LANES), F32)
    kept, given = pl.pallas_call(
        functools.partial(weight_kernel, weight_dims),
        grid=(steps,),
        in_specs=[
            smem, smem, resident(hidden.shape),
            pl.BlockSpec((pairs, 2, 4 * rows, block), lambda i: (0, 0, 0, i)),
            resident(tile_shape), resident(shift_shape), slot_spec(block), slot_spec(block),
        ],
        out_specs=[pl.BlockSpec(share.shape, lambda i: (0, 0))] * 2,
        out_shape=[share, share],
        scratch_shapes=[
            pltpu.VMEM((2, 4 * pairs * rows, k_width), BF16),
            pltpu.VMEM((3 * SROWS, r2), BF16),
            pltpu.VMEM((2, part, k_width), BF16),
            pltpu.VMEM((2, part, k_width), BF16),
            pltpu.VMEM((2, 4 * pairs * rows, part), F32),
            pltpu.VMEM((2, 4 * pairs * rows, part), F32),
            pltpu.VMEM((r2, 2 * block), BF16),
            pltpu.VMEM((steps, 2, 3, SROWS, block), F32),
            pltpu.VMEM((steps, 2, SROWS, block), jnp.int32),
            pltpu.VMEM((8, 2 * pieces * LANES), F32),
            pltpu.VMEM((8, LANES), F32),
        ],
        compiler_params=params,
        cost_estimate=cost(4 * matmul, 20e6),
        name="weight",
    )(pos, seg_box, hidden, fields, tile, shift, across, index)

    axes = ("band", "row")
    devices = owners * band_axis
    groups = [[d for d in range(devices) if d % 2 == core] for core in range(2)]

    def swap_cores(array):
        return lax.ppermute(array, "row", [(i, i ^ 1) for i in range(owners)])

    mine = kept + swap_cores(given)
    copies = jnp.broadcast_to(mine[None], (devices // 2,) + mine.shape)
    everyones = lax.all_to_all(
        copies, axes, split_axis=0, concat_axis=0, tiled=True, axis_index_groups=groups
    )
    mine = jnp.sum(everyones, axis=0)
    other = swap_cores(mine)
    odd = lax.axis_index("row") % 2 == 1
    halves = [jnp.where(odd, other, mine), jnp.where(odd, mine, other)]
    halves = [x.reshape(3, pieces * LANES) for x in halves]
    return jnp.concatenate(halves, axis=1)[:, :segments]


def solution(mesh):
    in_specs = (
        P("row", None),
        P("row", None),
        P(),
        P(),
        P(),
        P(),
        P("band", "row", None, None, None),
    )
    return jax.shard_map(body, mesh=mesh, in_specs=in_specs, out_specs=P(), check_vma=False)
```

```python
import functools
import math

import jax
import jax.numpy as jnp
from jax import lax
from jax.experimental import pallas as pl
from jax.experimental.pallas import tpu as pltpu
from jax.sharding import PartitionSpec as P

SROWS = 16
SAMPLING = 0.5
SPREAD = 0.2
TWO_PI = 2.0 * math.pi
LANES = 128
F32 = jnp.float32
BLOCKS = (512, 2048, 256)
BF16 = jnp.bfloat16

SIN_HALF = (0.9999999971, -0.1666666029, 0.008333109246, -0.0001981365728, 2.616271295e-06)
COS_HALF = (0.9999999682, -0.4999993032, 0.04166421727, -0.001385868782, 2.327410856e-05)
SIN_WAVE = (0.9999999964, -0.166666488, 0.008331936401, -0.000194912576)
COS_WAVE = (0.9999999679, -0.499998396, 0.04165412354, -0.001357443708)
SIN_TURN = (
    6.283185307, -41.34170222, 81.60524741, -76.70580003,
    42.05775188, -15.08655272, 3.781282403, -0.6207370354,
)
COS_TURN = (
    0.9999999999, -19.73920874, 64.93938905, -85.45665775,
    60.24212493, -26.40463062, 7.800022219, -1.452987552,
)


def series(coeffs, t):
    value = jnp.full_like(t, coeffs[-1])
    for c in reversed(coeffs[:-1]):
        value = value * t + c
    return value


def turn_cos_sin(turns):
    t = turns - jnp.floor(turns + 0.5)
    square = t * t
    return series(COS_TURN, square), t * series(SIN_TURN, square)


def iota(shape, axis):
    return lax.broadcasted_iota(jnp.int32, shape, axis)


def focal_scale(m_positive, band, band_total):
    ratio = 1.0 + SPREAD * ((band.astype(F32) + 0.5) / band_total - 0.5)
    return m_positive / ratio


def band_lanes(first_band, bands, half, band_total, rows):
    pieces = []
    for b in range(bands):
        q = (iota((rows, half), 1).astype(F32) + 0.5) * SAMPLING
        band = jnp.full((rows, half), 1, jnp.int32) * (first_band + b)
        pieces.append(focal_scale(q, band, band_total))
    return jnp.concatenate(pieces, axis=1)


def column_tables(first_band, bands, half, band_total, cols, tile_ref, shift_ref):
    q = band_lanes(first_band, bands, half, band_total, LANES)
    c, s = turn_cos_sin(q * (iota(q.shape, 0).astype(F32) / cols))
    tile_ref[0] = c
    tile_ref[1] = s
    tiles = cols // (2 * LANES)
    q = band_lanes(first_band, bands, half, band_total, tiles)
    x = (iota(q.shape, 0).astype(F32) * LANES + 0.5) / cols - 0.5
    c, s = turn_cos_sin(q * x)
    shift_ref[0] = c
    shift_ref[1] = s


def write_table(cos_ref, sin_ref, tile_ref, shift_ref, first_tile, tiles):
    for i in range(tiles):
        sc = shift_ref[0, pl.ds(first_tile + i, 1), :]
        ss = shift_ref[1, pl.ds(first_tile + i, 1), :]
        for k in range(0, LANES, 16):
            tc = tile_ref[0, k : k + 16]
            ts = tile_ref[1, k : k + 16]
            rows = slice(i * LANES + k, i * LANES + k + 16)
            cos_ref[rows] = (tc * sc - ts * ss).astype(BF16)
            sin_ref[rows] = (ts * sc + tc * ss).astype(BF16)


def load_segments(coeffs_ref, boxes_ref, seg_ref):
    seg_ref[...] = jnp.zeros_like(seg_ref)
    seg_ref[0:3, : coeffs_ref.shape[1]] = coeffs_ref[...]
    seg_ref[3:7, : boxes_ref.shape[1]] = boxes_ref[...].astype(F32)


def reverse(x):
    back = LANES - 1 - iota((8, LANES), 1)
    pieces = [gather_lanes(x[k : k + 8], back) for k in range(0, x.shape[0], 8)]
    return pieces[0] if len(pieces) == 1 else jnp.concatenate(pieces, axis=0)


def gather_lanes(x, index):
    return jnp.take_along_axis(x, index, axis=1, mode="promise_in_bounds")


def tile_row_pieces(seg_ref, per_row, width):
    for t in range(SROWS):
        yield t, pltpu.roll(seg_ref[...], (width - t * per_row) % width, axis=1)[:, :LANES]


def probe_setup(pos_ref, freq_ref, amp_ref, j, rows, cols, total_rows, waves):
    row = pos_ref[0] * rows + iota((rows, LANES), 0)
    y = (row.astype(F32) + 0.5) / cols - total_rows / (2.0 * cols)
    c, s = turn_cos_sin(freq_ref[j, 1].astype(F32) * y)
    waves[2 * j] = amp_ref[j] * c
    waves[2 * j + 1] = amp_ref[j] * s


def column_wave(freq_ref, pairs, step, block, cols):
    row = iota((8, block), 0)
    freq = jnp.zeros((8, block), F32)
    for j in range(pairs):
        freq = jnp.where(row // 2 == j, freq_ref[j, 0].astype(F32), freq)
    x = ((iota((8, block), 1) + step * block).astype(F32) + 0.5) / cols - 0.5
    c, s = turn_cos_sin(freq * x)
    return jnp.where(row % 2 == 0, s, c)


def emit_pair(j, column, waves, fields, here, lanes, g, rows, x_ref, even_ref, odd_ref):
    from_sin = column[2 * j : 2 * j + 1, lanes] * waves[2 * j, here]
    from_cos = column[2 * j + 1 : 2 * j + 2, lanes] * waves[2 * j + 1, here]
    parts = []
    for wave in (from_cos + from_sin, from_cos - from_sin):
        square = wave * wave
        parts.append(
            (
                series(COS_WAVE, square).astype(BF16),
                (wave * series(SIN_WAVE, square)).astype(BF16),
            )
        )
    for k in range(2):
        for o in range(2):
            at = (2 * k + o) * rows + g
            near = fields[0][o] * parts[0][k]
            far = fields[1][o] * parts[1][k]
            x_ref[j, 0, at : at + 16, lanes] = near
            x_ref[j, 1, at : at + 16, lanes] = far
            at = at + 4 * j * rows
            even_ref[at : at + 16, lanes] = near + far
            odd_ref[at : at + 16, lanes] = near - far


def emit_half_way(pairs, total_ref, y_ref, rows, bands, half, vloc, owners):
    r2 = 2 * rows
    m = iota((half, half), 0)
    n = iota((half, half), 1)
    straight = (m == n).astype(F32).astype(BF16)
    turned = (m + n == half - 1).astype(F32).astype(BF16)
    nt = (((1,), (1,)), ((), ()))
    for b in range(bands):
        for p in range(2 * pairs):
            at = slice(p * r2, (p + 1) * r2)
            cos_part = total_ref[0, at, b * half : (b + 1) * half]
            sin_part = total_ref[1, at, b * half : (b + 1) * half]
            swapped = jnp.concatenate([sin_part[rows:], -sin_part[:rows]], axis=0)
            low = lax.dot_general(
                turned, (cos_part - swapped).astype(BF16), nt, preferred_element_type=F32
            ).astype(BF16)
            high = lax.dot_general(
                straight, (cos_part + swapped).astype(BF16), nt, preferred_element_type=F32
            ).astype(BF16)
            if owners:
                each = half // vloc
                for d in range(each):
                    own = slice(d * vloc, (d + 1) * vloc)
                    y_ref[d, b, p * vloc : (p + 1) * vloc, :] = low[own]
                    y_ref[each + d, b, p * vloc : (p + 1) * vloc, :] = high[own]
            else:
                y_ref[b, p, :half, :] = low
                y_ref[b, p, half:, :] = high


def field_kernel(
    dims, pos_ref, box_ref, freq_ref, amp_ref, coeffs_ref, boxes_ref,
    amplitude_ref, amplitude_far_ref, map_ref, map_far_ref,
    x_ref, tile_ref, shift_ref, across_ref, index_ref, y_ref, *rest
):
    dims, pairs = dims
    (
        seg_ref, tables, bases, slot_tables, waves, cos_ref, sin_ref, even_ref, odd_ref, total_ref, slot_map,
    ) = rest
    rows, cols, block, bands, half, band_total, total_rows, per_row, vloc, owners = dims
    step = pl.program_id(0)
    row0 = pos_ref[0] * rows
    chunks = block // LANES
    maps = (map_ref, map_far_ref)
    amplitudes = (amplitude_ref, amplitude_far_ref)

    @pl.when(step == 0)
    def _():
        load_segments(coeffs_ref, boxes_ref, seg_ref)
        width = seg_ref.shape[1]
        groups = rows // 8
        values = [[jnp.zeros((8, LANES), F32)] * 3 for _ in range(groups)]
        base = [jnp.zeros((8, LANES), jnp.int32)] * groups
        for t, piece in tile_row_pieces(seg_ref, per_row, width):
            part = [jnp.broadcast_to(piece[k : k + 1], (8, LANES)) for k in range(7)]
            low, high = part[3][:, :1], part[4][:, :1]
            mid_row = 0.5 * (part[3] + part[4])
            inv_row = 1.0 / (part[4] - part[3] + 1.0)
            mid = 0.5 * (part[5] + part[6])
            inv = 2.0 / (part[6] - part[5] + 1.0)
            slope = 0.5 * part[1] * inv
            slot_tables[0, t : t + 1] = mid[:1]
            slot_tables[1, t : t + 1] = inv[:1]
            for g in range(groups):
                here = (row0 + g * 8 + iota((8, LANES), 0)).astype(F32)
                mine = (here >= low) & (here <= high)
                new = (0.5 * part[0] + part[2] * ((here - mid_row) * inv_row), slope, mid)
                values[g] = [jnp.where(mine, n, v) for n, v in zip(new, values[g])]
                base[g] = jnp.where(mine, t * per_row, base[g])
        for g in range(groups):
            for k in range(3):
                tables[k, g * 8 : (g + 1) * 8] = values[g][k]
            bases[g * 8 : (g + 1) * 8] = base[g]
        for j in range(pairs):
            probe_setup(pos_ref, freq_ref, amp_ref, j, rows, cols, total_rows, waves)
        column_tables(pos_ref[1] * bands, bands, half, band_total, cols, tile_ref, shift_ref)
        total_ref[...] = jnp.zeros_like(total_ref)

    for t in range(SROWS):
        first = jnp.clip(box_ref[0, t * per_row] - row0, 0, rows - 1)
        for side in range(2):
            slot_map[side, t : t + 1, :] = maps[side][pl.ds(first, 1), :] - t * per_row

    column = column_wave(freq_ref, pairs, step, block, cols)
    write_table(cos_ref, sin_ref, tile_ref, shift_ref, step * chunks, chunks)

    for i in range(chunks):
        lanes = slice(i * LANES, (i + 1) * LANES)
        far_lanes = slice((chunks - 1 - i) * LANES, (chunks - i) * LANES)
        near_column = (iota((8, LANES), 1) + (step * block + i * LANES)).astype(F32)
        columns = (near_column, (cols - 1.0) - near_column)
        for side in range(2):
            for t in range(0, SROWS, 8):
                index = slot_map[side, t : t + 8, far_lanes if side else lanes] & (LANES - 1)
                if side:
                    index = reverse(index)
                mid = gather_lanes(slot_tables[0, t : t + 8], index)
                inv = gather_lanes(slot_tables[1, t : t + 8], index)
                across_ref[side, t : t + 8, lanes] = (columns[side] - mid) * inv
                index_ref[side, t : t + 8, lanes] = index
        for g in range(0, rows, 16):
            here = slice(g, g + 16)
            fields = []
            for side in range(2):
                source = far_lanes if side else lanes
                size = amplitudes[side][here, source].astype(F32)
                halves = []
                for h in (0, 8):
                    own = slice(g + h, g + h + 8)
                    index = maps[side][own, source] - bases[own]
                    if side:
                        index = reverse(index)
                    half_phase = gather_lanes(tables[0, own], index) + gather_lanes(
                        tables[1, own], index
                    ) * (columns[side] - gather_lanes(tables[2, own], index))
                    square = half_phase * half_phase
                    s = half_phase * series(SIN_HALF, square)
                    c = series(COS_HALF, square)
                    twice = s + s
                    own_size = size[h : h + 8]
                    if side:
                        own_size = reverse(own_size)
                    halves.append((own_size * (1.0 - twice * s), own_size * (twice * c)))
                both = [
                    jnp.concatenate([halves[0][o], halves[1][o]], axis=0).astype(BF16)
                    for o in range(2)
                ]
                fields.append(both)
            for j in range(pairs):
                emit_pair(
                    j, column, waves, fields, here, lanes, g, rows, x_ref, even_ref, odd_ref
                )

    total_ref[0] += jnp.dot(even_ref[...], cos_ref[...], preferred_element_type=F32)
    total_ref[1] += jnp.dot(odd_ref[...], sin_ref[...], preferred_element_type=F32)

    @pl.when(step == pl.num_programs(0) - 1)
    def _():
        emit_half_way(pairs, total_ref, y_ref, rows, bands, half, vloc, owners)


def row_table_kernel(dims, pos_ref, table_ref):
    rows, cols, bands, focal, band_total, total_rows, sources = dims
    r2 = 2 * rows
    for b in range(bands):
        band = jnp.full((rows, focal), 1, jnp.int32) * (pos_ref[1] * bands + b)
        q = (iota((rows, focal), 1).astype(F32) + (0.5 - focal / 2)) * SAMPLING
        q = focal_scale(q, band, band_total)
        tile_c, tile_s = turn_cos_sin(q * (iota(q.shape, 0).astype(F32) / cols))
        first = iota((sources, focal), 0).astype(F32) * rows + 0.5
        y = first / cols - total_rows / (2.0 * cols)
        shift_c, shift_s = turn_cos_sin(jnp.broadcast_to(q[:1], y.shape) * y)
        for d in range(sources):
            sc, ss = shift_c[d : d + 1], shift_s[d : d + 1]
            c = (tile_c * sc - tile_s * ss).astype(BF16)
            s_value = tile_s * sc + tile_c * ss
            s = s_value.astype(BF16)
            table_ref[b, d * r2 : d * r2 + rows, :focal] = c
            table_ref[b, d * r2 : d * r2 + rows, focal:] = (-s_value).astype(BF16)
            table_ref[b, d * r2 + rows : (d + 1) * r2, :focal] = s
            table_ref[b, d * r2 + rows : (d + 1) * r2, focal:] = c


def focal_kernel(dims, y_ref, target_ref, table_ref, h_ref):
    rows, sources, scale = dims
    r2 = 2 * rows
    lhs = jnp.concatenate([y_ref[d] for d in range(sources)], axis=1)
    f = jnp.dot(lhs, table_ref[...], preferred_element_type=F32)
    residual = (f * (2.0 * scale) - target_ref[...]).astype(BF16)
    spread = lax.dot_general(
        residual, table_ref[...], (((1,), (1,)), ((), ())), preferred_element_type=F32
    )
    for d in range(sources):
        h_ref[d] = spread[:, d * r2 : (d + 1) * r2].astype(BF16)


def fold_hidden(pairs, h_ref, left_ref, rows, bands, half, vloc, sources):
    r2 = 2 * rows
    nt = (((1,), (1,)), ((), ()))
    m = iota((half, 2 * half), 0)
    v = iota((half, 2 * half), 1)
    upper = (v == half + m).astype(F32)
    lower = (v == half - 1 - m).astype(F32)
    even, odd = (upper + lower).astype(BF16), (upper - lower).astype(BF16)
    same = (iota((r2, r2), 0) == iota((r2, r2), 1)).astype(F32).astype(BF16)
    for b in range(bands):
        for p in range(2 * pairs):
            if sources:
                block_h = jnp.concatenate(
                    [h_ref[d, b, p * vloc : (p + 1) * vloc, :] for d in range(sources)], axis=0
                )
            else:
                block_h = h_ref[b, p]

            def fold(mirror):
                folded = jnp.dot(mirror, block_h, preferred_element_type=F32).astype(BF16)
                return lax.dot_general(same, folded, nt, preferred_element_type=F32)

            plus, minus = fold(even), fold(odd)
            at = slice(p * r2, (p + 1) * r2)
            left_ref[0, at, b * half : (b + 1) * half] = plus.astype(BF16)
            left_ref[1, at, b * half : (b + 1) * half] = jnp.concatenate(
                [-minus[rows:], minus[:rows]], axis=0
            ).astype(BF16)


def weight_kernel(
    dims, pos_ref, box_ref, h_ref, x_ref, tile_ref, shift_ref, across_ref, index_ref,
    out_ref, give_ref, left_ref, pick_ref, cos_ref, sin_ref, p_ref, q_ref, weight_ref, sums_ref,
    term_ref, flat_ref, slot_ref,
):
    rows, cols, block, part, bands, half, per_row, pairs, vloc, sources, scale = dims
    step = pl.program_id(0)
    row0 = pos_ref[0] * rows
    r2 = 2 * rows
    nt = (((1,), (1,)), ((), ()))

    @pl.when(step == 0)
    def _():
        fold_hidden(pairs, h_ref, left_ref, rows, bands, half, vloc, sources)
        slot = iota((SROWS, r2), 0)
        lane = iota((SROWS, r2), 1)
        here = (row0 + lane % rows).astype(F32)
        low = jnp.zeros((SROWS, r2), F32)
        high = jnp.zeros((SROWS, r2), F32)
        for t in range(SROWS):
            low = jnp.where(slot == t, box_ref[0, t * per_row].astype(F32), low)
            high = jnp.where(slot == t, box_ref[1, t * per_row].astype(F32), high)
        mine = ((here >= low) & (here <= high)).astype(F32)
        down = mine * ((here - 0.5 * (low + high)) / (0.5 * (high - low + 1.0)))
        down_high = down.astype(BF16)
        pick_ref[:SROWS] = mine.astype(BF16)
        pick_ref[SROWS : 2 * SROWS] = down_high
        pick_ref[2 * SROWS :] = (down - down_high.astype(F32)).astype(BF16)

    tiles = part // LANES
    for k in range(block // part):
        slot = k % 2
        write_table(
            cos_ref.at[slot], sin_ref.at[slot], tile_ref, shift_ref,
            step * (block // LANES) + k * tiles, tiles,
        )
        p_ref[slot] = lax.dot_general(left_ref[0], cos_ref[slot], nt, preferred_element_type=F32)
        q_ref[slot] = lax.dot_general(left_ref[1], sin_ref[slot], nt, preferred_element_type=F32)
        for i in range(tiles):
            lanes = slice(i * LANES, (i + 1) * LANES)
            at = slice(k * part + i * LANES, k * part + (i + 1) * LANES)
            for g in range(0, rows, 16):
                near, far = None, None
                for p in range(2 * pairs):
                    j, first = divmod(p, 2)
                    re = slice(p * r2 + g, p * r2 + g + 16)
                    im = slice(p * r2 + rows + g, p * r2 + rows + g + 16)
                    xre = slice(first * r2 + g, first * r2 + g + 16)
                    xim = slice(first * r2 + rows + g, first * r2 + rows + g + 16)
                    p_re, p_im = p_ref[slot, re, lanes], p_ref[slot, im, lanes]
                    q_re, q_im = q_ref[slot, re, lanes], q_ref[slot, im, lanes]
                    x = [
                        [x_ref[j, side, rows_, at].astype(F32) for rows_ in (xre, xim)]
                        for side in range(2)
                    ]
                    near_term = x[0][0] * (p_im + q_im) - x[0][1] * (p_re + q_re)
                    far_term = x[1][0] * (p_im - q_im) - x[1][1] * (p_re - q_re)
                    near = near_term if near is None else near + near_term
                    far = far_term if far is None else far + far_term
                for side, value in enumerate((near, far)):
                    high = value.astype(BF16)
                    to = slice(side * block + at.start, side * block + at.stop)
                    weight_ref[g : g + 16, to] = high
                    weight_ref[rows + g : rows + g + 16, to] = (
                        value - high.astype(F32)
                    ).astype(BF16)
    sums = jnp.dot(pick_ref[...], weight_ref[...], preferred_element_type=F32)
    for side in range(2):
        mine = sums[:, side * block : (side + 1) * block]
        sums_ref[step, side, 0] = mine[:SROWS]
        sums_ref[step, side, 1] = mine[:SROWS] * across_ref[side]
        sums_ref[step, side, 2] = mine[SROWS : 2 * SROWS] + mine[2 * SROWS :]
        term_ref[step, side] = index_ref[side]

    @pl.when(step == pl.num_programs(0) - 1)
    def _():
        tops = [box_ref[0, t * per_row] for t in range(SROWS)]
        bottoms = [box_ref[1, t * per_row] for t in range(SROWS)]
        first = sum((bottom < row0).astype(jnp.int32) for bottom in bottoms)
        last = sum((top < row0 + rows).astype(jnp.int32) for top in tops)

        def tile_row(t, carry):
            def add(i, total):
                for side in range(2):
                    index = term_ref[i, side, pl.ds(t, 1), :].astype(F32).astype(BF16)
                    inside = jnp.where(tile_index == index, one, zero)
                    terms = [sums_ref[i, side, q, pl.ds(t, 1), :] for q in range(3)]
                    highs = [x.astype(BF16).astype(F32) for x in terms]
                    lows = [x - h for x, h in zip(terms, highs)]
                    stacked = jnp.concatenate(highs + lows + lows[:2], axis=0).astype(BF16)
                    total = total + lax.dot_general(
                        stacked, inside, nt, preferred_element_type=F32
                    )
                return total

            total = lax.fori_loop(0, pl.num_programs(0), add, jnp.zeros((8, padded), F32))
            slot_ref[:, :padded] = total
            total = jnp.where(iota((8, LANES), 1) < per_row, slot_ref[...], 0.0)
            padding = jnp.zeros((8, flat_ref.shape[1] - LANES), F32)
            wide = jnp.concatenate([total, padding], axis=1)
            flat_ref[...] += pltpu.roll(wide, t * per_row, axis=1)
            return carry

        padded = -(-per_row // 16) * 16
        tile_index = iota((padded, block), 0).astype(F32).astype(BF16)
        one = jnp.ones((padded, block), BF16)
        zero = jnp.zeros((padded, block), BF16)
        slot_ref[...] = jnp.zeros_like(slot_ref)
        flat_ref[...] = jnp.zeros_like(flat_ref)
        lax.fori_loop(first, last, tile_row, 0)
        odd = pos_ref[0] % 2 == 1
        pieces = flat_ref.shape[1] // (2 * LANES)
        for q in range(3):
            value = (flat_ref[q : q + 1] + flat_ref[q + 3 : q + 4]) * scale
            for i in range(pieces):
                low = value[:, i * LANES : (i + 1) * LANES]
                high = value[:, (pieces + i) * LANES : (pieces + i + 1) * LANES]
                at = q * pieces + i
                out_ref[at : at + 1] = jnp.where(odd, high, low)
                give_ref[at : at + 1] = jnp.where(odd, low, high)


def body(amplitude, seg_map, seg_box, seg_coeffs, probe_freq, probe_amp, measured):
    rows, cols = amplitude.shape
    owners = lax.axis_size("row")
    band_axis = lax.axis_size("band")
    total_rows = rows * owners
    bands, vloc, probes, _, focal = measured.shape
    pairs = probes // 2
    half = focal // 2
    band_total = bands * band_axis
    segments = seg_coeffs.shape[1]
    per_row = segments // SROWS
    r2 = 2 * rows
    normf = 1.0 / math.sqrt(total_rows * cols)
    aligned = vloc % 16 == 0
    half_cols = cols // 2
    field_block, block, part = BLOCKS
    k_width = bands * half

    pos = jnp.stack([lax.axis_index("row"), lax.axis_index("band")]).astype(jnp.int32)
    width = -(-(segments + LANES) // LANES) * LANES
    smem = pl.BlockSpec(memory_space=pltpu.SMEM)
    whole = pl.BlockSpec(memory_space=pltpu.VMEM)
    params = pltpu.CompilerParams(dimension_semantics=("arbitrary",))

    def resident(shape):
        return pl.BlockSpec(shape, lambda i: (0,) * len(shape), pipeline_mode=pl.Buffered(1))

    def cost(flops, moved):
        return pl.CostEstimate(flops=int(flops), bytes_accessed=int(moved), transcendentals=0)

    def slot_spec(block):
        return pl.BlockSpec((2, SROWS, block), lambda i: (0, 0, i))

    near = pl.BlockSpec((rows, field_block), lambda i: (0, i))
    far = pl.BlockSpec((rows, field_block), lambda i: (0, cols // field_block - 1 - i))
    tile_shape = (2, LANES, k_width)
    shift_shape = (2, half_cols // LANES, k_width)
    arrays = 2 * pairs
    y_dims = (owners, bands, arrays * vloc, r2) if aligned else (bands, arrays, focal, r2)
    y_spec = pl.BlockSpec(y_dims, lambda i: (0,) * len(y_dims))
    y_shape = jax.ShapeDtypeStruct(y_dims, BF16)
    def field_dims(block):
        return (
            rows, cols, block, bands, half, band_total, total_rows, per_row, vloc, aligned
        )

    matmul = 2 * 4 * rows * half_cols * k_width * 2

    def table_scratch(block):
        return [pltpu.VMEM((block, k_width), BF16), pltpu.VMEM((block, k_width), BF16)]

    fields, tile, shift, across, index, half_way = pl.pallas_call(
        functools.partial(field_kernel, (field_dims(field_block), pairs)),
        grid=(half_cols // field_block,),
        in_specs=[
            smem, smem, smem, smem,
            resident(seg_coeffs.shape),
            resident(seg_box.shape),
            near, far, near, far,
        ],
        out_specs=[
            pl.BlockSpec((pairs, 2, 4 * rows, field_block), lambda i: (0, 0, 0, i)),
            pl.BlockSpec(tile_shape, lambda i: (0, 0, 0)),
            pl.BlockSpec(shift_shape, lambda i: (0, 0, 0)),
            slot_spec(field_block),
            slot_spec(field_block),
            y_spec,
        ],
        out_shape=[
            jax.ShapeDtypeStruct((pairs, 2, 4 * rows, half_cols), BF16),
            jax.ShapeDtypeStruct(tile_shape, F32),
            jax.ShapeDtypeStruct(shift_shape, F32),
            jax.ShapeDtypeStruct((2, SROWS, half_cols), F32),
            jax.ShapeDtypeStruct((2, SROWS, half_cols), jnp.int32),
            y_shape,
        ],
        scratch_shapes=[
            pltpu.VMEM((8, width), F32),
            pltpu.VMEM((3, rows, LANES), F32),
            pltpu.VMEM((rows, LANES), jnp.int32),
            pltpu.VMEM((2, SROWS, LANES), F32),
            pltpu.VMEM((2 * pairs, rows, LANES), F32),
            *table_scratch(field_block),
            pltpu.VMEM((4 * pairs * rows, field_block), BF16),
            pltpu.VMEM((4 * pairs * rows, field_block), BF16),
            pltpu.VMEM((2, 4 * pairs * rows, k_width), F32),
            pltpu.VMEM((2, SROWS, field_block), jnp.int32),
        ],
        compiler_params=params,
        cost_estimate=cost(4 * matmul, 20e6),
        name="field",
    )(pos, seg_box, probe_freq, probe_amp, seg_coeffs, seg_box,
      amplitude, amplitude, seg_map, seg_map)

    if not aligned:
        half_way = (
            half_way.reshape(bands, arrays, owners, vloc, r2)
            .transpose(2, 0, 1, 3, 4)
            .reshape(owners, bands, arrays * vloc, r2)
        )
    received = lax.all_to_all(half_way, "row", split_axis=0, concat_axis=0, tiled=True)

    row_table = pl.pallas_call(
        functools.partial(
            row_table_kernel, (rows, cols, bands, focal, band_total, total_rows, owners)
        ),
        in_specs=[smem],
        out_specs=whole,
        out_shape=jax.ShapeDtypeStruct((bands, owners * r2, 2 * focal), BF16),
        cost_estimate=cost(1e6, 2e6),
        name="row_table",
    )(pos)

    plus, minus = measured[:, :, 0::2], measured[:, :, 1::2]
    total, difference = plus + minus, plus - minus
    turned = jnp.stack([difference[:, :, :, 1], -difference[:, :, :, 0]], axis=3)
    targets = jnp.stack([total, turned], axis=3)
    targets = targets.transpose(0, 2, 3, 1, 4, 5).reshape(bands, arrays * vloc, 2 * focal)

    y_block = pl.BlockSpec((owners, None, arrays * vloc, r2), lambda b: (0, b, 0, 0))
    spread = pl.pallas_call(
        functools.partial(focal_kernel, (rows, owners, normf)),
        grid=(bands,),
        in_specs=[
            y_block,
            pl.BlockSpec((None, arrays * vloc, 2 * focal), lambda b: (b, 0, 0)),
            pl.BlockSpec((None, owners * r2, 2 * focal), lambda b: (b, 0, 0)),
        ],
        out_specs=y_block,
        out_shape=jax.ShapeDtypeStruct((owners, bands, arrays * vloc, r2), BF16),
        compiler_params=pltpu.CompilerParams(
            dimension_semantics=("arbitrary",), vmem_limit_bytes=24 << 20
        ),
        cost_estimate=cost(8 * bands * arrays * vloc * owners * r2 * focal, 4e6),
        name="focal",
    )(received, targets, row_table)
    hidden = lax.all_to_all(spread, "row", split_axis=0, concat_axis=0, tiled=True)
    if not aligned:
        hidden = (
            hidden.reshape(owners, bands, arrays, vloc, r2)
            .transpose(1, 2, 0, 3, 4)
            .reshape(bands, arrays, focal, r2)
        )

    scale = 2.0 * normf / (band_total * probes)
    steps = half_cols // block
    weight_dims = (
        rows, cols, block, part, bands, half, per_row, pairs, vloc,
        owners if aligned else 0, scale,
    )
    pieces = -(-segments // (2 * LANES))
    share = jax.ShapeDtypeStruct((3 * pieces, LANES), F32)
    kept, given = pl.pallas_call(
        functools.partial(weight_kernel, weight_dims),
        grid=(steps,),
        in_specs=[
            smem, smem, resident(hidden.shape),
            pl.BlockSpec((pairs, 2, 4 * rows, block), lambda i: (0, 0, 0, i)),
            resident(tile_shape), resident(shift_shape), slot_spec(block), slot_spec(block),
        ],
        out_specs=[pl.BlockSpec(share.shape, lambda i: (0, 0))] * 2,
        out_shape=[share, share],
        scratch_shapes=[
            pltpu.VMEM((2, 4 * pairs * rows, k_width), BF16),
            pltpu.VMEM((3 * SROWS, r2), BF16),
            pltpu.VMEM((2, part, k_width), BF16),
            pltpu.VMEM((2, part, k_width), BF16),
            pltpu.VMEM((2, 4 * pairs * rows, part), F32),
            pltpu.VMEM((2, 4 * pairs * rows, part), F32),
            pltpu.VMEM((r2, 2 * block), BF16),
            pltpu.VMEM((steps, 2, 3, SROWS, block), F32),
            pltpu.VMEM((steps, 2, SROWS, block), jnp.int32),
            pltpu.VMEM((8, 2 * pieces * LANES), F32),
            pltpu.VMEM((8, LANES), F32),
        ],
        compiler_params=params,
        cost_estimate=cost(4 * matmul, 20e6),
        name="weight",
    )(pos, seg_box, hidden, fields, tile, shift, across, index)

    axes = ("band", "row")
    devices = owners * band_axis
    groups = [[d for d in range(devices) if d % 2 == core] for core in range(2)]

    def swap_cores(array):
        return lax.ppermute(array, "row", [(i, i ^ 1) for i in range(owners)])

    mine = kept + swap_cores(given)
    copies = jnp.broadcast_to(mine[None], (devices // 2,) + mine.shape)
    everyones = lax.all_to_all(
        copies, axes, split_axis=0, concat_axis=0, tiled=True, axis_index_groups=groups
    )
    mine = jnp.sum(everyones, axis=0)
    other = swap_cores(mine)
    odd = lax.axis_index("row") % 2 == 1
    halves = [jnp.where(odd, other, mine), jnp.where(odd, mine, other)]
    halves = [x.reshape(3, pieces * LANES) for x in halves]
    return jnp.concatenate(halves, axis=1)[:, :segments]


def solution(mesh):
    in_specs = (
        P("row", None),
        P("row", None),
        P(),
        P(),
        P(),
        P(),
        P("band", "row", None, None, None),
    )
    return jax.shard_map(body, mesh=mesh, in_specs=in_specs, out_specs=P(), check_vma=False)
```

```python
import functools
import math

import jax
import jax.numpy as jnp
from jax import lax
from jax.experimental import pallas as pl
from jax.experimental.pallas import tpu as pltpu
from jax.sharding import PartitionSpec as P

SROWS = 16
SAMPLING = 0.5
SPREAD = 0.2
TWO_PI = 2.0 * math.pi
LANES = 128
F32 = jnp.float32
BLOCKS = (512, 2048, 256)
BF16 = jnp.bfloat16

SIN_HALF = (0.9999999971, -0.1666666029, 0.008333109246, -0.0001981365728, 2.616271295e-06)
COS_HALF = (0.9999999682, -0.4999993032, 0.04166421727, -0.001385868782, 2.327410856e-05)
SIN_WAVE = (0.9999999964, -0.166666488, 0.008331936401, -0.000194912576)
COS_WAVE = (0.9999999679, -0.499998396, 0.04165412354, -0.001357443708)
SIN_TURN = (
    6.283185307, -41.34170222, 81.60524741, -76.70580003,
    42.05775188, -15.08655272, 3.781282403, -0.6207370354,
)
COS_TURN = (
    0.9999999999, -19.73920874, 64.93938905, -85.45665775,
    60.24212493, -26.40463062, 7.800022219, -1.452987552,
)


def series(coeffs, t):
    value = jnp.full_like(t, coeffs[-1])
    for c in reversed(coeffs[:-1]):
        value = value * t + c
    return value


def turn_cos_sin(turns):
    t = turns - jnp.floor(turns + 0.5)
    square = t * t
    return series(COS_TURN, square), t * series(SIN_TURN, square)


def iota(shape, axis):
    return lax.broadcasted_iota(jnp.int32, shape, axis)


def focal_scale(m_positive, band, band_total):
    ratio = 1.0 + SPREAD * ((band.astype(F32) + 0.5) / band_total - 0.5)
    return m_positive / ratio


def band_lanes(first_band, bands, half, band_total, rows):
    pieces = []
    for b in range(bands):
        q = (iota((rows, half), 1).astype(F32) + 0.5) * SAMPLING
        band = jnp.full((rows, half), 1, jnp.int32) * (first_band + b)
        pieces.append(focal_scale(q, band, band_total))
    return jnp.concatenate(pieces, axis=1)


def column_tables(first_band, bands, half, band_total, cols, tile_ref, shift_ref):
    q = band_lanes(first_band, bands, half, band_total, LANES)
    c, s = turn_cos_sin(q * (iota(q.shape, 0).astype(F32) / cols))
    tile_ref[0] = c
    tile_ref[1] = s
    tiles = cols // (2 * LANES)
    q = band_lanes(first_band, bands, half, band_total, tiles)
    x = (iota(q.shape, 0).astype(F32) * LANES + 0.5) / cols - 0.5
    c, s = turn_cos_sin(q * x)
    shift_ref[0] = c
    shift_ref[1] = s


def write_table(cos_ref, sin_ref, tile_ref, shift_ref, first_tile, tiles):
    for i in range(tiles):
        sc = shift_ref[0, pl.ds(first_tile + i, 1), :]
        ss = shift_ref[1, pl.ds(first_tile + i, 1), :]
        for k in range(0, LANES, 16):
            tc = tile_ref[0, k : k + 16]
            ts = tile_ref[1, k : k + 16]
            rows = slice(i * LANES + k, i * LANES + k + 16)
            cos_ref[rows] = (tc * sc - ts * ss).astype(BF16)
            sin_ref[rows] = (ts * sc + tc * ss).astype(BF16)


def load_segments(coeffs_ref, boxes_ref, seg_ref):
    seg_ref[...] = jnp.zeros_like(seg_ref)
    seg_ref[0:3, : coeffs_ref.shape[1]] = coeffs_ref[...]
    seg_ref[3:7, : boxes_ref.shape[1]] = boxes_ref[...].astype(F32)


def reverse(x):
    back = LANES - 1 - iota((8, LANES), 1)
    pieces = [gather_lanes(x[k : k + 8], back) for k in range(0, x.shape[0], 8)]
    return pieces[0] if len(pieces) == 1 else jnp.concatenate(pieces, axis=0)


def gather_lanes(x, index):
    return jnp.take_along_axis(x, index, axis=1, mode="promise_in_bounds")


def tile_row_pieces(seg_ref, per_row, width):
    for t in range(SROWS):
        yield t, pltpu.roll(seg_ref[...], (width - t * per_row) % width, axis=1)[:, :LANES]


def probe_setup(pos_ref, freq_ref, amp_ref, j, rows, cols, total_rows, waves):
    row = pos_ref[0] * rows + iota((rows, LANES), 0)
    y = (row.astype(F32) + 0.5) / cols - total_rows / (2.0 * cols)
    c, s = turn_cos_sin(freq_ref[j, 1].astype(F32) * y)
    waves[2 * j] = amp_ref[j] * c
    waves[2 * j + 1] = amp_ref[j] * s


def column_wave(freq_ref, pairs, step, block, cols):
    row = iota((8, block), 0)
    freq = jnp.zeros((8, block), F32)
    for j in range(pairs):
        freq = jnp.where(row // 2 == j, freq_ref[j, 0].astype(F32), freq)
    x = ((iota((8, block), 1) + step * block).astype(F32) + 0.5) / cols - 0.5
    c, s = turn_cos_sin(freq * x)
    return jnp.where(row % 2 == 0, s, c)


def emit_pair(j, column, waves, fields, here, lanes, g, rows, x_ref, even_ref, odd_ref):
    from_sin = column[2 * j : 2 * j + 1, lanes] * waves[2 * j, here]
    from_cos = column[2 * j + 1 : 2 * j + 2, lanes] * waves[2 * j + 1, here]
    parts = []
    for wave in (from_cos + from_sin, from_cos - from_sin):
        square = wave * wave
        parts.append(
            (
                series(COS_WAVE, square).astype(BF16),
                (wave * series(SIN_WAVE, square)).astype(BF16),
            )
        )
    for k in range(2):
        for o in range(2):
            at = (2 * k + o) * rows + g
            near = fields[0][o] * parts[0][k]
            far = fields[1][o] * parts[1][k]
            x_ref[j, 0, at : at + 16, lanes] = near
            x_ref[j, 1, at : at + 16, lanes] = far
            at = at + 4 * j * rows
            even_ref[at : at + 16, lanes] = near + far
            odd_ref[at : at + 16, lanes] = near - far


def emit_half_way(pairs, total_ref, y_ref, rows, bands, half, vloc, owners):
    r2 = 2 * rows
    m = iota((half, half), 0)
    n = iota((half, half), 1)
    straight = (m == n).astype(F32).astype(BF16)
    turned = (m + n == half - 1).astype(F32).astype(BF16)
    nt = (((1,), (1,)), ((), ()))
    for b in range(bands):
        for p in range(2 * pairs):
            at = slice(p * r2, (p + 1) * r2)
            cos_part = total_ref[0, at, b * half : (b + 1) * half]
            sin_part = total_ref[1, at, b * half : (b + 1) * half]
            swapped = jnp.concatenate([sin_part[rows:], -sin_part[:rows]], axis=0)
            low = lax.dot_general(
                turned, (cos_part - swapped).astype(BF16), nt, preferred_element_type=F32
            ).astype(BF16)
            high = lax.dot_general(
                straight, (cos_part + swapped).astype(BF16), nt, preferred_element_type=F32
            ).astype(BF16)
            if owners:
                each = half // vloc
                for d in range(each):
                    own = slice(d * vloc, (d + 1) * vloc)
                    y_ref[d, b, p * vloc : (p + 1) * vloc, :] = low[own]
                    y_ref[each + d, b, p * vloc : (p + 1) * vloc, :] = high[own]
            else:
                y_ref[b, p, :half, :] = low
                y_ref[b, p, half:, :] = high


def field_kernel(
    dims, pos_ref, box_ref, freq_ref, amp_ref, coeffs_ref, boxes_ref,
    amplitude_ref, amplitude_far_ref, map_ref, map_far_ref,
    x_ref, tile_ref, shift_ref, across_ref, index_ref, y_ref, *rest
):
    dims, pairs = dims
    (
        seg_ref, tables, bases, slot_tables, waves, cos_ref, sin_ref, even_ref, odd_ref, total_ref, slot_map,
    ) = rest
    rows, cols, block, bands, half, band_total, total_rows, per_row, vloc, owners = dims
    step = pl.program_id(0)
    row0 = pos_ref[0] * rows
    chunks = block // LANES
    maps = (map_ref, map_far_ref)
    amplitudes = (amplitude_ref, amplitude_far_ref)

    @pl.when(step == 0)
    def _():
        load_segments(coeffs_ref, boxes_ref, seg_ref)
        width = seg_ref.shape[1]
        groups = rows // 8
        values = [[jnp.zeros((8, LANES), F32)] * 3 for _ in range(groups)]
        base = [jnp.zeros((8, LANES), jnp.int32)] * groups
        for t, piece in tile_row_pieces(seg_ref, per_row, width):
            part = [jnp.broadcast_to(piece[k : k + 1], (8, LANES)) for k in range(7)]
            low, high = part[3][:, :1], part[4][:, :1]
            mid_row = 0.5 * (part[3] + part[4])
            inv_row = 1.0 / (part[4] - part[3] + 1.0)
            mid = 0.5 * (part[5] + part[6])
            inv = 2.0 / (part[6] - part[5] + 1.0)
            slope = 0.5 * part[1] * inv
            slot_tables[0, t : t + 1] = mid[:1]
            slot_tables[1, t : t + 1] = inv[:1]
            for g in range(groups):
                here = (row0 + g * 8 + iota((8, LANES), 0)).astype(F32)
                mine = (here >= low) & (here <= high)
                new = (0.5 * part[0] + part[2] * ((here - mid_row) * inv_row), slope, mid)
                values[g] = [jnp.where(mine, n, v) for n, v in zip(new, values[g])]
                base[g] = jnp.where(mine, t * per_row, base[g])
        for g in range(groups):
            for k in range(3):
                tables[k, g * 8 : (g + 1) * 8] = values[g][k]
            bases[g * 8 : (g + 1) * 8] = base[g]
        for j in range(pairs):
            probe_setup(pos_ref, freq_ref, amp_ref, j, rows, cols, total_rows, waves)
        column_tables(pos_ref[1] * bands, bands, half, band_total, cols, tile_ref, shift_ref)
        total_ref[...] = jnp.zeros_like(total_ref)

    for t in range(SROWS):
        first = jnp.clip(box_ref[0, t * per_row] - row0, 0, rows - 1)
        for side in range(2):
            slot_map[side, t : t + 1, :] = maps[side][pl.ds(first, 1), :] - t * per_row

    column = column_wave(freq_ref, pairs, step, block, cols)
    write_table(cos_ref, sin_ref, tile_ref, shift_ref, step * chunks, chunks)

    for i in range(chunks):
        lanes = slice(i * LANES, (i + 1) * LANES)
        far_lanes = slice((chunks - 1 - i) * LANES, (chunks - i) * LANES)
        near_column = (iota((8, LANES), 1) + (step * block + i * LANES)).astype(F32)
        columns = (near_column, (cols - 1.0) - near_column)
        for side in range(2):
            for t in range(0, SROWS, 8):
                index = slot_map[side, t : t + 8, far_lanes if side else lanes] & (LANES - 1)
                if side:
                    index = reverse(index)
                mid = gather_lanes(slot_tables[0, t : t + 8], index)
                inv = gather_lanes(slot_tables[1, t : t + 8], index)
                across_ref[side, t : t + 8, lanes] = (columns[side] - mid) * inv
                index_ref[side, t : t + 8, lanes] = index
        for g in range(0, rows, 16):
            here = slice(g, g + 16)
            fields = []
            for side in range(2):
                source = far_lanes if side else lanes
                size = amplitudes[side][here, source].astype(F32)
                halves = []
                for h in (0, 8):
                    own = slice(g + h, g + h + 8)
                    index = maps[side][own, source] - bases[own]
                    if side:
                        index = reverse(index)
                    half_phase = gather_lanes(tables[0, own], index) + gather_lanes(
                        tables[1, own], index
                    ) * (columns[side] - gather_lanes(tables[2, own], index))
                    square = half_phase * half_phase
                    s = half_phase * series(SIN_HALF, square)
                    c = series(COS_HALF, square)
                    twice = s + s
                    own_size = size[h : h + 8]
                    if side:
                        own_size = reverse(own_size)
                    halves.append((own_size * (1.0 - twice * s), own_size * (twice * c)))
                both = [
                    jnp.concatenate([halves[0][o], halves[1][o]], axis=0).astype(BF16)
                    for o in range(2)
                ]
                fields.append(both)
            for j in range(pairs):
                emit_pair(
                    j, column, waves, fields, here, lanes, g, rows, x_ref, even_ref, odd_ref
                )

    total_ref[0] += jnp.dot(even_ref[...], cos_ref[...], preferred_element_type=F32)
    total_ref[1] += jnp.dot(odd_ref[...], sin_ref[...], preferred_element_type=F32)

    @pl.when(step == pl.num_programs(0) - 1)
    def _():
        emit_half_way(pairs, total_ref, y_ref, rows, bands, half, vloc, owners)


def row_table_kernel(dims, pos_ref, table_ref):
    rows, cols, bands, focal, band_total, total_rows, sources = dims
    r2 = 2 * rows
    for b in range(bands):
        band = jnp.full((rows, focal), 1, jnp.int32) * (pos_ref[1] * bands + b)
        q = (iota((rows, focal), 1).astype(F32) + (0.5 - focal / 2)) * SAMPLING
        q = focal_scale(q, band, band_total)
        tile_c, tile_s = turn_cos_sin(q * (iota(q.shape, 0).astype(F32) / cols))
        first = iota((sources, focal), 0).astype(F32) * rows + 0.5
        y = first / cols - total_rows / (2.0 * cols)
        shift_c, shift_s = turn_cos_sin(jnp.broadcast_to(q[:1], y.shape) * y)
        for d in range(sources):
            sc, ss = shift_c[d : d + 1], shift_s[d : d + 1]
            c = (tile_c * sc - tile_s * ss).astype(BF16)
            s_value = tile_s * sc + tile_c * ss
            s = s_value.astype(BF16)
            table_ref[b, d * r2 : d * r2 + rows, :focal] = c
            table_ref[b, d * r2 : d * r2 + rows, focal:] = (-s_value).astype(BF16)
            table_ref[b, d * r2 + rows : (d + 1) * r2, :focal] = s
            table_ref[b, d * r2 + rows : (d + 1) * r2, focal:] = c


def focal_kernel(dims, y_ref, target_ref, table_ref, h_ref):
    rows, sources, scale = dims
    r2 = 2 * rows
    lhs = jnp.concatenate([y_ref[d] for d in range(sources)], axis=1)
    f = jnp.dot(lhs, table_ref[...], preferred_element_type=F32)
    residual = (f * (2.0 * scale) - target_ref[...]).astype(BF16)
    spread = lax.dot_general(
        residual, table_ref[...], (((1,), (1,)), ((), ())), preferred_element_type=F32
    )
    for d in range(sources):
        h_ref[d] = spread[:, d * r2 : (d + 1) * r2].astype(BF16)


def fold_hidden(pairs, h_ref, left_ref, rows, bands, half, vloc, sources):
    r2 = 2 * rows
    nt = (((1,), (1,)), ((), ()))
    m = iota((half, 2 * half), 0)
    v = iota((half, 2 * half), 1)
    upper = (v == half + m).astype(F32)
    lower = (v == half - 1 - m).astype(F32)
    even, odd = (upper + lower).astype(BF16), (upper - lower).astype(BF16)
    same = (iota((r2, r2), 0) == iota((r2, r2), 1)).astype(F32).astype(BF16)
    for b in range(bands):
        for p in range(2 * pairs):
            if sources:
                block_h = jnp.concatenate(
                    [h_ref[d, b, p * vloc : (p + 1) * vloc, :] for d in range(sources)], axis=0
                )
            else:
                block_h = h_ref[b, p]

            def fold(mirror):
                folded = jnp.dot(mirror, block_h, preferred_element_type=F32).astype(BF16)
                return lax.dot_general(same, folded, nt, preferred_element_type=F32)

            plus, minus = fold(even), fold(odd)
            at = slice(p * r2, (p + 1) * r2)
            left_ref[0, at, b * half : (b + 1) * half] = plus.astype(BF16)
            left_ref[1, at, b * half : (b + 1) * half] = jnp.concatenate(
                [-minus[rows:], minus[:rows]], axis=0
            ).astype(BF16)


def weight_kernel(
    dims, pos_ref, box_ref, h_ref, x_ref, tile_ref, shift_ref, across_ref, index_ref,
    out_ref, give_ref, left_ref, pick_ref, cos_ref, sin_ref, p_ref, q_ref, weight_ref, sums_ref,
    term_ref, flat_ref, slot_ref,
):
    rows, cols, block, part, bands, half, per_row, pairs, vloc, sources, scale = dims
    step = pl.program_id(0)
    row0 = pos_ref[0] * rows
    r2 = 2 * rows
    nt = (((1,), (1,)), ((), ()))

    @pl.when(step == 0)
    def _():
        fold_hidden(pairs, h_ref, left_ref, rows, bands, half, vloc, sources)
        slot = iota((SROWS, r2), 0)
        lane = iota((SROWS, r2), 1)
        here = (row0 + lane % rows).astype(F32)
        low = jnp.zeros((SROWS, r2), F32)
        high = jnp.zeros((SROWS, r2), F32)
        for t in range(SROWS):
            low = jnp.where(slot == t, box_ref[0, t * per_row].astype(F32), low)
            high = jnp.where(slot == t, box_ref[1, t * per_row].astype(F32), high)
        mine = ((here >= low) & (here <= high)).astype(F32)
        down = mine * ((here - 0.5 * (low + high)) / (0.5 * (high - low + 1.0)))
        down_high = down.astype(BF16)
        pick_ref[:SROWS] = mine.astype(BF16)
        pick_ref[SROWS : 2 * SROWS] = down_high
        pick_ref[2 * SROWS :] = (down - down_high.astype(F32)).astype(BF16)

    tiles = part // LANES
    for k in range(block // part):
        slot = k % 2
        write_table(
            cos_ref.at[slot], sin_ref.at[slot], tile_ref, shift_ref,
            step * (block // LANES) + k * tiles, tiles,
        )
        p_ref[slot] = lax.dot_general(left_ref[0], cos_ref[slot], nt, preferred_element_type=F32)
        q_ref[slot] = lax.dot_general(left_ref[1], sin_ref[slot], nt, preferred_element_type=F32)
        for i in range(tiles):
            lanes = slice(i * LANES, (i + 1) * LANES)
            at = slice(k * part + i * LANES, k * part + (i + 1) * LANES)
            for g in range(0, rows, 16):
                near, far = None, None
                for p in range(2 * pairs):
                    j, first = divmod(p, 2)
                    re = slice(p * r2 + g, p * r2 + g + 16)
                    im = slice(p * r2 + rows + g, p * r2 + rows + g + 16)
                    xre = slice(first * r2 + g, first * r2 + g + 16)
                    xim = slice(first * r2 + rows + g, first * r2 + rows + g + 16)
                    p_re, p_im = p_ref[slot, re, lanes], p_ref[slot, im, lanes]
                    q_re, q_im = q_ref[slot, re, lanes], q_ref[slot, im, lanes]
                    x = [
                        [x_ref[j, side, rows_, at].astype(F32) for rows_ in (xre, xim)]
                        for side in range(2)
                    ]
                    near_term = x[0][0] * (p_im + q_im) - x[0][1] * (p_re + q_re)
                    far_term = x[1][0] * (p_im - q_im) - x[1][1] * (p_re - q_re)
                    near = near_term if near is None else near + near_term
                    far = far_term if far is None else far + far_term
                for side, value in enumerate((near, far)):
                    high = value.astype(BF16)
                    to = slice(side * block + at.start, side * block + at.stop)
                    weight_ref[g : g + 16, to] = high
                    weight_ref[rows + g : rows + g + 16, to] = (
                        value - high.astype(F32)
                    ).astype(BF16)
    sums = jnp.dot(pick_ref[...], weight_ref[...], preferred_element_type=F32)
    for side in range(2):
        mine = sums[:, side * block : (side + 1) * block]
        sums_ref[step, side, 0] = mine[:SROWS]
        sums_ref[step, side, 1] = mine[:SROWS] * across_ref[side]
        sums_ref[step, side, 2] = mine[SROWS : 2 * SROWS] + mine[2 * SROWS :]
        term_ref[step, side] = index_ref[side]

    @pl.when(step == pl.num_programs(0) - 1)
    def _():
        tops = [box_ref[0, t * per_row] for t in range(SROWS)]
        bottoms = [box_ref[1, t * per_row] for t in range(SROWS)]
        first = sum((bottom < row0).astype(jnp.int32) for bottom in bottoms)
        last = sum((top < row0 + rows).astype(jnp.int32) for top in tops)

        def tile_row(t, carry):
            def add(i, total):
                for side in range(2):
                    index = term_ref[i, side, pl.ds(t, 1), :].astype(F32).astype(BF16)
                    inside = jnp.where(tile_index == index, one, zero)
                    terms = [sums_ref[i, side, q, pl.ds(t, 1), :] for q in range(3)]
                    highs = [x.astype(BF16).astype(F32) for x in terms]
                    lows = [x - h for x, h in zip(terms, highs)]
                    stacked = jnp.concatenate(highs + lows + lows[:2], axis=0).astype(BF16)
                    total = total + lax.dot_general(
                        stacked, inside, nt, preferred_element_type=F32
                    )
                return total

            total = lax.fori_loop(0, pl.num_programs(0), add, jnp.zeros((8, padded), F32))
            slot_ref[:, :padded] = total
            total = jnp.where(iota((8, LANES), 1) < per_row, slot_ref[...], 0.0)
            padding = jnp.zeros((8, flat_ref.shape[1] - LANES), F32)
            wide = jnp.concatenate([total, padding], axis=1)
            flat_ref[...] += pltpu.roll(wide, t * per_row, axis=1)
            return carry

        padded = -(-per_row // 16) * 16
        tile_index = iota((padded, block), 0).astype(F32).astype(BF16)
        one = jnp.ones((padded, block), BF16)
        zero = jnp.zeros((padded, block), BF16)
        slot_ref[...] = jnp.zeros_like(slot_ref)
        flat_ref[...] = jnp.zeros_like(flat_ref)
        lax.fori_loop(first, last, tile_row, 0)
        odd = pos_ref[0] % 2 == 1
        pieces = flat_ref.shape[1] // (2 * LANES)
        for q in range(3):
            value = (flat_ref[q : q + 1] + flat_ref[q + 3 : q + 4]) * scale
            for i in range(pieces):
                low = value[:, i * LANES : (i + 1) * LANES]
                high = value[:, (pieces + i) * LANES : (pieces + i + 1) * LANES]
                at = q * pieces + i
                out_ref[at : at + 1] = jnp.where(odd, high, low)
                give_ref[at : at + 1] = jnp.where(odd, low, high)


def body(amplitude, seg_map, seg_box, seg_coeffs, probe_freq, probe_amp, measured):
    rows, cols = amplitude.shape
    owners = lax.axis_size("row")
    band_axis = lax.axis_size("band")
    total_rows = rows * owners
    bands, vloc, probes, _, focal = measured.shape
    pairs = probes // 2
    half = focal // 2
    band_total = bands * band_axis
    segments = seg_coeffs.shape[1]
    per_row = segments // SROWS
    r2 = 2 * rows
    normf = 1.0 / math.sqrt(total_rows * cols)
    aligned = vloc % 16 == 0
    half_cols = cols // 2
    field_block, block, part = BLOCKS
    k_width = bands * half

    pos = jnp.stack([lax.axis_index("row"), lax.axis_index("band")]).astype(jnp.int32)
    width = -(-(segments + LANES) // LANES) * LANES
    smem = pl.BlockSpec(memory_space=pltpu.SMEM)
    whole = pl.BlockSpec(memory_space=pltpu.VMEM)
    params = pltpu.CompilerParams(dimension_semantics=("arbitrary",))

    def resident(shape):
        return pl.BlockSpec(shape, lambda i: (0,) * len(shape), pipeline_mode=pl.Buffered(1))

    def cost(flops, moved):
        return pl.CostEstimate(flops=int(flops), bytes_accessed=int(moved), transcendentals=0)

    def slot_spec(block):
        return pl.BlockSpec((2, SROWS, block), lambda i: (0, 0, i))

    near = pl.BlockSpec((rows, field_block), lambda i: (0, i))
    far = pl.BlockSpec((rows, field_block), lambda i: (0, cols // field_block - 1 - i))
    tile_shape = (2, LANES, k_width)
    shift_shape = (2, half_cols // LANES, k_width)
    arrays = 2 * pairs
    y_dims = (owners, bands, arrays * vloc, r2) if aligned else (bands, arrays, focal, r2)
    y_spec = pl.BlockSpec(y_dims, lambda i: (0,) * len(y_dims))
    y_shape = jax.ShapeDtypeStruct(y_dims, BF16)
    def field_dims(block):
        return (
            rows, cols, block, bands, half, band_total, total_rows, per_row, vloc, aligned
        )

    matmul = 2 * 4 * rows * half_cols * k_width * 2

    def table_scratch(block):
        return [pltpu.VMEM((block, k_width), BF16), pltpu.VMEM((block, k_width), BF16)]

    fields, tile, shift, across, index, half_way = pl.pallas_call(
        functools.partial(field_kernel, (field_dims(field_block), pairs)),
        grid=(half_cols // field_block,),
        in_specs=[
            smem, smem, smem, smem,
            resident(seg_coeffs.shape),
            resident(seg_box.shape),
            near, far, near, far,
        ],
        out_specs=[
            pl.BlockSpec((pairs, 2, 4 * rows, field_block), lambda i: (0, 0, 0, i)),
            pl.BlockSpec(tile_shape, lambda i: (0, 0, 0)),
            pl.BlockSpec(shift_shape, lambda i: (0, 0, 0)),
            slot_spec(field_block),
            slot_spec(field_block),
            y_spec,
        ],
        out_shape=[
            jax.ShapeDtypeStruct((pairs, 2, 4 * rows, half_cols), BF16),
            jax.ShapeDtypeStruct(tile_shape, F32),
            jax.ShapeDtypeStruct(shift_shape, F32),
            jax.ShapeDtypeStruct((2, SROWS, half_cols), F32),
            jax.ShapeDtypeStruct((2, SROWS, half_cols), jnp.int32),
            y_shape,
        ],
        scratch_shapes=[
            pltpu.VMEM((8, width), F32),
            pltpu.VMEM((3, rows, LANES), F32),
            pltpu.VMEM((rows, LANES), jnp.int32),
            pltpu.VMEM((2, SROWS, LANES), F32),
            pltpu.VMEM((2 * pairs, rows, LANES), F32),
            *table_scratch(field_block),
            pltpu.VMEM((4 * pairs * rows, field_block), BF16),
            pltpu.VMEM((4 * pairs * rows, field_block), BF16),
            pltpu.VMEM((2, 4 * pairs * rows, k_width), F32),
            pltpu.VMEM((2, SROWS, field_block), jnp.int32),
        ],
        compiler_params=params,
        cost_estimate=cost(4 * matmul, 20e6),
        name="field",
    )(pos, seg_box, probe_freq, probe_amp, seg_coeffs, seg_box,
      amplitude, amplitude, seg_map, seg_map)

    if not aligned:
        half_way = (
            half_way.reshape(bands, arrays, owners, vloc, r2)
            .transpose(2, 0, 1, 3, 4)
            .reshape(owners, bands, arrays * vloc, r2)
        )
    received = lax.all_to_all(half_way, "row", split_axis=0, concat_axis=0, tiled=True)

    row_table = pl.pallas_call(
        functools.partial(
            row_table_kernel, (rows, cols, bands, focal, band_total, total_rows, owners)
        ),
        in_specs=[smem],
        out_specs=whole,
        out_shape=jax.ShapeDtypeStruct((bands, owners * r2, 2 * focal), BF16),
        cost_estimate=cost(1e6, 2e6),
        name="row_table",
    )(pos)

    plus, minus = measured[:, :, 0::2], measured[:, :, 1::2]
    total, difference = plus + minus, plus - minus
    turned = jnp.stack([difference[:, :, :, 1], -difference[:, :, :, 0]], axis=3)
    targets = jnp.stack([total, turned], axis=3)
    targets = targets.transpose(0, 2, 3, 1, 4, 5).reshape(bands, arrays * vloc, 2 * focal)

    y_block = pl.BlockSpec((owners, None, arrays * vloc, r2), lambda b: (0, b, 0, 0))
    spread = pl.pallas_call(
        functools.partial(focal_kernel, (rows, owners, normf)),
        grid=(bands,),
        in_specs=[
            y_block,
            pl.BlockSpec((None, arrays * vloc, 2 * focal), lambda b: (b, 0, 0)),
            pl.BlockSpec((None, owners * r2, 2 * focal), lambda b: (b, 0, 0)),
        ],
        out_specs=y_block,
        out_shape=jax.ShapeDtypeStruct((owners, bands, arrays * vloc, r2), BF16),
        compiler_params=pltpu.CompilerParams(
            dimension_semantics=("arbitrary",), vmem_limit_bytes=24 << 20
        ),
        cost_estimate=cost(8 * bands * arrays * vloc * owners * r2 * focal, 4e6),
        name="focal",
    )(received, targets, row_table)
    hidden = lax.all_to_all(spread, "row", split_axis=0, concat_axis=0, tiled=True)
    if not aligned:
        hidden = (
            hidden.reshape(owners, bands, arrays, vloc, r2)
            .transpose(1, 2, 0, 3, 4)
            .reshape(bands, arrays, focal, r2)
        )

    scale = 2.0 * normf / (band_total * probes)
    steps = half_cols // block
    weight_dims = (
        rows, cols, block, part, bands, half, per_row, pairs, vloc,
        owners if aligned else 0, scale,
    )
    pieces = -(-segments // (2 * LANES))
    share = jax.ShapeDtypeStruct((3 * pieces, LANES), F32)
    kept, given = pl.pallas_call(
        functools.partial(weight_kernel, weight_dims),
        grid=(steps,),
        in_specs=[
            smem, smem, resident(hidden.shape),
            pl.BlockSpec((pairs, 2, 4 * rows, block), lambda i: (0, 0, 0, i)),
            resident(tile_shape), resident(shift_shape), slot_spec(block), slot_spec(block),
        ],
        out_specs=[pl.BlockSpec(share.shape, lambda i: (0, 0))] * 2,
        out_shape=[share, share],
        scratch_shapes=[
            pltpu.VMEM((2, 4 * pairs * rows, k_width), BF16),
            pltpu.VMEM((3 * SROWS, r2), BF16),
            pltpu.VMEM((2, part, k_width), BF16),
            pltpu.VMEM((2, part, k_width), BF16),
            pltpu.VMEM((2, 4 * pairs * rows, part), F32),
            pltpu.VMEM((2, 4 * pairs * rows, part), F32),
            pltpu.VMEM((r2, 2 * block), BF16),
            pltpu.VMEM((steps, 2, 3, SROWS, block), F32),
            pltpu.VMEM((steps, 2, SROWS, block), jnp.int32),
            pltpu.VMEM((8, 2 * pieces * LANES), F32),
            pltpu.VMEM((8, LANES), F32),
        ],
        compiler_params=pltpu.CompilerParams(
            dimension_semantics=("arbitrary",), vmem_limit_bytes=51 << 20
        ),
        cost_estimate=cost(4 * matmul, 20e6),
        name="weight",
    )(pos, seg_box, hidden, fields, tile, shift, across, index)

    axes = ("band", "row")
    devices = owners * band_axis
    groups = [[d for d in range(devices) if d % 2 == core] for core in range(2)]

    def swap_cores(array):
        return lax.ppermute(array, "row", [(i, i ^ 1) for i in range(owners)])

    mine = kept + swap_cores(given)
    copies = jnp.broadcast_to(mine[None], (devices // 2,) + mine.shape)
    everyones = lax.all_to_all(
        copies, axes, split_axis=0, concat_axis=0, tiled=True, axis_index_groups=groups
    )
    mine = jnp.sum(everyones, axis=0)
    other = swap_cores(mine)
    odd = lax.axis_index("row") % 2 == 1
    halves = [jnp.where(odd, other, mine), jnp.where(odd, mine, other)]
    halves = [x.reshape(3, pieces * LANES) for x in halves]
    return jnp.concatenate(halves, axis=1)[:, :segments]


def solution(mesh):
    in_specs = (
        P("row", None),
        P("row", None),
        P(),
        P(),
        P(),
        P(),
        P("band", "row", None, None, None),
    )
    return jax.shard_map(body, mesh=mesh, in_specs=in_specs, out_specs=P(), check_vma=False)
```
